1024 devices in a mesh: sx: 8 (over z), sy: 16 (over y, core), ev: 8 (over x).
Axes of the slice: x: 8, y: 8, z: 8, core: 2. Of those that a mesh axis runs over, the one named last changes fastest.
Arguments:
- adjoint_state: float32 [8, 9, 64, 128, 128], P('ev', None, 'sx', 'sy'), may hold values from -6 to 6
- forward_state: bfloat16 [8, 3, 9, 64, 128, 128], P('ev', None, None, 'sx', 'sy'), may hold values from -6 to 6
- inv_density: float32 [64, 128, 128], P('sx', 'sy'), may hold values from 0.6 to 1.6
- lame_lambda: float32 [64, 128, 128], P('sx', 'sy'), may hold values from 0.15 to 0.5
- shear_modulus: float32 [64, 128, 128], P('sx', 'sy'), may hold values from 0.1 to 0.4
- station_block: int32 [8, 4096, 1], P('ev', ('sx', 'sy')), may hold values from 0 to 15; in each aligned block of 32 rows (0 to 31, 32 to 63, ..., all dimensions but the last counted through in order) at most 4 rows name the same one
- station_cell: int32 [8, 4096], P('ev', ('sx', 'sy')), may hold values from 0 to 63
- station_trace: float32 [8, 4096, 9], P('ev', ('sx', 'sy')), may hold values from -6 to 6
- source_count: int32 [8, 128], P('ev', ('sx', 'sy')), may hold values from 1 to 32, 3080 in all within a row
Outputs:
- adjoint_final: float32 [8, 9, 64, 128, 128], P('ev', None, 'sx', 'sy')
- kernels: float32 [3, 64, 128, 128], P(None, 'sx', 'sy')
The draws below stay inside these ranges and needn't reach their ends.
Inputs may be any that keep to these rules, and one draw needn't show every extreme that they name: `station_block`: among the 32 rows of one device no block is named more than 4 times.
All inputs are finite; a program needn't handle non-finite values. No bound on the sum of `source_count` on one device may be relied on, other than what follows from the above.
Results may differ from the reference program's by a relative error of at most 0.0003.
Values sent between devices are 32-bit elements; how exact they have to be, the bound alone decides.
No kernel may reach another device: no remote copies, remote signals or barrier semaphores. Data moves between devices by JAX's collectives and lax.ppermute only.
A program may use at most 32 MiB of HBM per device.

```python
import math
import jax
import jax.numpy as jnp
import numpy as np
from jax import lax

CX = 8
CY = 8
CZ = 128
STEPS = 3
S_DEV = 32
CAP = 4
EVENTS = 8
NX = 64
NY = 128
BLOCKS = 128
STATIONS = 4096
N_SX = 8
N_SY = 16


def touch_ends(result, own_key, smallest, top_value):
    extent = result.shape
    index_at = [jax.random.randint(jax.random.fold_in(own_key, axis), (), 0, extent[axis]) for axis in range(len(extent))]
    result = result.at[tuple(index_at)].set(smallest)
    longest = extent.index(max(extent))
    index_at[longest] = (index_at[longest] + 1) % extent[longest]
    return result.at[tuple(index_at)].set(top_value)


def shard_levels(own_key, shape, split, smallest, top_value):
    def one(dim, parts):
        heights = jax.random.uniform(jax.random.fold_in(jax.random.fold_in(own_key, 6), dim), (parts,), jnp.float32, smallest / len(split), top_value / len(split))
        return jnp.repeat(jnp.exp(heights), shape[dim] // parts).reshape((-1,) + (1,) * (len(shape) - dim - 1))

    loudness = one(*split[0])
    for cut in split[1:]:
        loudness = loudness * one(*cut)
    return loudness


def profile(amount, total, most, lean):
    loads = [(1 << 20) // math.isqrt(rank ** lean) + 1 for rank in range(2, amount + 1)]
    spare, given = total - most - (amount - 1), [1] * (amount - 1)
    while spare > 0:
        movable = [i for i in range(amount - 1) if given[i] < most]
        whole, remaining = sum([loads[i] for i in movable]), spare
        for i in movable:
            extra = min(most - given[i], max(1, remaining * loads[i] // whole), spare)
            given[i] = given[i] + extra
            spare = spare - extra
    return np.array([most] + given)


def uneven(key, count, total, reach, slope):
    if count == 2:
        one = jax.random.randint(key, (), max(1, total - reach), min(reach, total - 1) + 1)
        return jnp.stack([one, total - one])
    sizes = jnp.asarray(profile(count, total, reach, slope), jnp.int32)
    pairs = (count - 1) // 2
    giver, taker = sizes[1:1 + 2 * pairs:2], sizes[2:2 + 2 * pairs:2]
    margin = jnp.minimum(giver - 1, reach - taker)
    passed = jax.random.randint(jax.random.fold_in(key, 1), (pairs,), 0, 1 << 20) % (margin + 1)
    sizes = sizes.at[1:1 + 2 * pairs:2].set(giver - passed).at[2:2 + 2 * pairs:2].set(taker + passed)
    return sizes[jax.random.permutation(jax.random.fold_in(key, 2), count)]


def shared_out(stream_key, own, number, rows, number_of, top, bound, skew):
    sequence = jax.random.permutation(stream_key, number_of)
    crowded, usual = portions_of(number_of, rows * top, bound, skew, True), portions_of(number_of, rows * top, bound, skew, False)
    places = jnp.arange(number_of)

    def named(lengths, offset_by):
        used = int((lengths > 0).sum())
        fixed = max(1, used // 4)
        moved = fixed + (places - fixed + offset_by * (used - fixed)) % max(1, number_of - fixed)
        return jnp.zeros((number_of,), jnp.int32).at[sequence[jnp.where(places < fixed, places, moved)]].set(jnp.asarray(lengths, jnp.int32))

    lengths = jnp.where(number % 4 == 0, named(crowded, number // 4), named(usual, number - number // 4 - 1))
    mixed = jax.random.permutation(jax.random.fold_in(own, 3), number_of)
    giver, receiver = mixed[0:number_of // 2 * 2:2], mixed[1:number_of // 2 * 2:2]
    slack = jnp.minimum(lengths[giver] - 1, bound - lengths[receiver]) // 2
    slack = jnp.where((giver == sequence[0]) | (receiver == sequence[0]) | (lengths[receiver] == 0), 0, jnp.maximum(slack, 0))
    moved = jax.random.randint(jax.random.fold_in(own, 4), (number_of // 2,), 0, 1 << 20) % (slack + 1)
    lengths = lengths.at[giver].add(-moved).at[receiver].add(moved)
    labels = jnp.searchsorted(jnp.cumsum(lengths), jnp.arange(rows * top), side="right").astype(jnp.int32)
    table = labels.reshape(top, rows).T
    table = table[jax.random.permutation(jax.random.fold_in(own, 1), rows)]
    offset_by = jax.random.randint(jax.random.fold_in(own, 2), (rows, 1), 0, top)
    return jnp.take_along_axis(table, (jnp.arange(top)[None, :] + offset_by) % top, axis=1)


def portions_of(count, total, bound, lean, full):
    loads = [(1 << 20) // math.isqrt(standing ** lean) + 1 for standing in range(1, count + 1)]
    largest = bound if full else min(bound, max(-(-total // count), total * loads[0] // sum(loads)))
    least = 1 if total - largest >= count - 1 else 0
    holding, spare = [largest] + [least] * (count - 1), total - largest - least * (count - 1)
    while spare > 0:
        free = [i for i in range(1, count) if holding[i] < largest] or [i for i in range(1, count) if holding[i] < bound]
        whole, left = sum([loads[i] for i in free]), spare
        for i in free:
            more = min(bound - holding[i], max(1, left * loads[i] // whole), spare)
            holding[i] = holding[i] + more
            spare = spare - more
    return np.array(holding)


def gaussian(own_key, dims, width, reach, shards=(), kind=jnp.bfloat16):
    result = jax.random.normal(own_key, dims, jnp.float32) * width
    if len(shards) > 0:
        result = shard_levels(own_key, dims, shards, -0.22, 0.18) * result
    return jnp.clip(result, min=-reach, max=reach).astype(kind)


def setup_inputs(seed: int = 0) -> dict:
    key_of = jax.random.split(jax.random.key(seed), 10)
    adjoint_state = gaussian(key_of[0], (EVENTS, 9, NX, NY, CZ), 1.0, 6.0, ((0, 8), (2, 8), (3, 16)), jnp.float32)
    forward_state = gaussian(key_of[1], (EVENTS, STEPS, 9, NX, NY, CZ), 1.0, 6.0, ((0, 8), (3, 8), (4, 16)))
    inv_density = jnp.clip(jnp.exp(math.log(1.6) - 0.98082923 * jax.random.uniform(key_of[2], (NX, NY, CZ), jnp.float32) ** shard_levels(key_of[2], (NX, NY, CZ), ((0, 8), (1, 16)), -0.2, 0.2)), 0.6, 1.6)
    lame_lambda = jnp.clip(jnp.exp(math.log(0.5) - 1.2039728 * jax.random.uniform(key_of[3], (NX, NY, CZ), jnp.float32) ** shard_levels(key_of[3], (NX, NY, CZ), ((0, 8), (1, 16)), -0.2, 0.2)), 0.15, 0.5)
    shear_modulus = jnp.clip(jnp.exp(math.log(0.4) - 1.3862944 * jax.random.uniform(key_of[4], (NX, NY, CZ), jnp.float32) ** shard_levels(key_of[4], (NX, NY, CZ), ((0, 8), (1, 16)), -0.2, 0.2)), 0.1, 0.4)
    station_block_keys = jax.random.split(jax.random.fold_in(key_of[5], 1), EVENTS * STATIONS // S_DEV)
    station_block_turns = jax.random.permutation(jax.random.fold_in(key_of[5], 3), EVENTS * STATIONS // S_DEV)
    station_block = jax.vmap(lambda own, number: shared_out(jax.random.fold_in(key_of[5], 2), own, number, S_DEV, N_SY, 1, CAP, 2))(station_block_keys, station_block_turns).reshape((EVENTS, STATIONS, 1))
    station_cell = touch_ends(jax.random.randint(key_of[6], (EVENTS, STATIONS), 0, CX * CY), jax.random.fold_in(key_of[6], 1), 0, (CX * CY) - 1).astype(jnp.int32)
    station_trace = gaussian(key_of[7], (EVENTS, STATIONS, 3 * STEPS), 1.0, 6.0, ((0, 8), (1, 128)), jnp.float32)
    source_count = jax.vmap(lambda own: uneven(own, BLOCKS, ((N_SX * N_SY - 1) * 3 * S_DEV) // 4 + S_DEV, S_DEV, 1))(jax.random.split(key_of[8], EVENTS)).reshape((EVENTS, BLOCKS)).astype(jnp.int32)
    return {"adjoint_state": adjoint_state, "forward_state": forward_state, "inv_density": inv_density, "lame_lambda": lame_lambda, "shear_modulus": shear_modulus, "station_block": station_block, "station_cell": station_cell, "station_trace": station_trace, "source_count": source_count}


DT = 0.35
stress_faces = ([0], [3, 4], [1], [3, 5])
velocity_faces = ([1, 2], [0], [0, 2], [1])


def shift_upper(field, axis, plane):
    size = field.shape[axis]
    inner = lax.slice_in_dim(field, 1, size, axis=axis)
    return jnp.concatenate([inner, plane], axis=axis)


def shift_lower(field, axis, plane):
    size = field.shape[axis]
    inner = lax.slice_in_dim(field, 0, size - 1, axis=axis)
    return jnp.concatenate([plane, inner], axis=axis)


def above_diff(field):
    zeros_plane = jnp.zeros(field.shape[:-1] + (1,), jnp.float32)
    return jnp.concatenate([field[..., 1:], zeros_plane], axis=-1) - field


def below_diff(field):
    zeros_plane = jnp.zeros(field.shape[:-1] + (1,), jnp.float32)
    return field - jnp.concatenate([zeros_plane, field[..., :-1]], axis=-1)


def accelerate(stress, planes, inv_density, force):
    high_x, low_x, high_y, low_y = planes
    next_x = shift_upper(stress[:, stress_faces[0]], 2, high_x)
    prev_x = shift_lower(stress[:, stress_faces[1]], 2, low_x)
    next_y = shift_upper(stress[:, stress_faces[2]], 3, high_y)
    prev_y = shift_lower(stress[:, stress_faces[3]], 3, low_y)
    sxx, syy, szz, sxy, sxz, syz = [stress[:, c] for c in range(6)]
    accel_x = (next_x[:, 0] - sxx) + (sxy - prev_y[:, 0]) + below_diff(sxz)
    accel_y = (sxy - prev_x[:, 0]) + (next_y[:, 0] - syy) + below_diff(syz)
    accel_z = (sxz - prev_x[:, 1]) + (syz - prev_y[:, 1]) + above_diff(szz)
    accel = jnp.stack([accel_x, accel_y, accel_z], axis=1)
    accel = accel.at[..., 0].add(force)
    return DT * inv_density * accel


def strain_rates(velocity, planes):
    high_x, low_x, high_y, low_y = planes
    next_x = shift_upper(velocity[:, velocity_faces[0]], 2, high_x)
    prev_x = shift_lower(velocity[:, velocity_faces[1]], 2, low_x)
    next_y = shift_upper(velocity[:, velocity_faces[2]], 3, high_y)
    prev_y = shift_lower(velocity[:, velocity_faces[3]], 3, low_y)
    vel_x, vel_y, vel_z = velocity[:, 0], velocity[:, 1], velocity[:, 2]
    rate_xx = vel_x - prev_x[:, 0]
    rate_yy = vel_y - prev_y[:, 0]
    rate_zz = below_diff(vel_z)
    rate_xy = 0.5 * ((next_y[:, 0] - vel_x) + (next_x[:, 0] - vel_y))
    rate_xz = 0.5 * (above_diff(vel_x) + (next_x[:, 1] - vel_z))
    rate_yz = 0.5 * (above_diff(vel_y) + (next_y[:, 1] - vel_z))
    return jnp.stack([rate_xx, rate_yy, rate_zz, rate_xy, rate_xz, rate_yz], axis=1)


def stress_update(stress, rates, lame_lambda, shear_modulus, strains):
    trace = rates[:, 0] + rates[:, 1] + rates[:, 2]
    diagonal = stress[:, :3] + DT * (lame_lambda * trace[:, None] + 2.0 * shear_modulus * rates[:, :3])
    offdiag = stress[:, 3:] + DT * 2.0 * shear_modulus * rates[:, 3:]
    forward_trace = strains[:, 0] + strains[:, 1] + strains[:, 2]
    lambda_term = DT * forward_trace * trace
    shear_term = DT * 2.0 * (jnp.sum(strains[:, :3] * rates[:, :3], axis=1) + 2.0 * jnp.sum(strains[:, 3:] * rates[:, 3:], axis=1))
    return jnp.concatenate([diagonal, offdiag], axis=1), lambda_term, shear_term


def zero_planes(stack, faces):
    events, comps, size_x, size_y, size_z = stack.shape
    return (jnp.zeros((events, len(faces[0]), 1, size_y, size_z), jnp.float32),
            jnp.zeros((events, len(faces[1]), 1, size_y, size_z), jnp.float32),
            jnp.zeros((events, len(faces[2]), size_x, 1, size_z), jnp.float32),
            jnp.zeros((events, len(faces[3]), size_x, 1, size_z), jnp.float32))


def reference(adjoint_state, forward_state, inv_density, lame_lambda, shear_modulus, station_block, station_cell, station_trace, source_count):
    stations = station_cell.shape[1]
    index = jnp.arange(stations, dtype=jnp.int32)
    owner = index // S_DEV
    within = index % S_DEV
    row_x = index // (N_SY * S_DEV)

    def one_event(event):
        state = adjoint_state[event][None]
        forward = forward_state[event][None]
        counts = source_count[event]
        live = (within < counts[owner]).astype(jnp.float32)
        cells = station_cell[event]
        grid_x = (row_x * CX + cells // CY).astype(jnp.int32)
        grid_y = (station_block[event, :, 0] * CY + cells % CY).astype(jnp.int32)
        traces = station_trace[event] * live[:, None]
        surface = jnp.zeros((NX, NY, 3 * STEPS), jnp.float32).at[grid_x, grid_y].add(traces)
        zero_k = jnp.zeros((1, NX, NY, CZ), jnp.float32)
        rho_kernel, lambda_kernel, shear_kernel = zero_k, zero_k, zero_k
        for step in range(STEPS):
            force = jnp.moveaxis(surface[:, :, 3 * step:3 * step + 3], 2, 0)[None]
            stress = state[:, 3:]
            change = accelerate(stress, zero_planes(stress, stress_faces), inv_density, force)
            velocity = state[:, :3] + change
            rho_kernel = rho_kernel + jnp.sum(forward[:, step, :3].astype(jnp.float32) * change, axis=1)
            rates = strain_rates(velocity, zero_planes(velocity, velocity_faces))
            stress, lambda_term, shear_term = stress_update(stress, rates, lame_lambda, shear_modulus, forward[:, step, 3:].astype(jnp.float32))
            lambda_kernel = lambda_kernel + lambda_term
            shear_kernel = shear_kernel + shear_term
            state = jnp.concatenate([velocity, stress], axis=1)
        return state[0], jnp.concatenate([rho_kernel, lambda_kernel, shear_kernel], axis=0)

    states, event_kernels = lax.map(one_event, jnp.arange(EVENTS, dtype=jnp.int32))
    return states, jnp.sum(event_kernels, axis=0)
```

```python
import functools

import jax
import jax.numpy as jnp
from jax import lax
from jax.experimental import pallas as pl
from jax.experimental.pallas import tpu as pltpu
from jax.sharding import PartitionSpec as P

DT = 0.35
W = 3
B = 8
XE = B + 2 * W
XS = XE + 2
YR = 16
FIELDS = 12
DEAD = -1.0e6
MIB = 1 << 20
VMEM = pl.BlockSpec(memory_space=pltpu.VMEM)
SMEM = pl.BlockSpec(memory_space=pltpu.SMEM)


def x_faces_kernel(
    ny, count_ref, adj_ref, rho_ref, lam_ref, mu_ref, block_ref, cell_ref, trace_ref, low_ref, high_ref
):
    for out, first in ((low_ref, 0), (high_ref, B - W)):
        out[0:9] = adj_ref[:, first : first + W]
        out[9] = rho_ref[first : first + W]
        out[10] = lam_ref[first : first + W]
        out[11] = mu_ref[first : first + W]
    rows = trace_ref.shape[0]
    wide = jnp.concatenate(
        [trace_ref[...], block_ref[...].astype(jnp.float32), jnp.zeros((rows, 118), jnp.float32)], axis=1
    )
    turned = wide.T
    cell = cell_ref[...].astype(jnp.float32)
    cell_x = jnp.floor(cell * (1.0 / B))
    key = cell_x * ny + turned[9:10] * B + (cell - B * cell_x)
    live = lax.broadcasted_iota(jnp.int32, (1, rows), 1) < count_ref[0, 0]
    key = jnp.where(live, key, DEAD)
    values = jnp.where(live, turned[0:9], 0.0)
    pack = jnp.concatenate([key, values, jnp.zeros((6, rows), jnp.float32)], axis=0)
    pack = jnp.concatenate([pack, jnp.zeros((16, 128 - rows), jnp.float32)], axis=1)
    for out in (low_ref, high_ref):
        out[12, 0] = pack[0:8]
        out[12, 1] = pack[8:16]
        out[12, 2] = jnp.zeros((8, 128), jnp.float32)


def y_faces_kernel(
    ny, adj_ref, rho_ref, lam_ref, mu_ref, own_ref, low_ref, high_ref, face_low_ref, face_high_ref, tiles_ref
):
    params = (rho_ref, lam_ref, mu_ref)
    for out, first in ((face_low_ref, 0), (face_high_ref, B - W)):
        for f in range(FIELDS):
            for r in range(W):
                y = first + r
                at = (r * FIELDS + f) * YR
                own = (
                    adj_ref[pl.ds(f * 64 + y, B, stride=8), :]
                    if f < 9
                    else params[f - 9][pl.ds(y, B, stride=8), :]
                )
                out[pl.ds(at, W), :] = low_ref[pl.ds(f * 24 + y, W, stride=8), :]
                out[pl.ds(at + W, B), :] = own
                out[pl.ds(at + W + B, W), :] = high_ref[pl.ds(f * 24 + y, W, stride=8), :]
                out[pl.ds(at + XE, YR - XE), :] = jnp.zeros((YR - XE, 128), jnp.float32)
    row = lax.broadcasted_iota(jnp.int32, (8, 128), 0)
    lane = lax.broadcasted_iota(jnp.int32, (8, 128), 1)
    tile = jnp.zeros((8, 128), jnp.float32)
    for s, (ref, shift) in enumerate(((own_ref, W), (low_ref, W - B), (high_ref, W + B))):
        head = ref[pl.ds(12 * 24, 8), :]
        head = jnp.where(row == 0, head + float(shift * ny), head)
        tail = ref[pl.ds(12 * 24 + 8, 8), :]
        head = pltpu.roll(head, 32 * s, 1) if s else head
        tail = pltpu.roll(pltpu.roll(tail, 96, 1), 2 * s, 0) if s else pltpu.roll(tail, 96, 1)
        tile = jnp.where(lane // 32 == s, head, tile)
        tile = jnp.where((lane // 32 == 3) & (row // 2 == s), tail, tile)
    for d in range(tiles_ref.shape[0]):
        tiles_ref[d] = tile


def steps_kernel(
    ny,
    steps,
    place_ref,
    adj_ref,
    rho_ref,
    lam_ref,
    mu_ref,
    forward_ref,
    low_ref,
    high_ref,
    y_low_ref,
    y_high_ref,
    tiles_ref,
    state_ref,
    kernels_ref,
    ext,
    force,
    change_ref,
    rate_ref,
):
    params = (rho_ref, lam_ref, mu_ref)
    plane = XS * YR
    zero8 = jnp.zeros((8, 128), jnp.float32)
    for f in range(FIELDS):
        for e in range(XS):
            at = f * plane + e * YR
            if e == 0 or e == XS - 1:
                ext[pl.ds(at, 8), :] = zero8
            elif e <= W:
                ext[pl.ds(at, 8), :] = low_ref[f, e - 1]
            elif e <= W + B:
                ext[pl.ds(at, 8), :] = adj_ref[f, e - 1 - W] if f < 9 else params[f - 9][e - 1 - W]
            else:
                ext[pl.ds(at, 8), :] = high_ref[f, e - 1 - W - B]
            ext[pl.ds(at + 8, 8), :] = zero8
        for r in range(W):
            src = (r * FIELDS + f) * YR
            ext[pl.ds(f * plane + YR + 8 + r, XE, stride=YR), :] = y_high_ref[pl.ds(src, XE), :]
            ext[pl.ds(f * plane + YR + 13 + r, XE, stride=YR), :] = y_low_ref[pl.ds(src, XE), :]
    cells = XE * YR
    at = lax.broadcasted_iota(jnp.int32, (cells, 128), 0)
    local = at % YR
    local = jnp.where(local < 11, local, local - YR)
    y = place_ref[0] * B + local
    ident = jnp.where((y >= 0) & (y < ny), (at // YR) * ny + y, -10000000).astype(jnp.float32)
    lane = lax.broadcasted_iota(jnp.int32, (8, 128), 1)
    sources = tiles_ref.shape[0]
    hot, packed = [], []
    for d in range(sources):
        tile = tiles_ref[d]
        key = jnp.where(lane < 96, tile, DEAD)[0:1]
        hot.append((ident == key).astype(jnp.float32))
        tails = jnp.where(
            lane < 32, pltpu.roll(tile, 32, 1), jnp.where(lane < 64, pltpu.roll(tile, 64, 1), pltpu.roll(tile, 96, 1))
        )
        packed.append(jnp.concatenate([tile, tails], axis=0))
    surface = lax.dot_general(
        jnp.concatenate(hot, axis=1),
        jnp.concatenate(packed, axis=1),
        (((1,), (1,)), ((), ())),
        precision=lax.Precision.HIGHEST,
        preferred_element_type=jnp.float32,
    )
    for s, first, count in ((1, 0, W), (0, W, B), (2, W + B, W)):
        part = surface[first * YR : (first + count) * YR]
        top = lax.broadcasted_iota(jnp.int32, (count * YR, 128), 1) == 0
        for k in range(3 * steps):
            column = 1 + k if k < 7 else 8 + 2 * s + (k - 7)
            force[k, pl.ds(first * YR, count * YR), :] = jnp.where(top, part[:, column : column + 1], 0.0)

    lanes = lax.broadcasted_iota(jnp.int32, (YR, 128), 1)

    def y_up(v):
        return pltpu.roll(v, YR - 1, 0)

    def y_down(v):
        return pltpu.roll(v, 1, 0)

    def z_up(v):
        return jnp.where(lanes == 127, 0.0, pltpu.roll(v, 127, 1))

    def z_down(v):
        return jnp.where(lanes == 0, 0.0, pltpu.roll(v, 1, 1))

    def get(f, e):
        return ext[pl.ds(pl.multiple_of(f * plane + e * YR, YR), YR), :]

    def put(f, e, v):
        ext[pl.ds(pl.multiple_of(f * plane + e * YR, YR), YR), :] = v

    for x in range(B):
        for k in range(3):
            kernels_ref[k, x] = zero8

    for step in range(steps):

        def velocity(i, e):
            sxx, syy, szz, sxy, sxz, syz = [get(3 + f, e) for f in range(6)]
            ax = (get(3, e + 1) - sxx) + (sxy - y_down(sxy)) + (sxz - z_down(sxz))
            ay = (sxy - get(6, e - 1)) + (y_up(syy) - syy) + (syz - z_down(syz))
            az = (sxz - get(7, e - 1)) + (syz - y_down(syz)) + (z_up(szz) - szz)
            scale = DT * get(9, e)
            for c, accel in enumerate((ax, ay, az)):
                pushed = accel + force[3 * step + c, pl.ds(pl.multiple_of((e - 1) * YR, YR), YR), :]
                change = scale * pushed
                put(c, e, get(c, e) + change)
                change_ref[c, e] = change[0:8]

        def stress(i, e):
            vx, vy, vz = [get(f, e) for f in range(3)]
            exx = vx - get(0, e - 1)
            eyy = vy - y_down(vy)
            ezz = vz - z_down(vz)
            exy = 0.5 * ((y_up(vx) - vx) + (get(1, e + 1) - vy))
            exz = 0.5 * ((z_up(vx) - vx) + (get(2, e + 1) - vz))
            eyz = 0.5 * ((z_up(vy) - vy) + (y_up(vz) - vz))
            trace = exx + eyy + ezz
            lam = get(10, e) * trace
            twice = 2.0 * get(11, e)
            for f, rate in enumerate((exx, eyy, ezz, exy, exz, eyz)):
                if f < 3:
                    put(3 + f, e, get(3 + f, e) + DT * (lam + twice * rate))
                else:
                    put(3 + f, e, get(3 + f, e) + DT * twice * rate)
                rate_ref[f, e] = rate[0:8]

        def pair(body, first):
            def run(i, carry):
                e = first + 2 * i
                body(i, e)
                body(i, e + 1)
                return carry

            return run

        lax.fori_loop(0, (XE - 2 * step) // 2, pair(velocity, 1 + step), 0)
        lax.fori_loop(0, (XE - 2 * step - 2) // 2, pair(stress, 2 + step), 0)

        def sensitivities(x, carry):
            e = x + 1 + W
            f = [forward_ref[step, c, x].astype(jnp.float32) for c in range(9)]
            change = [change_ref[c, e] for c in range(3)]
            rate = [rate_ref[c, e] for c in range(6)]
            kernels_ref[0, x] += f[0] * change[0] + f[1] * change[1] + f[2] * change[2]
            trace = rate[0] + rate[1] + rate[2]
            kernels_ref[1, x] += DT * (f[3] + f[4] + f[5]) * trace
            kernels_ref[2, x] += (
                DT
                * 2.0
                * (
                    (f[3] * rate[0] + f[4] * rate[1] + f[5] * rate[2])
                    + 2.0 * (f[6] * rate[3] + f[7] * rate[4] + f[8] * rate[5])
                )
            )
            return carry

        lax.fori_loop(0, B, sensitivities, 0, unroll=2)

    for f in range(9):
        for x in range(B):
            state_ref[f, x] = ext[pl.ds(f * plane + (x + 1 + W) * YR, 8), :]


def sum_kernel(events, parts_ref, out_ref):
    size = parts_ref.shape[0] // events
    total = parts_ref[0:size]
    for s in range(1, events):
        total = total + parts_ref[size * s : size * s + size]
    for s in range(events):
        out_ref[size * s : size * s + size] = total


def f32(*shape):
    return jax.ShapeDtypeStruct(shape, jnp.float32)


def on_device(
    adjoint_state,
    forward_state,
    inv_density,
    lame_lambda,
    shear_modulus,
    station_block,
    station_cell,
    station_trace,
    source_count,
):
    n_sx, n_sy, n_ev = lax.axis_size("sx"), lax.axis_size("sy"), lax.axis_size("ev")
    steps = forward_state.shape[1]
    ny = n_sy * B
    adj = adjoint_state[0]
    up_x = [(i, i + 1) for i in range(n_sx - 1)]
    up_y = [(i, i + 1) for i in range(n_sy - 1)]
    down_x = [(b, a) for a, b in up_x]
    down_y = [(b, a) for a, b in up_y]

    low_face, high_face = pl.pallas_call(
        functools.partial(x_faces_kernel, ny),
        out_shape=[f32(13, W, 8, 128)] * 2,
        in_specs=[SMEM] + [VMEM] * 7,
        out_specs=[VMEM] * 2,
        compiler_params=pltpu.CompilerParams(vmem_limit_bytes=3 * MIB),
        name="x_faces",
    )(
        source_count,
        adj,
        inv_density,
        lame_lambda,
        shear_modulus,
        station_block[0],
        station_cell,
        station_trace[0],
    )
    low = lax.ppermute(high_face, "sx", up_x)
    high = lax.ppermute(low_face, "sx", down_x)

    flat = lambda a: a.reshape(-1, 128)
    y_low_face, y_high_face, tiles = pl.pallas_call(
        functools.partial(y_faces_kernel, ny),
        out_shape=[f32(W * FIELDS * YR, 128)] * 2 + [f32(n_sy, 8, 128)],
        in_specs=[VMEM] * 7,
        out_specs=[VMEM] * 3,
        compiler_params=pltpu.CompilerParams(vmem_limit_bytes=4 * MIB),
        name="y_faces",
    )(
        flat(adj),
        flat(inv_density),
        flat(lame_lambda),
        flat(shear_modulus),
        flat(low_face),
        flat(low),
        flat(high),
    )
    y_low = lax.ppermute(y_high_face, "sy", up_y)
    y_high = lax.ppermute(y_low_face, "sy", down_y)
    tiles = lax.all_to_all(tiles, "sy", split_axis=0, concat_axis=0, tiled=True)

    place = lax.axis_index("sy").astype(jnp.int32).reshape(1)
    state, kernels = pl.pallas_call(
        functools.partial(steps_kernel, ny, steps),
        out_shape=[f32(9, B, 8, 128), f32(3, B, 8, 128)],
        in_specs=[SMEM] + [VMEM] * 10,
        out_specs=[VMEM] * 2,
        scratch_shapes=[
            pltpu.VMEM((FIELDS * XS * YR, 128), jnp.float32),
            pltpu.VMEM((3 * steps, XE * YR, 128), jnp.float32),
            pltpu.VMEM((3, XS, 8, 128), jnp.float32),
            pltpu.VMEM((6, XS, 8, 128), jnp.float32),
        ],
        compiler_params=pltpu.CompilerParams(vmem_limit_bytes=8 * MIB),
        name="steps",
    )(
        place,
        adj,
        inv_density,
        lame_lambda,
        shear_modulus,
        forward_state[0],
        low,
        high,
        y_low,
        y_high,
        tiles,
    )

    parts = lax.all_to_all(kernels.reshape(3 * B, 8, 128), "ev", split_axis=0, concat_axis=0, tiled=True)
    shared = pl.pallas_call(
        functools.partial(sum_kernel, n_ev), out_shape=f32(3 * B, 8, 128), in_specs=[VMEM], out_specs=VMEM, compiler_params=pltpu.CompilerParams(vmem_limit_bytes=1 * MIB),
        name="event_sum"
    )(parts)
    total = lax.all_to_all(shared, "ev", split_axis=0, concat_axis=0, tiled=True)
    return state[None], total.reshape(3, B, 8, 128)


def solution(mesh):
    return jax.shard_map(
        on_device,
        mesh=mesh,
        in_specs=(
            P("ev", None, "sx", "sy", None),
            P("ev", None, None, "sx", "sy", None),
            P("sx", "sy", None),
            P("sx", "sy", None),
            P("sx", "sy", None),
            P("ev", ("sx", "sy"), None),
            P("ev", ("sx", "sy")),
            P("ev", ("sx", "sy"), None),
            P("ev", ("sx", "sy")),
        ),
        out_specs=(P("ev", None, "sx", "sy", None), P(None, "sx", "sy", None)),
        check_vma=False,
    )
```

```python
import functools

import jax
import jax.numpy as jnp
from jax import lax
from jax.experimental import pallas as pl
from jax.experimental.pallas import tpu as pltpu
from jax.sharding import PartitionSpec as P

DT = 0.35
W = 3
B = 8
XE = B + 2 * W
XS = XE + 2
YR = 16
FIELDS = 12
PLANE = XS * YR
DEAD = -1.0e6
MIB = 1 << 20
VMEM = pl.BlockSpec(memory_space=pltpu.VMEM)
SMEM = pl.BlockSpec(memory_space=pltpu.SMEM)
HBM = pl.BlockSpec(memory_space=pltpu.HBM)


def x_faces_kernel(adj_ref, rho_ref, lam_ref, mu_ref, low_ref, high_ref, base_ref, sems):
    copies = []
    for side, (out, first) in enumerate(((low_ref, 0), (high_ref, B - W))):
        pieces = [(adj_ref.at[:, pl.ds(first, W)], out.at[pl.ds(0, 9)])]
        pieces += [(p.at[pl.ds(first, W)], out.at[9 + i]) for i, p in enumerate((rho_ref, lam_ref, mu_ref))]
        for i, (source, target) in enumerate(pieces):
            copies.append(pltpu.make_async_copy(source, target, sems.at[side, i]))
    copies.append(pltpu.make_async_copy(adj_ref, base_ref.at[pl.ds(0, 9)], sems.at[2, 0]))
    for i, p in enumerate((rho_ref, lam_ref, mu_ref)):
        copies.append(pltpu.make_async_copy(p, base_ref.at[9 + i], sems.at[2, 1 + i]))
    for copy in copies:
        copy.start()
    for copy in copies:
        copy.wait()


def stations_kernel(ny, count_ref, block_hbm, cell_hbm, trace_hbm, tiles_ref, block_ref, cell_ref, trace_ref, sems):
    moves = ((block_hbm, block_ref), (cell_hbm, cell_ref), (trace_hbm, trace_ref))
    copies = [pltpu.make_async_copy(source, target, sems.at[i]) for i, (source, target) in enumerate(moves)]
    for copy in copies:
        copy.start()
    for copy in copies:
        copy.wait()
    rows = cell_ref.shape[1]
    cell = cell_ref[...]
    key = ((cell // B) * ny + block_ref[...] * B + cell % B).astype(jnp.float32)
    live = lax.broadcasted_iota(jnp.int32, (1, rows), 1) < count_ref[0, 0]
    parts = [jnp.where(live, key, DEAD)] + [jnp.where(live, trace_ref[k], 0.0) for k in range(9)]
    parts += [jnp.zeros((1, rows), jnp.float32)] * 6
    tile = jnp.concatenate(
        [jnp.concatenate(parts[:8], axis=0), jnp.concatenate(parts[8:], axis=0), jnp.zeros((8, 128 - 2 * rows), jnp.float32)],
        axis=1,
    )
    for d in range(tiles_ref.shape[0]):
        tiles_ref[d] = tile


def y_faces_kernel(base_ref, low_ref, high_ref, face_low_ref, face_high_ref):
    for out, first in ((face_low_ref, 0), (face_high_ref, B - W)):
        for f in range(FIELDS):
            for r in range(W):
                y = first + r
                at = (r * FIELDS + f) * YR
                out[pl.ds(at, W), :] = low_ref[pl.ds(f * 24 + y, W, stride=8), :]
                out[pl.ds(at + W, B), :] = base_ref[pl.ds(f * 64 + y, B, stride=8), :]
                out[pl.ds(at + W + B, W), :] = high_ref[pl.ds(f * 24 + y, W, stride=8), :]
                out[pl.ds(at + XE, YR - XE), :] = jnp.zeros((YR - XE, 128), jnp.float32)


def surface_kernel(ny, place_ref, tiles_ref, own_ref, low_ref, high_ref):
    cells = B * YR
    at = lax.broadcasted_iota(jnp.int32, (cells, 128), 0)
    local = at % YR
    local = jnp.where(local < 11, local, local - YR)
    y = place_ref[0] * B + local
    ident = jnp.where((y >= 0) & (y < ny), (at // YR) * ny + y, -10000000).astype(jnp.float32)
    group = lax.broadcasted_iota(jnp.int32, (8, 128), 1) // 32
    hot, packed = [], []
    for first in range(0, tiles_ref.shape[0], 4):
        heads = jnp.where(group == 0, tiles_ref[first], 0.0)
        tails = jnp.where(group == 0, pltpu.roll(tiles_ref[first], 96, 1), 0.0)
        for i in range(1, 4):
            tile = tiles_ref[first + i]
            heads = jnp.where(group == i, pltpu.roll(tile, 32 * i, 1), heads)
            tails = jnp.where(group == i, pltpu.roll(tile, (96 + 32 * i) % 128, 1) if i > 1 else tile, tails)
        hot.append((ident == heads[0:1]).astype(jnp.float32))
        packed.append(jnp.concatenate([heads, tails], axis=0))
    packed = jnp.concatenate(packed, axis=1)
    packed = jnp.concatenate([packed, jnp.zeros((112, packed.shape[1]), jnp.float32)], axis=0)
    surface = lax.dot_general(
        jnp.concatenate(hot, axis=1),
        packed,
        (((1,), (1,)), ((), ())),
        precision=lax.Precision.HIGHEST,
        preferred_element_type=jnp.float32,
    )
    own_ref[...] = surface
    low_ref[...] = surface[0 : W * YR]
    high_ref[...] = surface[(B - W) * YR :]


def block_kernel(base_ref, low_ref, high_ref, ext):
    zero8 = jnp.zeros((8, 128), jnp.float32)
    for f in range(FIELDS):
        for e in range(XS):
            at = f * PLANE + e * YR
            if e == 0 or e == XS - 1:
                ext[pl.ds(at, 8), :] = zero8
            elif e <= W:
                ext[pl.ds(at, 8), :] = low_ref[f, e - 1]
            elif e <= W + B:
                ext[pl.ds(at, 8), :] = base_ref[f, e - 1 - W]
            else:
                ext[pl.ds(at, 8), :] = high_ref[f, e - 1 - W - B]
            ext[pl.ds(at + 8, 8), :] = zero8


def steps_kernel(
    steps,
    _,
    forward_ref,
    y_low_ref,
    y_high_ref,
    own_ref,
    low_ref,
    high_ref,
    ext,
    state_ref,
    kernels_ref,
    force_ref,
    change_ref,
    rate_ref,
    sem,
):
    for f in range(FIELDS):
        for r in range(W):
            src = (r * FIELDS + f) * YR
            ext[pl.ds(f * PLANE + YR + 8 + r, XE, stride=YR), :] = y_high_ref[pl.ds(src, XE), :]
            ext[pl.ds(f * PLANE + YR + 13 + r, XE, stride=YR), :] = y_low_ref[pl.ds(src, XE), :]
    force_ref[pl.ds(0, W * YR), :] = low_ref[...]
    force_ref[pl.ds(W * YR, B * YR), :] = own_ref[...]
    force_ref[pl.ds((W + B) * YR, W * YR), :] = high_ref[...]

    lanes = lax.broadcasted_iota(jnp.int32, (YR, 128), 1)

    def y_up(v):
        return pltpu.roll(v, YR - 1, 0)

    def y_down(v):
        return pltpu.roll(v, 1, 0)

    def z_up(v):
        return jnp.where(lanes == 127, 0.0, pltpu.roll(v, 127, 1))

    def z_down(v):
        return jnp.where(lanes == 0, 0.0, pltpu.roll(v, 1, 1))

    def get(f, e):
        return ext[pl.ds(pl.multiple_of(f * PLANE + e * YR, YR), YR), :]

    def put(f, e, v):
        ext[pl.ds(pl.multiple_of(f * PLANE + e * YR, YR), YR), :] = v

    for step in range(steps):

        def velocity(e):
            sxx, syy, szz, sxy, sxz, syz = [get(3 + f, e) for f in range(6)]
            ax = (get(3, e + 1) - sxx) + (sxy - y_down(sxy)) + (sxz - z_down(sxz))
            ay = (sxy - get(6, e - 1)) + (y_up(syy) - syy) + (syz - z_down(syz))
            az = (sxz - get(7, e - 1)) + (syz - y_down(syz)) + (z_up(szz) - szz)
            scale = DT * get(9, e)
            surface = force_ref[pl.ds(pl.multiple_of((e - 1) * YR, YR), YR), :]
            for c, accel in enumerate((ax, ay, az)):
                force = jnp.where(lanes == 0, pltpu.roll(surface, 127 - 3 * step - c, 1), 0.0)
                change = scale * (accel + force)
                put(c, e, get(c, e) + change)
                change_ref[c, e] = change[0:8]

        def stress(e):
            vx, vy, vz = [get(f, e) for f in range(3)]
            exx = vx - get(0, e - 1)
            eyy = vy - y_down(vy)
            ezz = vz - z_down(vz)
            exy = 0.5 * ((y_up(vx) - vx) + (get(1, e + 1) - vy))
            exz = 0.5 * ((z_up(vx) - vx) + (get(2, e + 1) - vz))
            eyz = 0.5 * ((z_up(vy) - vy) + (y_up(vz) - vz))
            trace = exx + eyy + ezz
            lam = get(10, e) * trace
            twice = 2.0 * get(11, e)
            for f, rate in enumerate((exx, eyy, ezz, exy, exz, eyz)):
                if f < 3:
                    put(3 + f, e, get(3 + f, e) + DT * (lam + twice * rate))
                else:
                    put(3 + f, e, get(3 + f, e) + DT * twice * rate)
                rate_ref[f, e] = rate[0:8]

        def pair(body, first):
            def run(i, carry):
                e = first + 2 * i
                body(e)
                body(e + 1)
                return carry

            return run

        lax.fori_loop(0, (XE - 2 * step) // 2, pair(velocity, 1 + step), 0)
        lax.fori_loop(0, (XE - 2 * step - 2) // 2, pair(stress, 2 + step), 0)
        if step == steps - 1:
            copies = [
                pltpu.make_async_copy(
                    ext.reshape(FIELDS, XS, YR, 128).at[f, pl.ds(1 + W, B), pl.ds(0, B)], state_ref.at[f], sem.at[f]
                )
                for f in range(9)
            ]
            for copy in copies:
                copy.start()

        def sensitivities(x, carry):
            e = x + 1 + W
            f = [forward_ref[step, c, x].astype(jnp.float32) for c in range(9)]
            change = [change_ref[c, e] for c in range(3)]
            rate = [rate_ref[c, e] for c in range(6)]
            trace = rate[0] + rate[1] + rate[2]
            terms = (
                f[0] * change[0] + f[1] * change[1] + f[2] * change[2],
                DT * (f[3] + f[4] + f[5]) * trace,
                DT
                * 2.0
                * (
                    (f[3] * rate[0] + f[4] * rate[1] + f[5] * rate[2])
                    + 2.0 * (f[6] * rate[3] + f[7] * rate[4] + f[8] * rate[5])
                ),
            )
            for k, term in enumerate(terms):
                kernels_ref[k, x] = kernels_ref[k, x] + term if step else term
            return carry

        lax.fori_loop(0, B, sensitivities, 0, unroll=4)

    for copy in copies:
        copy.wait()


def sum_kernel(events, parts_ref, out_ref):
    size = parts_ref.shape[0] // events
    total = parts_ref[0:size]
    for s in range(1, events):
        total = total + parts_ref[size * s : size * s + size]
    for s in range(events):
        out_ref[size * s : size * s + size] = total


def f32(*shape):
    return jax.ShapeDtypeStruct(shape, jnp.float32)


def in_hbm(a):
    return pltpu.with_memory_space_constraint(a, pltpu.HBM)


def on_device(
    adjoint_state,
    forward_state,
    inv_density,
    lame_lambda,
    shear_modulus,
    station_block,
    station_cell,
    station_trace,
    source_count,
):
    n_sx, n_sy, n_ev = lax.axis_size("sx"), lax.axis_size("sy"), lax.axis_size("ev")
    steps = forward_state.shape[1]
    ny = n_sy * B
    adj = adjoint_state[0]
    up_x = [(i, i + 1) for i in range(n_sx - 1)]
    up_y = [(i, i + 1) for i in range(n_sy - 1)]
    down_x = [(b, a) for a, b in up_x]
    down_y = [(b, a) for a, b in up_y]

    low_face, high_face, base = pl.pallas_call(
        x_faces_kernel,
        out_shape=[f32(FIELDS, W, 8, 128)] * 2 + [f32(FIELDS, B, 8, 128)],
        in_specs=[HBM] * 4,
        out_specs=[VMEM] * 3,
        scratch_shapes=[pltpu.SemaphoreType.DMA((3, 4))],
        compiler_params=pltpu.CompilerParams(vmem_limit_bytes=3 * MIB),
        name="x_faces",
    )(in_hbm(adj), in_hbm(inv_density), in_hbm(lame_lambda), in_hbm(shear_modulus))
    low = lax.ppermute(high_face, "sx", up_x)
    high = lax.ppermute(low_face, "sx", down_x)

    rows = station_cell.shape[1]
    tiles = pl.pallas_call(
        functools.partial(stations_kernel, ny),
        out_shape=f32(n_sy, 8, 128),
        in_specs=[SMEM] + [HBM] * 3,
        out_specs=VMEM,
        scratch_shapes=[
            pltpu.VMEM((1, rows), jnp.int32),
            pltpu.VMEM((1, rows), jnp.int32),
            pltpu.VMEM((9, 1, rows), jnp.float32),
            pltpu.SemaphoreType.DMA((3,)),
        ],
        compiler_params=pltpu.CompilerParams(vmem_limit_bytes=MIB),
        name="stations",
    )(
        source_count,
        in_hbm(station_block[:, :, 0]),
        in_hbm(station_cell),
        in_hbm(jnp.transpose(station_trace, (2, 0, 1))),
    )
    tiles = lax.all_to_all(tiles, "sy", split_axis=0, concat_axis=0, tiled=True)

    flat = lambda a: a.reshape(-1, 128)
    y_low_face, y_high_face = pl.pallas_call(
        y_faces_kernel,
        out_shape=[f32(W * FIELDS * YR, 128)] * 2,
        in_specs=[VMEM] * 3,
        out_specs=[VMEM] * 2,
        compiler_params=pltpu.CompilerParams(vmem_limit_bytes=4 * MIB),
        name="y_faces",
    )(flat(base), flat(low), flat(high))
    y_low = lax.ppermute(y_high_face, "sy", up_y)
    y_high = lax.ppermute(y_low_face, "sy", down_y)

    place = lax.axis_index("sy").astype(jnp.int32).reshape(1)
    own_surface, low_surface, high_surface = pl.pallas_call(
        functools.partial(surface_kernel, ny),
        out_shape=[f32(B * YR, 128), f32(W * YR, 128), f32(W * YR, 128)],
        in_specs=[SMEM, VMEM],
        out_specs=[VMEM] * 3,
        compiler_params=pltpu.CompilerParams(vmem_limit_bytes=4 * MIB),
        name="surface",
    )(place, tiles)
    below = lax.ppermute(high_surface, "sx", up_x)
    above = lax.ppermute(low_surface, "sx", down_x)

    ext = pl.pallas_call(
        block_kernel,
        out_shape=f32(FIELDS * PLANE, 128),
        in_specs=[VMEM] * 3,
        out_specs=VMEM,
        compiler_params=pltpu.CompilerParams(vmem_limit_bytes=4 * MIB),
        name="block",
    )(base, low, high)

    _, state, kernels = pl.pallas_call(
        functools.partial(steps_kernel, steps),
        out_shape=[f32(FIELDS * PLANE, 128), f32(9, B, 8, 128), f32(3, B, 8, 128)],
        in_specs=[VMEM] * 7,
        out_specs=[VMEM, HBM, VMEM],
        input_output_aliases={0: 0},
        scratch_shapes=[
            pltpu.VMEM((XE * YR, 128), jnp.float32),
            pltpu.VMEM((3, XS, 8, 128), jnp.float32),
            pltpu.VMEM((6, XS, 8, 128), jnp.float32),
            pltpu.SemaphoreType.DMA((9,)),
        ],
        compiler_params=pltpu.CompilerParams(vmem_limit_bytes=8 * MIB),
        name="steps",
    )(ext, forward_state[0], y_low, y_high, own_surface, below, above)

    parts = lax.all_to_all(kernels.reshape(3 * B, 8, 128), "ev", split_axis=0, concat_axis=0, tiled=True)
    shared = pl.pallas_call(
        functools.partial(sum_kernel, n_ev), out_shape=f32(3 * B, 8, 128), in_specs=[VMEM], out_specs=VMEM, compiler_params=pltpu.CompilerParams(vmem_limit_bytes=1 * MIB),
        name="event_sum"
    )(parts)
    total = lax.all_to_all(shared, "ev", split_axis=0, concat_axis=0, tiled=True)
    return state[None], total.reshape(3, B, 8, 128)


def solution(mesh):
    return jax.shard_map(
        on_device,
        mesh=mesh,
        in_specs=(
            P("ev", None, "sx", "sy", None),
            P("ev", None, None, "sx", "sy", None),
            P("sx", "sy", None),
            P("sx", "sy", None),
            P("sx", "sy", None),
            P("ev", ("sx", "sy"), None),
            P("ev", ("sx", "sy")),
            P("ev", ("sx", "sy"), None),
            P("ev", ("sx", "sy")),
        ),
        out_specs=(P("ev", None, "sx", "sy", None), P(None, "sx", "sy", None)),
        check_vma=False,
    )
```

```python
import functools

import jax
import jax.numpy as jnp
from jax import lax
from jax.experimental import pallas as pl
from jax.experimental.pallas import tpu as pltpu
from jax.sharding import PartitionSpec as P

DT = 0.35
W = 3
B = 8
XE = B + 2 * W
XS = XE + 2
YR = 16
FIELDS = 12
PLANE = XS * YR
DEAD = -1.0e6
MIB = 1 << 20
VMEM = pl.BlockSpec(memory_space=pltpu.VMEM)
SMEM = pl.BlockSpec(memory_space=pltpu.SMEM)
HBM = pl.BlockSpec(memory_space=pltpu.HBM)


def x_faces_kernel(
    ny,
    adj_hbm,
    rho_hbm,
    lam_hbm,
    mu_hbm,
    count_ref,
    block_hbm,
    cell_hbm,
    trace_hbm,
    low_ref,
    high_ref,
    base_ref,
    block_ref,
    cell_ref,
    trace_ref,
    sems,
):
    params = (rho_hbm, lam_hbm, mu_hbm)
    rows_in = [
        pltpu.make_async_copy(source, target, sems.at[3, i])
        for i, (source, target) in enumerate(((block_hbm, block_ref), (cell_hbm, cell_ref), (trace_hbm, trace_ref)))
    ]
    copies = []
    for side, (out, first) in enumerate(((low_ref, 0), (high_ref, B - W))):
        pieces = [(adj_hbm.at[:, pl.ds(first, W)], out.at[pl.ds(0, 9)])]
        pieces += [(p.at[pl.ds(first, W)], out.at[9 + i]) for i, p in enumerate(params)]
        for i, (source, target) in enumerate(pieces):
            copies.append(pltpu.make_async_copy(source, target, sems.at[side, i]))
    copies.append(pltpu.make_async_copy(adj_hbm, base_ref.at[pl.ds(0, 9)], sems.at[2, 0]))
    for i, p in enumerate(params):
        copies.append(pltpu.make_async_copy(p, base_ref.at[9 + i], sems.at[2, 1 + i]))
    for copy in rows_in + copies:
        copy.start()
    for copy in rows_in:
        copy.wait()
    rows = cell_ref.shape[1]
    cell = cell_ref[...]
    key = ((cell // B) * ny + block_ref[...] * B + cell % B).astype(jnp.float32)
    live = lax.broadcasted_iota(jnp.int32, (1, rows), 1) < count_ref[0, 0]
    parts = [jnp.where(live, key, DEAD)] + [jnp.where(live, trace_ref[k], 0.0) for k in range(9)]
    parts += [jnp.zeros((1, rows), jnp.float32)] * 6
    pack = jnp.concatenate(
        [jnp.concatenate(parts[:8], axis=0), jnp.concatenate(parts[8:], axis=0), jnp.zeros((8, 128 - 2 * rows), jnp.float32)],
        axis=1,
    )
    for out in (low_ref, high_ref):
        out[FIELDS, 0] = pack
        for spare in range(1, W):
            out[FIELDS, spare] = jnp.zeros((8, 128), jnp.float32)
    for copy in copies:
        copy.wait()


def tiles_kernel(ny, own_ref, low_ref, high_ref, tiles_ref):
    row = lax.broadcasted_iota(jnp.int32, (8, 128), 0)
    group = lax.broadcasted_iota(jnp.int32, (8, 128), 1) // 32
    tile = jnp.zeros((8, 128), jnp.float32)
    for s, (ref, shift) in enumerate(((own_ref, W), (low_ref, W - B), (high_ref, W + B))):
        pack = ref[FIELDS, 0]
        head = jnp.where(row == 0, pack + float(shift * ny), pack)
        head = pltpu.roll(head, 32 * s, 1) if s else head
        tail = pltpu.roll(pack, 64, 1)
        tail = pltpu.roll(tail, 2 * s, 0) if s else tail
        tile = jnp.where(group == s, head, tile)
        tile = jnp.where((group == 3) & (row // 2 == s), tail, tile)
    for d in range(tiles_ref.shape[0]):
        tiles_ref[d] = tile


def y_faces_kernel(base_ref, low_ref, high_ref, face_low_ref, face_high_ref):
    for out, first in ((face_low_ref, 0), (face_high_ref, B - W)):
        for f in range(FIELDS):
            for r in range(W):
                y = first + r
                at = (r * FIELDS + f) * YR
                out[pl.ds(at, W), :] = low_ref[pl.ds(f * 24 + y, W, stride=8), :]
                out[pl.ds(at + W, B), :] = base_ref[pl.ds(f * 64 + y, B, stride=8), :]
                out[pl.ds(at + W + B, W), :] = high_ref[pl.ds(f * 24 + y, W, stride=8), :]
                out[pl.ds(at + XE, YR - XE), :] = jnp.zeros((YR - XE, 128), jnp.float32)


def surface_kernel(ny, place_ref, tiles_ref, surface_ref):
    group = lax.broadcasted_iota(jnp.int32, (8, 128), 1) // 32
    for s, first, count in ((0, W, B), (1, 0, W), (2, W + B, W)):
        cells = count * YR
        at = lax.broadcasted_iota(jnp.int32, (cells, 128), 0)
        local = at % YR
        local = jnp.where(local < 11, local, local - YR)
        y = place_ref[0] * B + local
        ident = jnp.where((y >= 0) & (y < ny), (first + at // YR) * ny + y, -10000000).astype(jnp.float32)
        hot, packed = [], []
        for source in range(0, tiles_ref.shape[0], 4):
            heads = tails = jnp.zeros((8, 128), jnp.float32)
            for i in range(4):
                tile = tiles_ref[source + i]
                head, tail = (32 * (i - s)) % 128, (32 * (i - 3)) % 128
                heads = jnp.where(group == i, pltpu.roll(tile, head, 1) if head else tile, heads)
                tails = jnp.where(group == i, pltpu.roll(tile, tail, 1) if tail else tile, tails)
            hot.append((ident == heads[0:1]).astype(jnp.float32))
            packed.append(jnp.concatenate([heads, pltpu.roll(tails, 8 - 2 * s, 0) if s else tails], axis=0))
        packed = jnp.concatenate(packed, axis=1)
        packed = jnp.concatenate([packed, jnp.zeros((112, packed.shape[1]), jnp.float32)], axis=0)
        surface_ref[pl.ds(first * YR, cells), :] = lax.dot_general(
            jnp.concatenate(hot, axis=1),
            packed,
            (((1,), (1,)), ((), ())),
            precision=lax.Precision.HIGHEST,
            preferred_element_type=jnp.float32,
        )


def block_kernel(base_ref, low_ref, high_ref, ext):
    zero8 = jnp.zeros((8, 128), jnp.float32)
    for f in range(FIELDS):
        for e in range(XS):
            at = f * PLANE + e * YR
            if e == 0 or e == XS - 1:
                ext[pl.ds(at, 8), :] = zero8
            elif e <= W:
                ext[pl.ds(at, 8), :] = low_ref[f, e - 1]
            elif e <= W + B:
                ext[pl.ds(at, 8), :] = base_ref[f, e - 1 - W]
            else:
                ext[pl.ds(at, 8), :] = high_ref[f, e - 1 - W - B]
            ext[pl.ds(at + 8, 8), :] = zero8


def steps_kernel(
    steps,
    _,
    forward_ref,
    y_low_ref,
    y_high_ref,
    force_ref,
    ext,
    state_ref,
    kernels_ref,
    change_ref,
    rate_ref,
    sem,
):
    for f in range(FIELDS):
        for r in range(W):
            src = (r * FIELDS + f) * YR
            ext[pl.ds(f * PLANE + YR + 8 + r, XE, stride=YR), :] = y_high_ref[pl.ds(src, XE), :]
            ext[pl.ds(f * PLANE + YR + 13 + r, XE, stride=YR), :] = y_low_ref[pl.ds(src, XE), :]

    lanes = lax.broadcasted_iota(jnp.int32, (YR, 128), 1)

    def y_up(v):
        return pltpu.roll(v, YR - 1, 0)

    def y_down(v):
        return pltpu.roll(v, 1, 0)

    def z_up(v):
        return jnp.where(lanes == 127, 0.0, pltpu.roll(v, 127, 1))

    def z_down(v):
        return jnp.where(lanes == 0, 0.0, pltpu.roll(v, 1, 1))

    def get(f, e):
        return ext[pl.ds(pl.multiple_of(f * PLANE + e * YR, YR), YR), :]

    def put(f, e, v):
        ext[pl.ds(pl.multiple_of(f * PLANE + e * YR, YR), YR), :] = v

    for step in range(steps):

        def velocity(e):
            sxx, syy, szz, sxy, sxz, syz = [get(3 + f, e) for f in range(6)]
            ax = (get(3, e + 1) - sxx) + (sxy - y_down(sxy)) + (sxz - z_down(sxz))
            ay = (sxy - get(6, e - 1)) + (y_up(syy) - syy) + (syz - z_down(syz))
            az = (sxz - get(7, e - 1)) + (syz - y_down(syz)) + (z_up(szz) - szz)
            scale = DT * get(9, e)
            surface = force_ref[pl.ds(pl.multiple_of((e - 1) * YR, YR), YR), :]
            for c, accel in enumerate((ax, ay, az)):
                force = jnp.where(lanes == 0, pltpu.roll(surface, 127 - 3 * step - c, 1), 0.0)
                change = scale * (accel + force)
                put(c, e, get(c, e) + change)
                change_ref[c, e] = change[0:8]

        def stress(e):
            vx, vy, vz = [get(f, e) for f in range(3)]
            exx = vx - get(0, e - 1)
            eyy = vy - y_down(vy)
            ezz = vz - z_down(vz)
            exy = 0.5 * ((y_up(vx) - vx) + (get(1, e + 1) - vy))
            exz = 0.5 * ((z_up(vx) - vx) + (get(2, e + 1) - vz))
            eyz = 0.5 * ((z_up(vy) - vy) + (y_up(vz) - vz))
            trace = exx + eyy + ezz
            lam = get(10, e) * trace
            twice = 2.0 * get(11, e)
            for f, rate in enumerate((exx, eyy, ezz, exy, exz, eyz)):
                if f < 3:
                    put(3 + f, e, get(3 + f, e) + DT * (lam + twice * rate))
                else:
                    put(3 + f, e, get(3 + f, e) + DT * twice * rate)
                rate_ref[f, e] = rate[0:8]

        def pair(body, first):
            def run(i, carry):
                e = first + 2 * i
                body(e)
                body(e + 1)
                return carry

            return run

        lax.fori_loop(0, (XE - 2 * step) // 2, pair(velocity, 1 + step), 0)
        lax.fori_loop(0, (XE - 2 * step - 2) // 2, pair(stress, 2 + step), 0)
        if step == steps - 1:
            copies = [
                pltpu.make_async_copy(
                    ext.reshape(FIELDS, XS, YR, 128).at[f, pl.ds(1 + W, B), pl.ds(0, B)], state_ref.at[f], sem.at[f]
                )
                for f in range(9)
            ]
            for copy in copies:
                copy.start()

        def sensitivities(x, carry):
            e = x + 1 + W
            f = [forward_ref[step, c, x].astype(jnp.float32) for c in range(9)]
            change = [change_ref[c, e] for c in range(3)]
            rate = [rate_ref[c, e] for c in range(6)]
            trace = rate[0] + rate[1] + rate[2]
            terms = (
                f[0] * change[0] + f[1] * change[1] + f[2] * change[2],
                DT * (f[3] + f[4] + f[5]) * trace,
                DT
                * 2.0
                * (
                    (f[3] * rate[0] + f[4] * rate[1] + f[5] * rate[2])
                    + 2.0 * (f[6] * rate[3] + f[7] * rate[4] + f[8] * rate[5])
                ),
            )
            for k, term in enumerate(terms):
                kernels_ref[k, x] = kernels_ref[k, x] + term if step else term
            return carry

        lax.fori_loop(0, B, sensitivities, 0, unroll=4)

    for copy in copies:
        copy.wait()


def sum_kernel(events, parts_ref, out_ref):
    size = parts_ref.shape[0] // events
    total = parts_ref[0:size]
    for s in range(1, events):
        total = total + parts_ref[size * s : size * s + size]
    for s in range(events):
        out_ref[size * s : size * s + size] = total


def f32(*shape):
    return jax.ShapeDtypeStruct(shape, jnp.float32)


def in_hbm(a):
    return pltpu.with_memory_space_constraint(a, pltpu.HBM)


def on_device(
    adjoint_state,
    forward_state,
    inv_density,
    lame_lambda,
    shear_modulus,
    station_block,
    station_cell,
    station_trace,
    source_count,
):
    n_sx, n_sy, n_ev = lax.axis_size("sx"), lax.axis_size("sy"), lax.axis_size("ev")
    steps = forward_state.shape[1]
    ny = n_sy * B
    adj = adjoint_state[0]
    up_x = [(i, i + 1) for i in range(n_sx - 1)]
    up_y = [(i, i + 1) for i in range(n_sy - 1)]
    down_x = [(b, a) for a, b in up_x]
    down_y = [(b, a) for a, b in up_y]

    rows = station_cell.shape[1]
    low_face, high_face, base = pl.pallas_call(
        functools.partial(x_faces_kernel, ny),
        out_shape=[f32(FIELDS + 1, W, 8, 128)] * 2 + [f32(FIELDS, B, 8, 128)],
        in_specs=[HBM] * 4 + [SMEM] + [HBM] * 3,
        out_specs=[VMEM] * 3,
        scratch_shapes=[
            pltpu.VMEM((1, rows), jnp.int32),
            pltpu.VMEM((1, rows), jnp.int32),
            pltpu.VMEM((9, 1, rows), jnp.float32),
            pltpu.SemaphoreType.DMA((4, 4)),
        ],
        compiler_params=pltpu.CompilerParams(vmem_limit_bytes=3 * MIB),
        name="x_faces",
    )(
        in_hbm(adj),
        in_hbm(inv_density),
        in_hbm(lame_lambda),
        in_hbm(shear_modulus),
        source_count,
        in_hbm(station_block[:, :, 0]),
        in_hbm(station_cell),
        in_hbm(jnp.transpose(station_trace, (2, 0, 1))),
    )
    low = lax.ppermute(high_face, "sx", up_x)
    high = lax.ppermute(low_face, "sx", down_x)

    tiles = pl.pallas_call(
        functools.partial(tiles_kernel, ny),
        out_shape=f32(n_sy, 8, 128),
        in_specs=[VMEM] * 3,
        out_specs=VMEM,
        compiler_params=pltpu.CompilerParams(vmem_limit_bytes=2 * MIB),
        name="tiles",
    )(low_face, low, high)
    tiles = lax.all_to_all(tiles, "sy", split_axis=0, concat_axis=0, tiled=True)

    flat = lambda a: a.reshape(-1, 128)
    y_low_face, y_high_face = pl.pallas_call(
        y_faces_kernel,
        out_shape=[f32(W * FIELDS * YR, 128)] * 2,
        in_specs=[VMEM] * 3,
        out_specs=[VMEM] * 2,
        compiler_params=pltpu.CompilerParams(vmem_limit_bytes=4 * MIB),
        name="y_faces",
    )(flat(base), flat(low), flat(high))
    y_low = lax.ppermute(y_high_face, "sy", up_y)
    y_high = lax.ppermute(y_low_face, "sy", down_y)

    place = lax.axis_index("sy").astype(jnp.int32).reshape(1)
    surface = pl.pallas_call(
        functools.partial(surface_kernel, ny),
        out_shape=f32(XE * YR, 128),
        in_specs=[SMEM, VMEM],
        out_specs=VMEM,
        compiler_params=pltpu.CompilerParams(vmem_limit_bytes=4 * MIB),
        name="surface",
    )(place, tiles)

    ext = pl.pallas_call(
        block_kernel,
        out_shape=f32(FIELDS * PLANE, 128),
        in_specs=[VMEM] * 3,
        out_specs=VMEM,
        compiler_params=pltpu.CompilerParams(vmem_limit_bytes=4 * MIB),
        name="block",
    )(base, low, high)

    _, state, kernels = pl.pallas_call(
        functools.partial(steps_kernel, steps),
        out_shape=[f32(FIELDS * PLANE, 128), f32(9, B, 8, 128), f32(3, B, 8, 128)],
        in_specs=[VMEM] * 5,
        out_specs=[VMEM, HBM, VMEM],
        input_output_aliases={0: 0},
        scratch_shapes=[
            pltpu.VMEM((3, XS, 8, 128), jnp.float32),
            pltpu.VMEM((6, XS, 8, 128), jnp.float32),
            pltpu.SemaphoreType.DMA((9,)),
        ],
        compiler_params=pltpu.CompilerParams(vmem_limit_bytes=8 * MIB),
        name="steps",
    )(ext, forward_state[0], y_low, y_high, surface)

    parts = lax.all_to_all(kernels.reshape(3 * B, 8, 128), "ev", split_axis=0, concat_axis=0, tiled=True)
    shared = pl.pallas_call(
        functools.partial(sum_kernel, n_ev), out_shape=f32(3 * B, 8, 128), in_specs=[VMEM], out_specs=VMEM, compiler_params=pltpu.CompilerParams(vmem_limit_bytes=1 * MIB),
        name="event_sum"
    )(parts)
    total = lax.all_to_all(shared, "ev", split_axis=0, concat_axis=0, tiled=True)
    return state[None], total.reshape(3, B, 8, 128)


def solution(mesh):
    return jax.shard_map(
        on_device,
        mesh=mesh,
        in_specs=(
            P("ev", None, "sx", "sy", None),
            P("ev", None, None, "sx", "sy", None),
            P("sx", "sy", None),
            P("sx", "sy", None),
            P("sx", "sy", None),
            P("ev", ("sx", "sy"), None),
            P("ev", ("sx", "sy")),
            P("ev", ("sx", "sy"), None),
            P("ev", ("sx", "sy")),
        ),
        out_specs=(P("ev", None, "sx", "sy", None), P(None, "sx", "sy", None)),
        check_vma=False,
    )
```

```python
import functools

import jax
import jax.numpy as jnp
from jax import lax
from jax.experimental import pallas as pl
from jax.experimental.pallas import tpu as pltpu
from jax.sharding import PartitionSpec as P

DT = 0.35
W = 3
B = 8
XE = B + 2 * W
XS = XE + 2
YR = 16
FIELDS = 12
PLANE = XS * YR
X_HIGH = (2, 3, 3, 3, 3, 3, 3, 3, 3, 3, 2, 2)
X_LOW = (3, 2, 2, 3, 2, 2, 3, 3, 2, 3, 2, 2)
Y_HIGH = (3, 2, 3, 3, 3, 3, 3, 3, 3, 3, 2, 2)
Y_LOW = (2, 3, 2, 2, 3, 2, 3, 2, 3, 3, 2, 2)


def starts(counts):
    return [sum(counts[:f]) for f in range(len(counts) + 1)]


DEAD = -1.0e6
MIB = 1 << 20
VMEM = pl.BlockSpec(memory_space=pltpu.VMEM)
SMEM = pl.BlockSpec(memory_space=pltpu.SMEM)
HBM = pl.BlockSpec(memory_space=pltpu.HBM)


def x_faces_kernel(
    ny,
    adj_hbm,
    rho_hbm,
    lam_hbm,
    mu_hbm,
    count_ref,
    block_hbm,
    cell_hbm,
    trace_hbm,
    low_ref,
    high_ref,
    base_ref,
    block_ref,
    cell_ref,
    trace_ref,
    sems,
):
    params = (rho_hbm, lam_hbm, mu_hbm)
    rows_in = [
        pltpu.make_async_copy(source, target, sems.at[3, i])
        for i, (source, target) in enumerate(((block_hbm, block_ref), (cell_hbm, cell_ref), (trace_hbm, trace_ref)))
    ]
    copies = []
    for side, (out, counts) in enumerate(((low_ref, X_HIGH), (high_ref, X_LOW))):
        for f, (at, count) in enumerate(zip(starts(counts), counts)):
            planes = pl.ds(B - count if side else 0, count)
            source = adj_hbm.at[f, planes] if f < 9 else params[f - 9].at[planes]
            copies.append(pltpu.make_async_copy(source, out.at[pl.ds(at, count)], sems.at[side, f]))
    copies.append(pltpu.make_async_copy(adj_hbm, base_ref.at[pl.ds(0, 9)], sems.at[2, 0]))
    for i, p in enumerate(params):
        copies.append(pltpu.make_async_copy(p, base_ref.at[9 + i], sems.at[2, 1 + i]))
    for copy in rows_in + copies:
        copy.start()
    for copy in rows_in:
        copy.wait()
    rows = cell_ref.shape[1]
    cell = cell_ref[...]
    key = ((cell // B) * ny + block_ref[...] * B + cell % B).astype(jnp.float32)
    live = lax.broadcasted_iota(jnp.int32, (1, rows), 1) < count_ref[0, 0]
    parts = [jnp.where(live, key, DEAD)] + [jnp.where(live, trace_ref[k], 0.0) for k in range(9)]
    parts += [jnp.zeros((1, rows), jnp.float32)] * 6
    pack = jnp.concatenate(
        [jnp.concatenate(parts[:8], axis=0), jnp.concatenate(parts[8:], axis=0), jnp.zeros((8, 128 - 2 * rows), jnp.float32)],
        axis=1,
    )
    low_ref[sum(X_HIGH)] = pack
    high_ref[sum(X_LOW)] = pack
    for copy in copies:
        copy.wait()


def tiles_kernel(ny, own_ref, low_ref, high_ref, tiles_ref):
    row = lax.broadcasted_iota(jnp.int32, (8, 128), 0)
    group = lax.broadcasted_iota(jnp.int32, (8, 128), 1) // 32
    tile = jnp.zeros((8, 128), jnp.float32)
    for s, (ref, shift) in enumerate(((own_ref, W), (low_ref, W - B), (high_ref, W + B))):
        pack = ref[ref.shape[0] - 1]
        head = jnp.where(row == 0, pack + float(shift * ny), pack)
        head = pltpu.roll(head, 32 * s, 1) if s else head
        tail = pltpu.roll(pack, 64, 1)
        tail = pltpu.roll(tail, 2 * s, 0) if s else tail
        tile = jnp.where(group == s, head, tile)
        tile = jnp.where((group == 3) & (row // 2 == s), tail, tile)
    for d in range(tiles_ref.shape[0]):
        tiles_ref[d] = tile


def y_faces_kernel(base_ref, low_ref, high_ref, face_low_ref, face_high_ref):
    x_low, x_high = starts(X_LOW), starts(X_HIGH)
    for side, (out, counts) in enumerate(((face_low_ref, Y_HIGH), (face_high_ref, Y_LOW))):
        for f, (at, count) in enumerate(zip(starts(counts), counts)):
            for r in range(count):
                y = B - count + r if side else r
                row = (at + r) * XE
                below, above = X_LOW[f], X_HIGH[f]
                if below < W:
                    out[pl.ds(row, W - below), :] = jnp.zeros((W - below, 128), jnp.float32)
                out[pl.ds(row + W - below, below), :] = low_ref[pl.ds(x_low[f] * 8 + y, below, stride=8), :]
                out[pl.ds(row + W, B), :] = base_ref[pl.ds(f * 64 + y, B, stride=8), :]
                out[pl.ds(row + W + B, above), :] = high_ref[pl.ds(x_high[f] * 8 + y, above, stride=8), :]
                if above < W:
                    out[pl.ds(row + W + B + above, W - above), :] = jnp.zeros((W - above, 128), jnp.float32)


def surface_kernel(ny, place_ref, tiles_ref, surface_ref):
    group = lax.broadcasted_iota(jnp.int32, (8, 128), 1) // 32
    for s, first, count in ((0, W, B), (1, 0, W), (2, W + B, W)):
        cells = count * YR
        at = lax.broadcasted_iota(jnp.int32, (cells, 128), 0)
        local = at % YR
        local = jnp.where(local < 11, local, local - YR)
        y = place_ref[0] * B + local
        ident = jnp.where((y >= 0) & (y < ny), (first + at // YR) * ny + y, -10000000).astype(jnp.float32)
        hot, packed = [], []
        for source in range(0, tiles_ref.shape[0], 4):
            heads = tails = jnp.zeros((8, 128), jnp.float32)
            for i in range(4):
                tile = tiles_ref[source + i]
                head, tail = (32 * (i - s)) % 128, (32 * (i - 3)) % 128
                heads = jnp.where(group == i, pltpu.roll(tile, head, 1) if head else tile, heads)
                tails = jnp.where(group == i, pltpu.roll(tile, tail, 1) if tail else tile, tails)
            hot.append((ident == heads[0:1]).astype(jnp.float32))
            packed.append(jnp.concatenate([heads, pltpu.roll(tails, 8 - 2 * s, 0) if s else tails], axis=0))
        packed = jnp.concatenate(packed, axis=1)
        packed = jnp.concatenate([packed, jnp.zeros((112, packed.shape[1]), jnp.float32)], axis=0)
        surface_ref[pl.ds(first * YR, cells), :] = lax.dot_general(
            jnp.concatenate(hot, axis=1),
            packed,
            (((1,), (1,)), ((), ())),
            precision=lax.Precision.HIGHEST,
            preferred_element_type=jnp.float32,
        )


def block_kernel(base_ref, low_ref, high_ref, ext):
    zero8 = jnp.zeros((8, 128), jnp.float32)
    x_low, x_high = starts(X_LOW), starts(X_HIGH)
    for f in range(FIELDS):
        for e in range(XS):
            x = e - 1 - W
            if 0 <= x < B:
                plane = base_ref[f, x]
            elif -X_LOW[f] <= x < 0:
                plane = low_ref[x_low[f] + X_LOW[f] + x]
            elif B <= x < B + X_HIGH[f]:
                plane = high_ref[x_high[f] + x - B]
            else:
                plane = zero8
            ext[pl.ds(f * PLANE + e * YR, 8), :] = plane
            ext[pl.ds(f * PLANE + e * YR + 8, 8), :] = zero8


def steps_kernel(
    steps,
    _,
    forward_hbm,
    y_low_ref,
    y_high_ref,
    force_ref,
    ext,
    state_ref,
    kernels_ref,
    change_ref,
    rate_ref,
    forward_ref,
    sem,
    load_sem,
):
    loads = [pltpu.make_async_copy(forward_hbm.at[t], forward_ref.at[t], load_sem.at[t]) for t in range(steps)]
    for load in loads:
        load.start()
    for ref, counts, first in ((y_high_ref, Y_HIGH, 8), (y_low_ref, Y_LOW, YR)):
        for f, (at, count) in enumerate(zip(starts(counts), counts)):
            for r in range(count):
                row = f * PLANE + YR + (first + r if first == 8 else first - count + r)
                ext[pl.ds(row, XE, stride=YR), :] = ref[pl.ds((at + r) * XE, XE), :]

    lanes = lax.broadcasted_iota(jnp.int32, (YR, 128), 1)

    def y_up(v):
        return pltpu.roll(v, YR - 1, 0)

    def y_down(v):
        return pltpu.roll(v, 1, 0)

    def z_up(v):
        return jnp.where(lanes == 127, 0.0, pltpu.roll(v, 127, 1))

    def z_down(v):
        return jnp.where(lanes == 0, 0.0, pltpu.roll(v, 1, 1))

    def get(f, e):
        return ext[pl.ds(pl.multiple_of(f * PLANE + e * YR, YR), YR), :]

    def put(f, e, v):
        ext[pl.ds(pl.multiple_of(f * PLANE + e * YR, YR), YR), :] = v

    for step in range(steps):

        def velocity(e):
            sxx, syy, szz, sxy, sxz, syz = [get(3 + f, e) for f in range(6)]
            ax = (get(3, e + 1) - sxx) + (sxy - y_down(sxy)) + (sxz - z_down(sxz))
            ay = (sxy - get(6, e - 1)) + (y_up(syy) - syy) + (syz - z_down(syz))
            az = (sxz - get(7, e - 1)) + (syz - y_down(syz)) + (z_up(szz) - szz)
            scale = DT * get(9, e)
            surface = force_ref[pl.ds(pl.multiple_of((e - 1) * YR, YR), YR), :]
            for c, accel in enumerate((ax, ay, az)):
                force = jnp.where(lanes == 0, pltpu.roll(surface, 127 - 3 * step - c, 1), 0.0)
                change = scale * (accel + force)
                put(c, e, get(c, e) + change)
                change_ref[c, e] = change[0:8]

        def stress(e):
            vx, vy, vz = [get(f, e) for f in range(3)]
            exx = vx - get(0, e - 1)
            eyy = vy - y_down(vy)
            ezz = vz - z_down(vz)
            exy = 0.5 * ((y_up(vx) - vx) + (get(1, e + 1) - vy))
            exz = 0.5 * ((z_up(vx) - vx) + (get(2, e + 1) - vz))
            eyz = 0.5 * ((z_up(vy) - vy) + (y_up(vz) - vz))
            trace = exx + eyy + ezz
            lam = get(10, e) * trace
            twice = 2.0 * get(11, e)
            for f, rate in enumerate((exx, eyy, ezz, exy, exz, eyz)):
                if f < 3:
                    put(3 + f, e, get(3 + f, e) + DT * (lam + twice * rate))
                else:
                    put(3 + f, e, get(3 + f, e) + DT * twice * rate)
                rate_ref[f, e] = rate[0:8]

        def pair(body, first):
            def run(i, carry):
                e = first + 2 * i
                body(e)
                body(e + 1)
                return carry

            return run

        lax.fori_loop(0, (XE - 2 * step) // 2, pair(velocity, 1 + step), 0)
        lax.fori_loop(0, (XE - 2 * step - 2) // 2, pair(stress, 2 + step), 0)
        if step == steps - 1:
            copies = [
                pltpu.make_async_copy(
                    ext.reshape(FIELDS, XS, YR, 128).at[f, pl.ds(1 + W, B), pl.ds(0, B)], state_ref.at[f], sem.at[f]
                )
                for f in range(9)
            ]
            for copy in copies:
                copy.start()

        loads[step].wait()

        def sensitivities(x, carry):
            e = x + 1 + W
            f = [forward_ref[step, c, x].astype(jnp.float32) for c in range(9)]
            change = [change_ref[c, e] for c in range(3)]
            rate = [rate_ref[c, e] for c in range(6)]
            trace = rate[0] + rate[1] + rate[2]
            terms = (
                f[0] * change[0] + f[1] * change[1] + f[2] * change[2],
                DT * (f[3] + f[4] + f[5]) * trace,
                DT
                * 2.0
                * (
                    (f[3] * rate[0] + f[4] * rate[1] + f[5] * rate[2])
                    + 2.0 * (f[6] * rate[3] + f[7] * rate[4] + f[8] * rate[5])
                ),
            )
            for k, term in enumerate(terms):
                kernels_ref[k, x] = kernels_ref[k, x] + term if step else term
            return carry

        lax.fori_loop(0, B, sensitivities, 0, unroll=4)

    for copy in copies:
        copy.wait()


def sum_kernel(events, parts_ref, out_ref):
    size = parts_ref.shape[0] // events
    total = parts_ref[0:size]
    for s in range(1, events):
        total = total + parts_ref[size * s : size * s + size]
    for s in range(events):
        out_ref[size * s : size * s + size] = total


def f32(*shape):
    return jax.ShapeDtypeStruct(shape, jnp.float32)


def in_hbm(a):
    return pltpu.with_memory_space_constraint(a, pltpu.HBM)


def on_device(
    adjoint_state,
    forward_state,
    inv_density,
    lame_lambda,
    shear_modulus,
    station_block,
    station_cell,
    station_trace,
    source_count,
):
    n_sx, n_sy, n_ev = lax.axis_size("sx"), lax.axis_size("sy"), lax.axis_size("ev")
    steps = forward_state.shape[1]
    ny = n_sy * B
    adj = adjoint_state[0]
    up_x = [(i, i + 1) for i in range(n_sx - 1)]
    up_y = [(i, i + 1) for i in range(n_sy - 1)]
    down_x = [(b, a) for a, b in up_x]
    down_y = [(b, a) for a, b in up_y]

    rows = station_cell.shape[1]
    low_face, high_face, base = pl.pallas_call(
        functools.partial(x_faces_kernel, ny),
        out_shape=[f32(sum(X_HIGH) + 1, 8, 128), f32(sum(X_LOW) + 1, 8, 128), f32(FIELDS, B, 8, 128)],
        in_specs=[HBM] * 4 + [SMEM] + [HBM] * 3,
        out_specs=[VMEM] * 3,
        scratch_shapes=[
            pltpu.VMEM((1, rows), jnp.int32),
            pltpu.VMEM((1, rows), jnp.int32),
            pltpu.VMEM((9, 1, rows), jnp.float32),
            pltpu.SemaphoreType.DMA((4, FIELDS)),
        ],
        compiler_params=pltpu.CompilerParams(vmem_limit_bytes=3 * MIB),
        name="x_faces",
    )(
        in_hbm(adj),
        in_hbm(inv_density),
        in_hbm(lame_lambda),
        in_hbm(shear_modulus),
        source_count,
        in_hbm(station_block[:, :, 0]),
        in_hbm(station_cell),
        in_hbm(jnp.transpose(station_trace, (2, 0, 1))),
    )
    low = lax.ppermute(high_face, "sx", up_x)
    high = lax.ppermute(low_face, "sx", down_x)

    tiles = pl.pallas_call(
        functools.partial(tiles_kernel, ny),
        out_shape=f32(n_sy, 8, 128),
        in_specs=[VMEM] * 3,
        out_specs=VMEM,
        compiler_params=pltpu.CompilerParams(vmem_limit_bytes=2 * MIB),
        name="tiles",
    )(low_face, low, high)
    tiles = lax.all_to_all(tiles, "sy", split_axis=0, concat_axis=0, tiled=True)

    flat = lambda a: a.reshape(-1, 128)
    y_low_face, y_high_face = pl.pallas_call(
        y_faces_kernel,
        out_shape=[f32(-(-XE * sum(c) // 8) * 8, 128) for c in (Y_HIGH, Y_LOW)],
        in_specs=[VMEM] * 3,
        out_specs=[VMEM] * 2,
        compiler_params=pltpu.CompilerParams(vmem_limit_bytes=4 * MIB),
        name="y_faces",
    )(flat(base), flat(low), flat(high))
    y_low = lax.ppermute(y_high_face, "sy", up_y)
    y_high = lax.ppermute(y_low_face, "sy", down_y)

    place = lax.axis_index("sy").astype(jnp.int32).reshape(1)
    surface = pl.pallas_call(
        functools.partial(surface_kernel, ny),
        out_shape=f32(XE * YR, 128),
        in_specs=[SMEM, VMEM],
        out_specs=VMEM,
        compiler_params=pltpu.CompilerParams(vmem_limit_bytes=4 * MIB),
        name="surface",
    )(place, tiles)

    ext = pl.pallas_call(
        block_kernel,
        out_shape=f32(FIELDS * PLANE, 128),
        in_specs=[VMEM] * 3,
        out_specs=VMEM,
        compiler_params=pltpu.CompilerParams(vmem_limit_bytes=4 * MIB),
        name="block",
    )(base, low, high)

    _, state, kernels = pl.pallas_call(
        functools.partial(steps_kernel, steps),
        out_shape=[f32(FIELDS * PLANE, 128), f32(9, B, 8, 128), f32(3, B, 8, 128)],
        in_specs=[VMEM, HBM, VMEM, VMEM, VMEM],
        out_specs=[VMEM, HBM, VMEM],
        input_output_aliases={0: 0},
        scratch_shapes=[
            pltpu.VMEM((3, XS, 8, 128), jnp.float32),
            pltpu.VMEM((6, XS, 8, 128), jnp.float32),
            pltpu.VMEM(forward_state.shape[1:], forward_state.dtype),
            pltpu.SemaphoreType.DMA((9,)),
            pltpu.SemaphoreType.DMA((steps,)),
        ],
        compiler_params=pltpu.CompilerParams(vmem_limit_bytes=8 * MIB),
        name="steps",
    )(ext, in_hbm(forward_state[0]), y_low, y_high, surface)

    parts = lax.all_to_all(kernels.reshape(3 * B, 8, 128), "ev", split_axis=0, concat_axis=0, tiled=True)
    shared = pl.pallas_call(
        functools.partial(sum_kernel, n_ev), out_shape=f32(3 * B, 8, 128), in_specs=[VMEM], out_specs=VMEM, compiler_params=pltpu.CompilerParams(vmem_limit_bytes=1 * MIB),
        name="event_sum"
    )(parts)
    total = lax.all_to_all(shared, "ev", split_axis=0, concat_axis=0, tiled=True)
    return state[None], total.reshape(3, B, 8, 128)


def solution(mesh):
    return jax.shard_map(
        on_device,
        mesh=mesh,
        in_specs=(
            P("ev", None, "sx", "sy", None),
            P("ev", None, None, "sx", "sy", None),
            P("sx", "sy", None),
            P("sx", "sy", None),
            P("sx", "sy", None),
            P("ev", ("sx", "sy"), None),
            P("ev", ("sx", "sy")),
            P("ev", ("sx", "sy"), None),
            P("ev", ("sx", "sy")),
        ),
        out_specs=(P("ev", None, "sx", "sy", None), P(None, "sx", "sy", None)),
        check_vma=False,
    )
```

```python
import functools

import jax
import jax.numpy as jnp
from jax import lax
from jax.experimental import pallas as pl
from jax.experimental.pallas import tpu as pltpu
from jax.sharding import PartitionSpec as P

DT = 0.35
W = 3
B = 8
XE = B + 2 * W
XS = XE + 2
YR = 16
FIELDS = 12
PLANE = XS * YR
X_HIGH = (2, 3, 3, 3, 3, 3, 3, 3, 3, 3, 2, 2)
X_LOW = (3, 2, 2, 3, 2, 2, 3, 3, 2, 3, 2, 2)
Y_HIGH = (3, 2, 3, 3, 3, 3, 3, 3, 3, 3, 2, 2)
Y_LOW = (2, 3, 2, 2, 3, 2, 3, 2, 3, 3, 2, 2)


PLANES = max(sum(X_HIGH), sum(X_LOW)) + 1


def starts(counts):
    return [sum(counts[:f]) for f in range(len(counts) + 1)]


DEAD = -1.0e6
MIB = 1 << 20
VMEM = pl.BlockSpec(memory_space=pltpu.VMEM)
SMEM = pl.BlockSpec(memory_space=pltpu.SMEM)
HBM = pl.BlockSpec(memory_space=pltpu.HBM)


def x_faces_kernel(
    ny,
    odd_ref,
    adj_hbm,
    rho_hbm,
    lam_hbm,
    mu_hbm,
    count_ref,
    block_hbm,
    cell_hbm,
    trace_hbm,
    first_ref,
    second_ref,
    base_ref,
    block_ref,
    cell_ref,
    trace_ref,
    sems,
):
    params = (rho_hbm, lam_hbm, mu_hbm)
    rows_in = [
        pltpu.make_async_copy(source, target, sems.at[3, i])
        for i, (source, target) in enumerate(((block_hbm, block_ref), (cell_hbm, cell_ref), (trace_hbm, trace_ref)))
    ]

    def faces(low_ref, high_ref):
        copies = []
        for side, (out, counts) in enumerate(((low_ref, X_HIGH), (high_ref, X_LOW))):
            for f, (at, count) in enumerate(zip(starts(counts), counts)):
                planes = pl.ds(B - count if side else 0, count)
                source = adj_hbm.at[f, planes] if f < 9 else params[f - 9].at[planes]
                copies.append(pltpu.make_async_copy(source, out.at[pl.ds(at, count)], sems.at[side, f]))
        return copies

    own = [pltpu.make_async_copy(adj_hbm, base_ref.at[pl.ds(0, 9)], sems.at[2, 0])]
    for i, p in enumerate(params):
        own.append(pltpu.make_async_copy(p, base_ref.at[9 + i], sems.at[2, 1 + i]))
    for copy in rows_in:
        copy.start()

    @pl.when(odd_ref[0] == 0)
    def _():
        for copy in faces(second_ref, first_ref):
            copy.start()

    @pl.when(odd_ref[0] == 1)
    def _():
        for copy in faces(first_ref, second_ref):
            copy.start()

    for copy in own:
        copy.start()
    for copy in rows_in:
        copy.wait()
    rows = cell_ref.shape[1]
    cell = cell_ref[...]
    key = ((cell // B) * ny + block_ref[...] * B + cell % B).astype(jnp.float32)
    live = lax.broadcasted_iota(jnp.int32, (1, rows), 1) < count_ref[0, 0]
    parts = [jnp.where(live, key, DEAD)] + [jnp.where(live, trace_ref[k], 0.0) for k in range(9)]
    parts += [jnp.zeros((1, rows), jnp.float32)] * 6
    pack = jnp.concatenate(
        [jnp.concatenate(parts[:8], axis=0), jnp.concatenate(parts[8:], axis=0), jnp.zeros((8, 128 - 2 * rows), jnp.float32)],
        axis=1,
    )
    first_ref[PLANES - 1] = pack
    second_ref[PLANES - 1] = pack

    @pl.when(odd_ref[0] == 0)
    def _():
        for copy in faces(second_ref, first_ref):
            copy.wait()

    @pl.when(odd_ref[0] == 1)
    def _():
        for copy in faces(first_ref, second_ref):
            copy.wait()

    for copy in own:
        copy.wait()


def by_side(odd_ref, first_ref, second_ref, body):
    @pl.when(odd_ref[0] == 0)
    def _():
        body(second_ref, first_ref)

    @pl.when(odd_ref[0] == 1)
    def _():
        body(first_ref, second_ref)


def tiles_kernel(ny, odd_ref, own_ref, first_ref, second_ref, tiles_ref):
    row = lax.broadcasted_iota(jnp.int32, (8, 128), 0)
    group = lax.broadcasted_iota(jnp.int32, (8, 128), 1) // 32
    tile = jnp.zeros((8, 128), jnp.float32)
    even = odd_ref[0] == 0
    one, two = first_ref[PLANES - 1], second_ref[PLANES - 1]
    packs = (own_ref[PLANES - 1], jnp.where(even, two, one), jnp.where(even, one, two))
    for s, (pack, shift) in enumerate(zip(packs, (W, W - B, W + B))):
        head = jnp.where(row == 0, pack + float(shift * ny), pack)
        head = pltpu.roll(head, 32 * s, 1) if s else head
        tail = pltpu.roll(pack, 64, 1)
        tail = pltpu.roll(tail, 2 * s, 0) if s else tail
        tile = jnp.where(group == s, head, tile)
        tile = jnp.where((group == 3) & (row // 2 == s), tail, tile)
    for d in range(tiles_ref.shape[0]):
        tiles_ref[d] = tile


def y_faces_kernel(odd_ref, base_ref, first_ref, second_ref, face_low_ref, face_high_ref):
    by_side(odd_ref, first_ref, second_ref, functools.partial(y_faces, base_ref, face_low_ref, face_high_ref))


def y_faces(base_ref, face_low_ref, face_high_ref, low_ref, high_ref):
    x_low, x_high = starts(X_LOW), starts(X_HIGH)
    for side, (out, counts) in enumerate(((face_low_ref, Y_HIGH), (face_high_ref, Y_LOW))):
        for f, (at, count) in enumerate(zip(starts(counts), counts)):
            for r in range(count):
                y = B - count + r if side else r
                row = (at + r) * XE
                below, above = X_LOW[f], X_HIGH[f]
                if below < W:
                    out[pl.ds(row, W - below), :] = jnp.zeros((W - below, 128), jnp.float32)
                out[pl.ds(row + W - below, below), :] = low_ref[pl.ds(x_low[f] * 8 + y, below, stride=8), :]
                out[pl.ds(row + W, B), :] = base_ref[pl.ds(f * 64 + y, B, stride=8), :]
                out[pl.ds(row + W + B, above), :] = high_ref[pl.ds(x_high[f] * 8 + y, above, stride=8), :]
                if above < W:
                    out[pl.ds(row + W + B + above, W - above), :] = jnp.zeros((W - above, 128), jnp.float32)


def surface_kernel(ny, place_ref, tiles_ref, surface_ref):
    group = lax.broadcasted_iota(jnp.int32, (8, 128), 1) // 32
    for s, first, count in ((0, W, B), (1, 0, W), (2, W + B, W)):
        cells = count * YR
        at = lax.broadcasted_iota(jnp.int32, (cells, 128), 0)
        local = at % YR
        local = jnp.where(local < 11, local, local - YR)
        y = place_ref[0] * B + local
        ident = jnp.where((y >= 0) & (y < ny), (first + at // YR) * ny + y, -10000000).astype(jnp.float32)
        hot, packed = [], []
        for source in range(0, tiles_ref.shape[0], 4):
            heads = tails = jnp.zeros((8, 128), jnp.float32)
            for i in range(4):
                tile = tiles_ref[source + i]
                head, tail = (32 * (i - s)) % 128, (32 * (i - 3)) % 128
                heads = jnp.where(group == i, pltpu.roll(tile, head, 1) if head else tile, heads)
                tails = jnp.where(group == i, pltpu.roll(tile, tail, 1) if tail else tile, tails)
            hot.append((ident == heads[0:1]).astype(jnp.float32))
            packed.append(jnp.concatenate([heads, pltpu.roll(tails, 8 - 2 * s, 0) if s else tails], axis=0))
        packed = jnp.concatenate(packed, axis=1)
        packed = jnp.concatenate([packed, jnp.zeros((112, packed.shape[1]), jnp.float32)], axis=0)
        surface_ref[pl.ds(first * YR, cells), :] = lax.dot_general(
            jnp.concatenate(hot, axis=1),
            packed,
            (((1,), (1,)), ((), ())),
            precision=lax.Precision.HIGHEST,
            preferred_element_type=jnp.float32,
        )


def block_kernel(odd_ref, base_ref, first_ref, second_ref, ext):
    by_side(odd_ref, first_ref, second_ref, functools.partial(extend, base_ref, ext))


def extend(base_ref, ext, low_ref, high_ref):
    zero8 = jnp.zeros((8, 128), jnp.float32)
    x_low, x_high = starts(X_LOW), starts(X_HIGH)
    for f in range(FIELDS):
        for e in range(XS):
            x = e - 1 - W
            if 0 <= x < B:
                plane = base_ref[f, x]
            elif -X_LOW[f] <= x < 0:
                plane = low_ref[x_low[f] + X_LOW[f] + x]
            elif B <= x < B + X_HIGH[f]:
                plane = high_ref[x_high[f] + x - B]
            else:
                plane = zero8
            ext[pl.ds(f * PLANE + e * YR, 8), :] = plane
            ext[pl.ds(f * PLANE + e * YR + 8, 8), :] = zero8


def steps_kernel(
    steps,
    _,
    forward_hbm,
    y_low_ref,
    y_high_ref,
    force_ref,
    ext,
    state_ref,
    kernels_ref,
    change_ref,
    rate_ref,
    forward_ref,
    sem,
    load_sem,
):
    loads = [pltpu.make_async_copy(forward_hbm.at[t], forward_ref.at[t], load_sem.at[t]) for t in range(steps)]
    for load in loads:
        load.start()
    for ref, counts, first in ((y_high_ref, Y_HIGH, 8), (y_low_ref, Y_LOW, YR)):
        for f, (at, count) in enumerate(zip(starts(counts), counts)):
            for r in range(count):
                row = f * PLANE + YR + (first + r if first == 8 else first - count + r)
                ext[pl.ds(row, XE, stride=YR), :] = ref[pl.ds((at + r) * XE, XE), :]

    lanes = lax.broadcasted_iota(jnp.int32, (YR, 128), 1)

    def y_up(v):
        return pltpu.roll(v, YR - 1, 0)

    def y_down(v):
        return pltpu.roll(v, 1, 0)

    def z_up(v):
        return jnp.where(lanes == 127, 0.0, pltpu.roll(v, 127, 1))

    def z_down(v):
        return jnp.where(lanes == 0, 0.0, pltpu.roll(v, 1, 1))

    def get(f, e):
        return ext[pl.ds(pl.multiple_of(f * PLANE + e * YR, YR), YR), :]

    def put(f, e, v):
        ext[pl.ds(pl.multiple_of(f * PLANE + e * YR, YR), YR), :] = v

    for step in range(steps):

        def velocity(e):
            sxx, syy, szz, sxy, sxz, syz = [get(3 + f, e) for f in range(6)]
            ax = (get(3, e + 1) - sxx) + (sxy - y_down(sxy)) + (sxz - z_down(sxz))
            ay = (sxy - get(6, e - 1)) + (y_up(syy) - syy) + (syz - z_down(syz))
            az = (sxz - get(7, e - 1)) + (syz - y_down(syz)) + (z_up(szz) - szz)
            scale = DT * get(9, e)
            surface = force_ref[pl.ds(pl.multiple_of((e - 1) * YR, YR), YR), :]
            for c, accel in enumerate((ax, ay, az)):
                force = jnp.where(lanes == 0, pltpu.roll(surface, 127 - 3 * step - c, 1), 0.0)
                change = scale * (accel + force)
                put(c, e, get(c, e) + change)
                change_ref[c, e] = change[0:8]

        def stress(e):
            vx, vy, vz = [get(f, e) for f in range(3)]
            exx = vx - get(0, e - 1)
            eyy = vy - y_down(vy)
            ezz = vz - z_down(vz)
            exy = 0.5 * ((y_up(vx) - vx) + (get(1, e + 1) - vy))
            exz = 0.5 * ((z_up(vx) - vx) + (get(2, e + 1) - vz))
            eyz = 0.5 * ((z_up(vy) - vy) + (y_up(vz) - vz))
            trace = exx + eyy + ezz
            lam = get(10, e) * trace
            twice = 2.0 * get(11, e)
            for f, rate in enumerate((exx, eyy, ezz, exy, exz, eyz)):
                if f < 3:
                    put(3 + f, e, get(3 + f, e) + DT * (lam + twice * rate))
                else:
                    put(3 + f, e, get(3 + f, e) + DT * twice * rate)
                rate_ref[f, e] = rate[0:8]

        def pair(body, first):
            def run(i, carry):
                e = first + 2 * i
                body(e)
                body(e + 1)
                return carry

            return run

        lax.fori_loop(0, (XE - 2 * step) // 2, pair(velocity, 1 + step), 0)
        lax.fori_loop(0, (XE - 2 * step - 2) // 2, pair(stress, 2 + step), 0)
        if step == steps - 1:
            copies = [
                pltpu.make_async_copy(
                    ext.reshape(FIELDS, XS, YR, 128).at[f, pl.ds(1 + W, B), pl.ds(0, B)], state_ref.at[f], sem.at[f]
                )
                for f in range(9)
            ]
            for copy in copies:
                copy.start()

        loads[step].wait()

        def sensitivities(x, carry):
            e = x + 1 + W
            f = [forward_ref[step, c, x].astype(jnp.float32) for c in range(9)]
            change = [change_ref[c, e] for c in range(3)]
            rate = [rate_ref[c, e] for c in range(6)]
            trace = rate[0] + rate[1] + rate[2]
            terms = (
                f[0] * change[0] + f[1] * change[1] + f[2] * change[2],
                DT * (f[3] + f[4] + f[5]) * trace,
                DT
                * 2.0
                * (
                    (f[3] * rate[0] + f[4] * rate[1] + f[5] * rate[2])
                    + 2.0 * (f[6] * rate[3] + f[7] * rate[4] + f[8] * rate[5])
                ),
            )
            for k, term in enumerate(terms):
                kernels_ref[k, x] = kernels_ref[k, x] + term if step else term
            return carry

        lax.fori_loop(0, B, sensitivities, 0, unroll=4)

    for copy in copies:
        copy.wait()


def sum_kernel(events, parts_ref, out_ref):
    size = parts_ref.shape[0] // events
    total = parts_ref[0:size]
    for s in range(1, events):
        total = total + parts_ref[size * s : size * s + size]
    for s in range(events):
        out_ref[size * s : size * s + size] = total


def f32(*shape):
    return jax.ShapeDtypeStruct(shape, jnp.float32)


def swaps(start, count):
    pairs = [(i, i + 1) for i in range(start, count - 1, 2)]
    return pairs + [(b, a) for a, b in pairs]


def in_hbm(a):
    return pltpu.with_memory_space_constraint(a, pltpu.HBM)


def on_device(
    adjoint_state,
    forward_state,
    inv_density,
    lame_lambda,
    shear_modulus,
    station_block,
    station_cell,
    station_trace,
    source_count,
):
    n_sx, n_sy, n_ev = lax.axis_size("sx"), lax.axis_size("sy"), lax.axis_size("ev")
    steps = forward_state.shape[1]
    ny = n_sy * B
    adj = adjoint_state[0]
    up_y = [(i, i + 1) for i in range(n_sy - 1)]
    down_y = [(b, a) for a, b in up_y]

    rows = station_cell.shape[1]
    odd = (lax.axis_index("sx") & 1).astype(jnp.int32).reshape(1)
    first_face, second_face, base = pl.pallas_call(
        functools.partial(x_faces_kernel, ny),
        out_shape=[f32(PLANES, 8, 128)] * 2 + [f32(FIELDS, B, 8, 128)],
        in_specs=[SMEM] + [HBM] * 4 + [SMEM] + [HBM] * 3,
        out_specs=[VMEM] * 3,
        scratch_shapes=[
            pltpu.VMEM((1, rows), jnp.int32),
            pltpu.VMEM((1, rows), jnp.int32),
            pltpu.VMEM((9, 1, rows), jnp.float32),
            pltpu.SemaphoreType.DMA((4, FIELDS)),
        ],
        compiler_params=pltpu.CompilerParams(vmem_limit_bytes=3 * MIB),
        name="x_faces",
    )(
        odd,
        in_hbm(adj),
        in_hbm(inv_density),
        in_hbm(lame_lambda),
        in_hbm(shear_modulus),
        source_count,
        in_hbm(station_block[:, :, 0]),
        in_hbm(station_cell),
        in_hbm(jnp.transpose(station_trace, (2, 0, 1))),
    )
    first = lax.ppermute(first_face, "sx", swaps(0, n_sx))
    second = lax.ppermute(second_face, "sx", swaps(1, n_sx))

    tiles = pl.pallas_call(
        functools.partial(tiles_kernel, ny),
        out_shape=f32(n_sy, 8, 128),
        in_specs=[SMEM] + [VMEM] * 3,
        out_specs=VMEM,
        compiler_params=pltpu.CompilerParams(vmem_limit_bytes=2 * MIB),
        name="tiles",
    )(odd, first_face, first, second)
    tiles = lax.all_to_all(tiles, "sy", split_axis=0, concat_axis=0, tiled=True)

    flat = lambda a: a.reshape(-1, 128)
    y_low_face, y_high_face = pl.pallas_call(
        y_faces_kernel,
        out_shape=[f32(-(-XE * sum(c) // 8) * 8, 128) for c in (Y_HIGH, Y_LOW)],
        in_specs=[SMEM] + [VMEM] * 3,
        out_specs=[VMEM] * 2,
        compiler_params=pltpu.CompilerParams(vmem_limit_bytes=4 * MIB),
        name="y_faces",
    )(odd, flat(base), flat(first), flat(second))
    y_low = lax.ppermute(y_high_face, "sy", up_y)
    y_high = lax.ppermute(y_low_face, "sy", down_y)

    place = lax.axis_index("sy").astype(jnp.int32).reshape(1)
    surface = pl.pallas_call(
        functools.partial(surface_kernel, ny),
        out_shape=f32(XE * YR, 128),
        in_specs=[SMEM, VMEM],
        out_specs=VMEM,
        compiler_params=pltpu.CompilerParams(vmem_limit_bytes=4 * MIB),
        name="surface",
    )(place, tiles)

    ext = pl.pallas_call(
        block_kernel,
        out_shape=f32(FIELDS * PLANE, 128),
        in_specs=[SMEM] + [VMEM] * 3,
        out_specs=VMEM,
        compiler_params=pltpu.CompilerParams(vmem_limit_bytes=4 * MIB),
        name="block",
    )(odd, base, first, second)

    _, state, kernels = pl.pallas_call(
        functools.partial(steps_kernel, steps),
        out_shape=[f32(FIELDS * PLANE, 128), f32(9, B, 8, 128), f32(3, B, 8, 128)],
        in_specs=[VMEM, HBM, VMEM, VMEM, VMEM],
        out_specs=[VMEM, HBM, VMEM],
        input_output_aliases={0: 0},
        scratch_shapes=[
            pltpu.VMEM((3, XS, 8, 128), jnp.float32),
            pltpu.VMEM((6, XS, 8, 128), jnp.float32),
            pltpu.VMEM(forward_state.shape[1:], forward_state.dtype),
            pltpu.SemaphoreType.DMA((9,)),
            pltpu.SemaphoreType.DMA((steps,)),
        ],
        compiler_params=pltpu.CompilerParams(vmem_limit_bytes=8 * MIB),
        name="steps",
    )(ext, in_hbm(forward_state[0]), y_low, y_high, surface)

    parts = lax.all_to_all(kernels.reshape(3 * B, 8, 128), "ev", split_axis=0, concat_axis=0, tiled=True)
    shared = pl.pallas_call(
        functools.partial(sum_kernel, n_ev), out_shape=f32(3 * B, 8, 128), in_specs=[VMEM], out_specs=VMEM, compiler_params=pltpu.CompilerParams(vmem_limit_bytes=1 * MIB),
        name="event_sum"
    )(parts)
    total = lax.all_to_all(shared, "ev", split_axis=0, concat_axis=0, tiled=True)
    return state[None], total.reshape(3, B, 8, 128)


def solution(mesh):
    return jax.shard_map(
        on_device,
        mesh=mesh,
        in_specs=(
            P("ev", None, "sx", "sy", None),
            P("ev", None, None, "sx", "sy", None),
            P("sx", "sy", None),
            P("sx", "sy", None),
            P("sx", "sy", None),
            P("ev", ("sx", "sy"), None),
            P("ev", ("sx", "sy")),
            P("ev", ("sx", "sy"), None),
            P("ev", ("sx", "sy")),
        ),
        out_specs=(P("ev", None, "sx", "sy", None), P(None, "sx", "sy", None)),
        check_vma=False,
    )
```

```python
import functools

import jax
import jax.numpy as jnp
from jax import lax
from jax.experimental import pallas as pl
from jax.experimental.pallas import tpu as pltpu
from jax.sharding import PartitionSpec as P

DT = 0.35
W = 3
B = 8
XE = B + 2 * W
XS = XE + 2
YR = 16
FIELDS = 12
PLANE = XS * YR
X_HIGH = (2, 3, 3, 3, 3, 3, 3, 3, 3, 3, 2, 2)
X_LOW = (3, 2, 2, 3, 2, 2, 3, 3, 2, 3, 2, 2)
Y_HIGH = (3, 2, 3, 3, 3, 3, 3, 3, 3, 3, 2, 2)
Y_LOW = (2, 3, 2, 2, 3, 2, 3, 2, 3, 3, 2, 2)


PLANES = max(sum(X_HIGH), sum(X_LOW))


def starts(counts):
    return [sum(counts[:f]) for f in range(len(counts) + 1)]


DEAD = -1.0e6
MIB = 1 << 20
VMEM = pl.BlockSpec(memory_space=pltpu.VMEM)
SMEM = pl.BlockSpec(memory_space=pltpu.SMEM)
HBM = pl.BlockSpec(memory_space=pltpu.HBM)


def x_faces_kernel(
    ny,
    odd_ref,
    adj_hbm,
    rho_hbm,
    lam_hbm,
    mu_hbm,
    count_ref,
    block_hbm,
    cell_hbm,
    trace_hbm,
    first_ref,
    second_ref,
    base_ref,
    tiles_ref,
    block_ref,
    cell_ref,
    trace_ref,
    sems,
):
    params = (rho_hbm, lam_hbm, mu_hbm)
    rows_in = [
        pltpu.make_async_copy(source, target, sems.at[3, i])
        for i, (source, target) in enumerate(((block_hbm, block_ref), (cell_hbm, cell_ref), (trace_hbm, trace_ref)))
    ]

    def faces(low_ref, high_ref):
        copies = []
        for side, (out, counts) in enumerate(((low_ref, X_HIGH), (high_ref, X_LOW))):
            for f, (at, count) in enumerate(zip(starts(counts), counts)):
                planes = pl.ds(B - count if side else 0, count)
                source = adj_hbm.at[f, planes] if f < 9 else params[f - 9].at[planes]
                copies.append(pltpu.make_async_copy(source, out.at[pl.ds(at, count)], sems.at[side, f]))
        return copies

    own = [pltpu.make_async_copy(adj_hbm, base_ref.at[pl.ds(0, 9)], sems.at[2, 0])]
    for i, p in enumerate(params):
        own.append(pltpu.make_async_copy(p, base_ref.at[9 + i], sems.at[2, 1 + i]))
    for copy in rows_in:
        copy.start()

    @pl.when(odd_ref[0] == 0)
    def _():
        for copy in faces(second_ref, first_ref):
            copy.start()

    @pl.when(odd_ref[0] == 1)
    def _():
        for copy in faces(first_ref, second_ref):
            copy.start()

    for copy in own:
        copy.start()
    for copy in rows_in:
        copy.wait()
    rows = cell_ref.shape[1]
    cell = cell_ref[...]
    key = ((cell // B) * ny + block_ref[...] * B + cell % B).astype(jnp.float32)
    live = lax.broadcasted_iota(jnp.int32, (1, rows), 1) < count_ref[0, 0]
    parts = [jnp.where(live, key, DEAD)] + [jnp.where(live, trace_ref[k], 0.0) for k in range(9)]
    parts += [jnp.zeros((1, rows), jnp.float32)] * 6
    pack = jnp.concatenate(
        [jnp.concatenate(parts[:8], axis=0), jnp.concatenate(parts[8:], axis=0), jnp.zeros((8, 128 - 2 * rows), jnp.float32)],
        axis=1,
    )
    for d in range(tiles_ref.shape[0]):
        tiles_ref[d] = pack

    @pl.when(odd_ref[0] == 0)
    def _():
        for copy in faces(second_ref, first_ref):
            copy.wait()

    @pl.when(odd_ref[0] == 1)
    def _():
        for copy in faces(first_ref, second_ref):
            copy.wait()

    for copy in own:
        copy.wait()


def by_side(odd_ref, first_ref, second_ref, body):
    @pl.when(odd_ref[0] == 0)
    def _():
        body(second_ref, first_ref)

    @pl.when(odd_ref[0] == 1)
    def _():
        body(first_ref, second_ref)


def y_faces_kernel(odd_ref, base_ref, first_ref, second_ref, face_low_ref, face_high_ref):
    by_side(odd_ref, first_ref, second_ref, functools.partial(y_faces, base_ref, face_low_ref, face_high_ref))


def y_faces(base_ref, face_low_ref, face_high_ref, low_ref, high_ref):
    x_low, x_high = starts(X_LOW), starts(X_HIGH)
    for side, (out, counts) in enumerate(((face_low_ref, Y_HIGH), (face_high_ref, Y_LOW))):
        for f, (at, count) in enumerate(zip(starts(counts), counts)):
            for r in range(count):
                y = B - count + r if side else r
                row = (at + r) * XE
                below, above = X_LOW[f], X_HIGH[f]
                if below < W:
                    out[pl.ds(row, W - below), :] = jnp.zeros((W - below, 128), jnp.float32)
                out[pl.ds(row + W - below, below), :] = low_ref[pl.ds(x_low[f] * 8 + y, below, stride=8), :]
                out[pl.ds(row + W, B), :] = base_ref[pl.ds(f * 64 + y, B, stride=8), :]
                out[pl.ds(row + W + B, above), :] = high_ref[pl.ds(x_high[f] * 8 + y, above, stride=8), :]
                if above < W:
                    out[pl.ds(row + W + B + above, W - above), :] = jnp.zeros((W - above, 128), jnp.float32)


def surface_kernel(ny, place_ref, odd_ref, tiles_ref, own_ref, first_ref, second_ref):
    cells = B * YR
    at = lax.broadcasted_iota(jnp.int32, (cells, 128), 0)
    local = at % YR
    local = jnp.where(local < 11, local, local - YR)
    y = place_ref[0] * B + local
    ident = jnp.where((y >= 0) & (y < ny), (at // YR) * ny + y, -10000000).astype(jnp.float32)
    group = lax.broadcasted_iota(jnp.int32, (8, 128), 1) // 32
    hot, packed = [], []
    for first in range(0, tiles_ref.shape[0], 4):
        heads = jnp.where(group == 0, tiles_ref[first], 0.0)
        tails = jnp.where(group == 0, pltpu.roll(tiles_ref[first], 96, 1), 0.0)
        for i in range(1, 4):
            tile = tiles_ref[first + i]
            heads = jnp.where(group == i, pltpu.roll(tile, 32 * i, 1), heads)
            tails = jnp.where(group == i, pltpu.roll(tile, (96 + 32 * i) % 128, 1) if i > 1 else tile, tails)
        hot.append((ident == heads[0:1]).astype(jnp.float32))
        packed.append(jnp.concatenate([heads, tails], axis=0))
    packed = jnp.concatenate(packed, axis=1)
    packed = jnp.concatenate([packed, jnp.zeros((112, packed.shape[1]), jnp.float32)], axis=0)
    surface = lax.dot_general(
        jnp.concatenate(hot, axis=1),
        packed,
        (((1,), (1,)), ((), ())),
        precision=lax.Precision.HIGHEST,
        preferred_element_type=jnp.float32,
    )
    own_ref[...] = surface
    low, high = surface[0 : W * YR], surface[(B - W) * YR :]
    even = odd_ref[0] == 0
    first_ref[...] = jnp.where(even, high, low)
    second_ref[...] = jnp.where(even, low, high)


def block_kernel(odd_ref, base_ref, first_ref, second_ref, ext):
    by_side(odd_ref, first_ref, second_ref, functools.partial(extend, base_ref, ext))


def extend(base_ref, ext, low_ref, high_ref):
    zero8 = jnp.zeros((8, 128), jnp.float32)
    x_low, x_high = starts(X_LOW), starts(X_HIGH)
    for f in range(FIELDS):
        for e in range(XS):
            x = e - 1 - W
            if 0 <= x < B:
                plane = base_ref[f, x]
            elif -X_LOW[f] <= x < 0:
                plane = low_ref[x_low[f] + X_LOW[f] + x]
            elif B <= x < B + X_HIGH[f]:
                plane = high_ref[x_high[f] + x - B]
            else:
                plane = zero8
            ext[pl.ds(f * PLANE + e * YR, 8), :] = plane
            ext[pl.ds(f * PLANE + e * YR + 8, 8), :] = zero8


def steps_kernel(
    steps,
    odd_ref,
    _,
    forward_hbm,
    y_low_ref,
    y_high_ref,
    own_ref,
    first_ref,
    second_ref,
    ext,
    state_ref,
    kernels_ref,
    change_ref,
    rate_ref,
    forward_ref,
    force_ref,
    sem,
    load_sem,
):
    loads = [pltpu.make_async_copy(forward_hbm.at[t], forward_ref.at[t], load_sem.at[t]) for t in range(steps)]
    for load in loads:
        load.start()
    for ref, counts, first in ((y_high_ref, Y_HIGH, 8), (y_low_ref, Y_LOW, YR)):
        for f, (at, count) in enumerate(zip(starts(counts), counts)):
            for r in range(count):
                row = f * PLANE + YR + (first + r if first == 8 else first - count + r)
                ext[pl.ds(row, XE, stride=YR), :] = ref[pl.ds((at + r) * XE, XE), :]

    even = odd_ref[0] == 0
    force_ref[pl.ds(0, W * YR), :] = jnp.where(even, second_ref[...], first_ref[...])
    force_ref[pl.ds(W * YR, B * YR), :] = own_ref[...]
    force_ref[pl.ds((W + B) * YR, W * YR), :] = jnp.where(even, first_ref[...], second_ref[...])
    lanes = lax.broadcasted_iota(jnp.int32, (YR, 128), 1)

    def y_up(v):
        return pltpu.roll(v, YR - 1, 0)

    def y_down(v):
        return pltpu.roll(v, 1, 0)

    def z_up(v):
        return jnp.where(lanes == 127, 0.0, pltpu.roll(v, 127, 1))

    def z_down(v):
        return jnp.where(lanes == 0, 0.0, pltpu.roll(v, 1, 1))

    def get(f, e):
        return ext[pl.ds(pl.multiple_of(f * PLANE + e * YR, YR), YR), :]

    def put(f, e, v):
        ext[pl.ds(pl.multiple_of(f * PLANE + e * YR, YR), YR), :] = v

    for step in range(steps):

        def velocity(e):
            sxx, syy, szz, sxy, sxz, syz = [get(3 + f, e) for f in range(6)]
            ax = (get(3, e + 1) - sxx) + (sxy - y_down(sxy)) + (sxz - z_down(sxz))
            ay = (sxy - get(6, e - 1)) + (y_up(syy) - syy) + (syz - z_down(syz))
            az = (sxz - get(7, e - 1)) + (syz - y_down(syz)) + (z_up(szz) - szz)
            scale = DT * get(9, e)
            surface = force_ref[pl.ds(pl.multiple_of((e - 1) * YR, YR), YR), :]
            for c, accel in enumerate((ax, ay, az)):
                force = jnp.where(lanes == 0, pltpu.roll(surface, 127 - 3 * step - c, 1), 0.0)
                change = scale * (accel + force)
                put(c, e, get(c, e) + change)
                change_ref[c, e] = change[0:8]

        def stress(e):
            vx, vy, vz = [get(f, e) for f in range(3)]
            exx = vx - get(0, e - 1)
            eyy = vy - y_down(vy)
            ezz = vz - z_down(vz)
            exy = 0.5 * ((y_up(vx) - vx) + (get(1, e + 1) - vy))
            exz = 0.5 * ((z_up(vx) - vx) + (get(2, e + 1) - vz))
            eyz = 0.5 * ((z_up(vy) - vy) + (y_up(vz) - vz))
            trace = exx + eyy + ezz
            lam = get(10, e) * trace
            twice = 2.0 * get(11, e)
            for f, rate in enumerate((exx, eyy, ezz, exy, exz, eyz)):
                if f < 3:
                    put(3 + f, e, get(3 + f, e) + DT * (lam + twice * rate))
                else:
                    put(3 + f, e, get(3 + f, e) + DT * twice * rate)
                rate_ref[f, e] = rate[0:8]

        def pair(body, first):
            def run(i, carry):
                e = first + 2 * i
                body(e)
                body(e + 1)
                return carry

            return run

        lax.fori_loop(0, (XE - 2 * step) // 2, pair(velocity, 1 + step), 0)
        lax.fori_loop(0, (XE - 2 * step - 2) // 2, pair(stress, 2 + step), 0)
        if step == steps - 1:
            copies = [
                pltpu.make_async_copy(
                    ext.reshape(FIELDS, XS, YR, 128).at[f, pl.ds(1 + W, B), pl.ds(0, B)], state_ref.at[f], sem.at[f]
                )
                for f in range(9)
            ]
            for copy in copies:
                copy.start()

        loads[step].wait()

        def sensitivities(x, carry):
            e = x + 1 + W
            f = [forward_ref[step, c, x].astype(jnp.float32) for c in range(9)]
            change = [change_ref[c, e] for c in range(3)]
            rate = [rate_ref[c, e] for c in range(6)]
            trace = rate[0] + rate[1] + rate[2]
            terms = (
                f[0] * change[0] + f[1] * change[1] + f[2] * change[2],
                DT * (f[3] + f[4] + f[5]) * trace,
                DT
                * 2.0
                * (
                    (f[3] * rate[0] + f[4] * rate[1] + f[5] * rate[2])
                    + 2.0 * (f[6] * rate[3] + f[7] * rate[4] + f[8] * rate[5])
                ),
            )
            for k, term in enumerate(terms):
                kernels_ref[k, x] = kernels_ref[k, x] + term if step else term
            return carry

        lax.fori_loop(0, B, sensitivities, 0, unroll=4)

    for copy in copies:
        copy.wait()


def sum_kernel(events, parts_ref, out_ref):
    size = parts_ref.shape[0] // events
    total = parts_ref[0:size]
    for s in range(1, events):
        total = total + parts_ref[size * s : size * s + size]
    for s in range(events):
        out_ref[size * s : size * s + size] = total


def f32(*shape):
    return jax.ShapeDtypeStruct(shape, jnp.float32)


def swaps(start, count):
    pairs = [(i, i + 1) for i in range(start, count - 1, 2)]
    return pairs + [(b, a) for a, b in pairs]


def in_hbm(a):
    return pltpu.with_memory_space_constraint(a, pltpu.HBM)


def on_device(
    adjoint_state,
    forward_state,
    inv_density,
    lame_lambda,
    shear_modulus,
    station_block,
    station_cell,
    station_trace,
    source_count,
):
    n_sx, n_sy, n_ev = lax.axis_size("sx"), lax.axis_size("sy"), lax.axis_size("ev")
    steps = forward_state.shape[1]
    ny = n_sy * B
    adj = adjoint_state[0]
    up_y = [(i, i + 1) for i in range(n_sy - 1)]
    down_y = [(b, a) for a, b in up_y]

    rows = station_cell.shape[1]
    odd = (lax.axis_index("sx") & 1).astype(jnp.int32).reshape(1)
    first_face, second_face, base, tiles = pl.pallas_call(
        functools.partial(x_faces_kernel, ny),
        out_shape=[f32(PLANES, 8, 128)] * 2 + [f32(FIELDS, B, 8, 128), f32(n_sy, 8, 128)],
        in_specs=[SMEM] + [HBM] * 4 + [SMEM] + [HBM] * 3,
        out_specs=[VMEM] * 4,
        scratch_shapes=[
            pltpu.VMEM((1, rows), jnp.int32),
            pltpu.VMEM((1, rows), jnp.int32),
            pltpu.VMEM((9, 1, rows), jnp.float32),
            pltpu.SemaphoreType.DMA((4, FIELDS)),
        ],
        compiler_params=pltpu.CompilerParams(vmem_limit_bytes=3 * MIB),
        name="x_faces",
    )(
        odd,
        in_hbm(adj),
        in_hbm(inv_density),
        in_hbm(lame_lambda),
        in_hbm(shear_modulus),
        source_count,
        in_hbm(station_block[:, :, 0]),
        in_hbm(station_cell),
        in_hbm(jnp.transpose(station_trace, (2, 0, 1))),
    )
    first = lax.ppermute(first_face, "sx", swaps(0, n_sx))
    second = lax.ppermute(second_face, "sx", swaps(1, n_sx))

    tiles = lax.all_to_all(tiles, "sy", split_axis=0, concat_axis=0, tiled=True)

    flat = lambda a: a.reshape(-1, 128)
    y_low_face, y_high_face = pl.pallas_call(
        y_faces_kernel,
        out_shape=[f32(-(-XE * sum(c) // 8) * 8, 128) for c in (Y_HIGH, Y_LOW)],
        in_specs=[SMEM] + [VMEM] * 3,
        out_specs=[VMEM] * 2,
        compiler_params=pltpu.CompilerParams(vmem_limit_bytes=4 * MIB),
        name="y_faces",
    )(odd, flat(base), flat(first), flat(second))
    y_low = lax.ppermute(y_high_face, "sy", up_y)
    y_high = lax.ppermute(y_low_face, "sy", down_y)

    place = lax.axis_index("sy").astype(jnp.int32).reshape(1)
    surface, first_edge, second_edge = pl.pallas_call(
        functools.partial(surface_kernel, ny),
        out_shape=[f32(B * YR, 128), f32(W * YR, 128), f32(W * YR, 128)],
        in_specs=[SMEM, SMEM, VMEM],
        out_specs=[VMEM] * 3,
        compiler_params=pltpu.CompilerParams(vmem_limit_bytes=4 * MIB),
        name="surface",
    )(place, odd, tiles)
    first_surface = lax.ppermute(first_edge, "sx", swaps(0, n_sx))
    second_surface = lax.ppermute(second_edge, "sx", swaps(1, n_sx))

    ext = pl.pallas_call(
        block_kernel,
        out_shape=f32(FIELDS * PLANE, 128),
        in_specs=[SMEM] + [VMEM] * 3,
        out_specs=VMEM,
        compiler_params=pltpu.CompilerParams(vmem_limit_bytes=4 * MIB),
        name="block",
    )(odd, base, first, second)

    _, state, kernels = pl.pallas_call(
        functools.partial(steps_kernel, steps),
        out_shape=[f32(FIELDS * PLANE, 128), f32(9, B, 8, 128), f32(3, B, 8, 128)],
        in_specs=[SMEM, VMEM, HBM] + [VMEM] * 5,
        out_specs=[VMEM, HBM, VMEM],
        input_output_aliases={1: 0},
        scratch_shapes=[
            pltpu.VMEM((3, XS, 8, 128), jnp.float32),
            pltpu.VMEM((6, XS, 8, 128), jnp.float32),
            pltpu.VMEM(forward_state.shape[1:], forward_state.dtype),
            pltpu.VMEM((XE * YR, 128), jnp.float32),
            pltpu.SemaphoreType.DMA((9,)),
            pltpu.SemaphoreType.DMA((steps,)),
        ],
        compiler_params=pltpu.CompilerParams(vmem_limit_bytes=8 * MIB),
        name="steps",
    )(odd, ext, in_hbm(forward_state[0]), y_low, y_high, surface, first_surface, second_surface)

    parts = lax.all_to_all(kernels.reshape(3 * B, 8, 128), "ev", split_axis=0, concat_axis=0, tiled=True)
    shared = pl.pallas_call(
        functools.partial(sum_kernel, n_ev), out_shape=f32(3 * B, 8, 128), in_specs=[VMEM], out_specs=VMEM, compiler_params=pltpu.CompilerParams(vmem_limit_bytes=1 * MIB),
        name="event_sum"
    )(parts)
    total = lax.all_to_all(shared, "ev", split_axis=0, concat_axis=0, tiled=True)
    return state[None], total.reshape(3, B, 8, 128)


def solution(mesh):
    return jax.shard_map(
        on_device,
        mesh=mesh,
        in_specs=(
            P("ev", None, "sx", "sy", None),
            P("ev", None, None, "sx", "sy", None),
            P("sx", "sy", None),
            P("sx", "sy", None),
            P("sx", "sy", None),
            P("ev", ("sx", "sy"), None),
            P("ev", ("sx", "sy")),
            P("ev", ("sx", "sy"), None),
            P("ev", ("sx", "sy")),
        ),
        out_specs=(P("ev", None, "sx", "sy", None), P(None, "sx", "sy", None)),
        check_vma=False,
    )
```

```python
import functools

import jax
import jax.numpy as jnp
from jax import lax
from jax.experimental import pallas as pl
from jax.experimental.pallas import tpu as pltpu
from jax.sharding import PartitionSpec as P

DT = 0.35
W = 3
B = 8
XE = B + 2 * W
XS = XE + 2
YR = 16
FIELDS = 12
PLANE = XS * YR
X_HIGH = (2, 3, 3, 3, 3, 3, 3, 3, 3, 3, 2, 2)
X_LOW = (3, 2, 2, 3, 2, 2, 3, 3, 2, 3, 2, 2)
Y_HIGH = (3, 2, 3, 3, 3, 3, 3, 3, 3, 3, 2, 2)
Y_LOW = (2, 3, 2, 2, 3, 2, 3, 2, 3, 3, 2, 2)


PLANES = max(sum(X_HIGH), sum(X_LOW)) + 1


def starts(counts):
    return [sum(counts[:f]) for f in range(len(counts) + 1)]


DEAD = -1.0e6
MIB = 1 << 20
VMEM = pl.BlockSpec(memory_space=pltpu.VMEM)
SMEM = pl.BlockSpec(memory_space=pltpu.SMEM)
HBM = pl.BlockSpec(memory_space=pltpu.HBM)


def x_faces_kernel(
    ny,
    odd_ref,
    adj_hbm,
    rho_hbm,
    lam_hbm,
    mu_hbm,
    count_ref,
    block_hbm,
    cell_hbm,
    trace_hbm,
    first_ref,
    second_ref,
    base_ref,
    block_ref,
    cell_ref,
    trace_ref,
    sems,
):
    params = (rho_hbm, lam_hbm, mu_hbm)
    rows_in = [
        pltpu.make_async_copy(source, target, sems.at[3, i])
        for i, (source, target) in enumerate(((block_hbm, block_ref), (cell_hbm, cell_ref), (trace_hbm, trace_ref)))
    ]

    own = [pltpu.make_async_copy(adj_hbm, base_ref.at[pl.ds(0, 9)], sems.at[2, 0])]
    for i, p in enumerate(params):
        own.append(pltpu.make_async_copy(p, base_ref.at[9 + i], sems.at[2, 1 + i]))
    for copy in rows_in:
        copy.start()

    for copy in own:
        copy.start()
    for copy in rows_in:
        copy.wait()
    rows = cell_ref.shape[1]
    cell = cell_ref[...]
    key = ((cell // B) * ny + block_ref[...] * B + cell % B).astype(jnp.float32)
    live = lax.broadcasted_iota(jnp.int32, (1, rows), 1) < count_ref[0, 0]
    parts = [jnp.where(live, key, DEAD)] + [jnp.where(live, trace_ref[k], 0.0) for k in range(9)]
    parts += [jnp.zeros((1, rows), jnp.float32)] * 6
    pack = jnp.concatenate(
        [jnp.concatenate(parts[:8], axis=0), jnp.concatenate(parts[8:], axis=0), jnp.zeros((8, 128 - 2 * rows), jnp.float32)],
        axis=1,
    )
    first_ref[PLANES - 1] = pack
    second_ref[PLANES - 1] = pack

    for copy in own:
        copy.wait()

    def faces(low_ref, high_ref):
        for out, counts, side in ((low_ref, X_HIGH, 0), (high_ref, X_LOW, 1)):
            for f, (at, count) in enumerate(zip(starts(counts), counts)):
                first = B - count if side else 0
                out[pl.ds(at, count)] = base_ref[f, pl.ds(first, count)]

    by_side(odd_ref, first_ref, second_ref, faces)


def by_side(odd_ref, first_ref, second_ref, body):
    @pl.when(odd_ref[0] == 0)
    def _():
        body(second_ref, first_ref)

    @pl.when(odd_ref[0] == 1)
    def _():
        body(first_ref, second_ref)


def tiles_kernel(ny, odd_ref, own_ref, first_ref, second_ref, tiles_ref):
    row = lax.broadcasted_iota(jnp.int32, (8, 128), 0)
    group = lax.broadcasted_iota(jnp.int32, (8, 128), 1) // 32
    tile = jnp.zeros((8, 128), jnp.float32)
    even = odd_ref[0] == 0
    one, two = first_ref[PLANES - 1], second_ref[PLANES - 1]
    packs = (own_ref[PLANES - 1], jnp.where(even, two, one), jnp.where(even, one, two))
    for s, (pack, shift) in enumerate(zip(packs, (W, W - B, W + B))):
        head = jnp.where(row == 0, pack + float(shift * ny), pack)
        head = pltpu.roll(head, 32 * s, 1) if s else head
        tail = pltpu.roll(pack, 64, 1)
        tail = pltpu.roll(tail, 2 * s, 0) if s else tail
        tile = jnp.where(group == s, head, tile)
        tile = jnp.where((group == 3) & (row // 2 == s), tail, tile)
    for d in range(tiles_ref.shape[0]):
        tiles_ref[d] = tile


def y_faces_kernel(odd_ref, base_ref, first_ref, second_ref, face_low_ref, face_high_ref):
    by_side(odd_ref, first_ref, second_ref, functools.partial(y_faces, base_ref, face_low_ref, face_high_ref))


def y_faces(base_ref, face_low_ref, face_high_ref, low_ref, high_ref):
    x_low, x_high = starts(X_LOW), starts(X_HIGH)
    for side, (out, counts) in enumerate(((face_low_ref, Y_HIGH), (face_high_ref, Y_LOW))):
        for f, (at, count) in enumerate(zip(starts(counts), counts)):
            for r in range(count):
                y = B - count + r if side else r
                row = (at + r) * XE
                below, above = X_LOW[f], X_HIGH[f]
                if below < W:
                    out[pl.ds(row, W - below), :] = jnp.zeros((W - below, 128), jnp.float32)
                out[pl.ds(row + W - below, below), :] = low_ref[pl.ds(x_low[f] * 8 + y, below, stride=8), :]
                out[pl.ds(row + W, B), :] = base_ref[pl.ds(f * 64 + y, B, stride=8), :]
                out[pl.ds(row + W + B, above), :] = high_ref[pl.ds(x_high[f] * 8 + y, above, stride=8), :]
                if above < W:
                    out[pl.ds(row + W + B + above, W - above), :] = jnp.zeros((W - above, 128), jnp.float32)


def surface_kernel(ny, place_ref, tiles_ref, surface_ref):
    group = lax.broadcasted_iota(jnp.int32, (8, 128), 1) // 32
    for s, first, count in ((0, W, B), (1, 0, W), (2, W + B, W)):
        cells = count * YR
        at = lax.broadcasted_iota(jnp.int32, (cells, 128), 0)
        local = at % YR
        local = jnp.where(local < 11, local, local - YR)
        y = place_ref[0] * B + local
        ident = jnp.where((y >= 0) & (y < ny), (first + at // YR) * ny + y, -10000000).astype(jnp.float32)
        hot, packed = [], []
        for source in range(0, tiles_ref.shape[0], 4):
            heads = tails = jnp.zeros((8, 128), jnp.float32)
            for i in range(4):
                tile = tiles_ref[source + i]
                head, tail = (32 * (i - s)) % 128, (32 * (i - 3)) % 128
                heads = jnp.where(group == i, pltpu.roll(tile, head, 1) if head else tile, heads)
                tails = jnp.where(group == i, pltpu.roll(tile, tail, 1) if tail else tile, tails)
            hot.append((ident == heads[0:1]).astype(jnp.float32))
            packed.append(jnp.concatenate([heads, pltpu.roll(tails, 8 - 2 * s, 0) if s else tails], axis=0))
        packed = jnp.concatenate(packed, axis=1)
        packed = jnp.concatenate([packed, jnp.zeros((112, packed.shape[1]), jnp.float32)], axis=0)
        surface_ref[pl.ds(first * YR, cells), :] = lax.dot_general(
            jnp.concatenate(hot, axis=1),
            packed,
            (((1,), (1,)), ((), ())),
            precision=lax.Precision.HIGHEST,
            preferred_element_type=jnp.float32,
        )


def block_kernel(odd_ref, base_ref, first_ref, second_ref, ext):
    by_side(odd_ref, first_ref, second_ref, functools.partial(extend, base_ref, ext))


def extend(base_ref, ext, low_ref, high_ref):
    zero8 = jnp.zeros((8, 128), jnp.float32)
    x_low, x_high = starts(X_LOW), starts(X_HIGH)
    for f in range(FIELDS):
        for e in range(XS):
            x = e - 1 - W
            if 0 <= x < B:
                plane = base_ref[f, x]
            elif -X_LOW[f] <= x < 0:
                plane = low_ref[x_low[f] + X_LOW[f] + x]
            elif B <= x < B + X_HIGH[f]:
                plane = high_ref[x_high[f] + x - B]
            else:
                plane = zero8
            ext[pl.ds(f * PLANE + e * YR, 8), :] = plane
            ext[pl.ds(f * PLANE + e * YR + 8, 8), :] = zero8


def steps_kernel(
    steps,
    _,
    forward_hbm,
    y_low_ref,
    y_high_ref,
    force_ref,
    ext,
    state_ref,
    kernels_ref,
    change_ref,
    rate_ref,
    forward_ref,
    sem,
    load_sem,
):
    loads = [pltpu.make_async_copy(forward_hbm.at[t], forward_ref.at[t], load_sem.at[t]) for t in range(steps)]
    for load in loads:
        load.start()
    for ref, counts, first in ((y_high_ref, Y_HIGH, 8), (y_low_ref, Y_LOW, YR)):
        for f, (at, count) in enumerate(zip(starts(counts), counts)):
            for r in range(count):
                row = f * PLANE + YR + (first + r if first == 8 else first - count + r)
                ext[pl.ds(row, XE, stride=YR), :] = ref[pl.ds((at + r) * XE, XE), :]

    lanes = lax.broadcasted_iota(jnp.int32, (YR, 128), 1)

    def y_up(v):
        return pltpu.roll(v, YR - 1, 0)

    def y_down(v):
        return pltpu.roll(v, 1, 0)

    def z_up(v):
        return jnp.where(lanes == 127, 0.0, pltpu.roll(v, 127, 1))

    def z_down(v):
        return jnp.where(lanes == 0, 0.0, pltpu.roll(v, 1, 1))

    def get(f, e):
        return ext[pl.ds(pl.multiple_of(f * PLANE + e * YR, YR), YR), :]

    def put(f, e, v):
        ext[pl.ds(pl.multiple_of(f * PLANE + e * YR, YR), YR), :] = v

    for step in range(steps):

        def velocity(e):
            sxx, syy, szz, sxy, sxz, syz = [get(3 + f, e) for f in range(6)]
            ax = (get(3, e + 1) - sxx) + (sxy - y_down(sxy)) + (sxz - z_down(sxz))
            ay = (sxy - get(6, e - 1)) + (y_up(syy) - syy) + (syz - z_down(syz))
            az = (sxz - get(7, e - 1)) + (syz - y_down(syz)) + (z_up(szz) - szz)
            scale = DT * get(9, e)
            surface = force_ref[pl.ds(pl.multiple_of((e - 1) * YR, YR), YR), :]
            for c, accel in enumerate((ax, ay, az)):
                force = jnp.where(lanes == 0, pltpu.roll(surface, 127 - 3 * step - c, 1), 0.0)
                change = scale * (accel + force)
                put(c, e, get(c, e) + change)
                change_ref[c, e] = change[0:8]

        def stress(e):
            vx, vy, vz = [get(f, e) for f in range(3)]
            exx = vx - get(0, e - 1)
            eyy = vy - y_down(vy)
            ezz = vz - z_down(vz)
            exy = 0.5 * ((y_up(vx) - vx) + (get(1, e + 1) - vy))
            exz = 0.5 * ((z_up(vx) - vx) + (get(2, e + 1) - vz))
            eyz = 0.5 * ((z_up(vy) - vy) + (y_up(vz) - vz))
            trace = exx + eyy + ezz
            lam = get(10, e) * trace
            twice = 2.0 * get(11, e)
            for f, rate in enumerate((exx, eyy, ezz, exy, exz, eyz)):
                if f < 3:
                    put(3 + f, e, get(3 + f, e) + DT * (lam + twice * rate))
                else:
                    put(3 + f, e, get(3 + f, e) + DT * twice * rate)
                rate_ref[f, e] = rate[0:8]

        def pair(body, first):
            def run(i, carry):
                e = first + 2 * i
                body(e)
                body(e + 1)
                return carry

            return run

        lax.fori_loop(0, (XE - 2 * step) // 2, pair(velocity, 1 + step), 0)
        lax.fori_loop(0, (XE - 2 * step - 2) // 2, pair(stress, 2 + step), 0)
        if step == steps - 1:
            copies = [
                pltpu.make_async_copy(
                    ext.reshape(FIELDS, XS, YR, 128).at[f, pl.ds(1 + W, B), pl.ds(0, B)], state_ref.at[f], sem.at[f]
                )
                for f in range(9)
            ]
            for copy in copies:
                copy.start()

        loads[step].wait()

        def sensitivities(x, carry):
            e = x + 1 + W
            f = [forward_ref[step, c, x].astype(jnp.float32) for c in range(9)]
            change = [change_ref[c, e] for c in range(3)]
            rate = [rate_ref[c, e] for c in range(6)]
            trace = rate[0] + rate[1] + rate[2]
            terms = (
                f[0] * change[0] + f[1] * change[1] + f[2] * change[2],
                DT * (f[3] + f[4] + f[5]) * trace,
                DT
                * 2.0
                * (
                    (f[3] * rate[0] + f[4] * rate[1] + f[5] * rate[2])
                    + 2.0 * (f[6] * rate[3] + f[7] * rate[4] + f[8] * rate[5])
                ),
            )
            for k, term in enumerate(terms):
                kernels_ref[k, x] = kernels_ref[k, x] + term if step else term
            return carry

        lax.fori_loop(0, B, sensitivities, 0, unroll=4)

    for copy in copies:
        copy.wait()


def sum_kernel(events, parts_ref, out_ref):
    size = parts_ref.shape[0] // events
    total = parts_ref[0:size]
    for s in range(1, events):
        total = total + parts_ref[size * s : size * s + size]
    for s in range(events):
        out_ref[size * s : size * s + size] = total


def f32(*shape):
    return jax.ShapeDtypeStruct(shape, jnp.float32)


def swaps(start, count):
    pairs = [(i, i + 1) for i in range(start, count - 1, 2)]
    return pairs + [(b, a) for a, b in pairs]


def in_hbm(a):
    return pltpu.with_memory_space_constraint(a, pltpu.HBM)


def on_device(
    adjoint_state,
    forward_state,
    inv_density,
    lame_lambda,
    shear_modulus,
    station_block,
    station_cell,
    station_trace,
    source_count,
):
    n_sx, n_sy, n_ev = lax.axis_size("sx"), lax.axis_size("sy"), lax.axis_size("ev")
    steps = forward_state.shape[1]
    ny = n_sy * B
    adj = adjoint_state[0]
    up_y = [(i, i + 1) for i in range(n_sy - 1)]
    down_y = [(b, a) for a, b in up_y]

    rows = station_cell.shape[1]
    odd = (lax.axis_index("sx") & 1).astype(jnp.int32).reshape(1)
    first_face, second_face, base = pl.pallas_call(
        functools.partial(x_faces_kernel, ny),
        out_shape=[f32(PLANES, 8, 128)] * 2 + [f32(FIELDS, B, 8, 128)],
        in_specs=[SMEM] + [HBM] * 4 + [SMEM] + [HBM] * 3,
        out_specs=[VMEM] * 3,
        scratch_shapes=[
            pltpu.VMEM((1, rows), jnp.int32),
            pltpu.VMEM((1, rows), jnp.int32),
            pltpu.VMEM((9, 1, rows), jnp.float32),
            pltpu.SemaphoreType.DMA((4, FIELDS)),
        ],
        compiler_params=pltpu.CompilerParams(vmem_limit_bytes=3 * MIB),
        name="x_faces",
    )(
        odd,
        in_hbm(adj),
        in_hbm(inv_density),
        in_hbm(lame_lambda),
        in_hbm(shear_modulus),
        source_count,
        in_hbm(station_block[:, :, 0]),
        in_hbm(station_cell),
        in_hbm(jnp.transpose(station_trace, (2, 0, 1))),
    )
    first = lax.ppermute(first_face, "sx", swaps(0, n_sx))
    second = lax.ppermute(second_face, "sx", swaps(1, n_sx))

    tiles = pl.pallas_call(
        functools.partial(tiles_kernel, ny),
        out_shape=f32(n_sy, 8, 128),
        in_specs=[SMEM] + [VMEM] * 3,
        out_specs=VMEM,
        compiler_params=pltpu.CompilerParams(vmem_limit_bytes=2 * MIB),
        name="tiles",
    )(odd, first_face, first, second)
    tiles = lax.all_to_all(tiles, "sy", split_axis=0, concat_axis=0, tiled=True)

    flat = lambda a: a.reshape(-1, 128)
    y_low_face, y_high_face = pl.pallas_call(
        y_faces_kernel,
        out_shape=[f32(-(-XE * sum(c) // 8) * 8, 128) for c in (Y_HIGH, Y_LOW)],
        in_specs=[SMEM] + [VMEM] * 3,
        out_specs=[VMEM] * 2,
        compiler_params=pltpu.CompilerParams(vmem_limit_bytes=4 * MIB),
        name="y_faces",
    )(odd, flat(base), flat(first), flat(second))
    y_low = lax.ppermute(y_high_face, "sy", up_y)
    y_high = lax.ppermute(y_low_face, "sy", down_y)

    place = lax.axis_index("sy").astype(jnp.int32).reshape(1)
    surface = pl.pallas_call(
        functools.partial(surface_kernel, ny),
        out_shape=f32(XE * YR, 128),
        in_specs=[SMEM, VMEM],
        out_specs=VMEM,
        compiler_params=pltpu.CompilerParams(vmem_limit_bytes=4 * MIB),
        name="surface",
    )(place, tiles)

    ext = pl.pallas_call(
        block_kernel,
        out_shape=f32(FIELDS * PLANE, 128),
        in_specs=[SMEM] + [VMEM] * 3,
        out_specs=VMEM,
        compiler_params=pltpu.CompilerParams(vmem_limit_bytes=4 * MIB),
        name="block",
    )(odd, base, first, second)

    _, state, kernels = pl.pallas_call(
        functools.partial(steps_kernel, steps),
        out_shape=[f32(FIELDS * PLANE, 128), f32(9, B, 8, 128), f32(3, B, 8, 128)],
        in_specs=[VMEM, HBM, VMEM, VMEM, VMEM],
        out_specs=[VMEM, HBM, VMEM],
        input_output_aliases={0: 0},
        scratch_shapes=[
            pltpu.VMEM((3, XS, 8, 128), jnp.float32),
            pltpu.VMEM((6, XS, 8, 128), jnp.float32),
            pltpu.VMEM(forward_state.shape[1:], forward_state.dtype),
            pltpu.SemaphoreType.DMA((9,)),
            pltpu.SemaphoreType.DMA((steps,)),
        ],
        compiler_params=pltpu.CompilerParams(vmem_limit_bytes=8 * MIB),
        name="steps",
    )(ext, in_hbm(forward_state[0]), y_low, y_high, surface)

    parts = lax.all_to_all(kernels.reshape(3 * B, 8, 128), "ev", split_axis=0, concat_axis=0, tiled=True)
    shared = pl.pallas_call(
        functools.partial(sum_kernel, n_ev), out_shape=f32(3 * B, 8, 128), in_specs=[VMEM], out_specs=VMEM, compiler_params=pltpu.CompilerParams(vmem_limit_bytes=1 * MIB),
        name="event_sum"
    )(parts)
    total = lax.all_to_all(shared, "ev", split_axis=0, concat_axis=0, tiled=True)
    return state[None], total.reshape(3, B, 8, 128)


def solution(mesh):
    return jax.shard_map(
        on_device,
        mesh=mesh,
        in_specs=(
            P("ev", None, "sx", "sy", None),
            P("ev", None, None, "sx", "sy", None),
            P("sx", "sy", None),
            P("sx", "sy", None),
            P("sx", "sy", None),
            P("ev", ("sx", "sy"), None),
            P("ev", ("sx", "sy")),
            P("ev", ("sx", "sy"), None),
            P("ev", ("sx", "sy")),
        ),
        out_specs=(P("ev", None, "sx", "sy", None), P(None, "sx", "sy", None)),
        check_vma=False,
    )
```

```python
import functools

import jax
import jax.numpy as jnp
from jax import lax
from jax.experimental import pallas as pl
from jax.experimental.pallas import tpu as pltpu
from jax.sharding import PartitionSpec as P

DT = 0.35
W = 3
B = 8
XE = B + 2 * W
XS = XE + 2
YR = 16
FIELDS = 12
PLANE = XS * YR
X_HIGH = (2, 3, 3, 3, 3, 3, 3, 3, 3, 3, 2, 2)
X_LOW = (3, 2, 2, 3, 2, 2, 3, 3, 2, 3, 2, 2)
Y_HIGH = (3, 2, 3, 3, 3, 3, 3, 3, 3, 3, 2, 2)
Y_LOW = (2, 3, 2, 2, 3, 2, 3, 2, 3, 3, 2, 2)


def starts(counts):
    return [sum(counts[:f]) for f in range(len(counts) + 1)]


DEAD = -1.0e6
MIB = 1 << 20
VMEM = pl.BlockSpec(memory_space=pltpu.VMEM)
SMEM = pl.BlockSpec(memory_space=pltpu.SMEM)
HBM = pl.BlockSpec(memory_space=pltpu.HBM)


def x_faces_kernel(
    ny,
    adj_hbm,
    rho_hbm,
    lam_hbm,
    mu_hbm,
    count_ref,
    block_hbm,
    cell_hbm,
    trace_hbm,
    low_ref,
    high_ref,
    base_ref,
    block_ref,
    cell_ref,
    trace_ref,
    sems,
):
    params = (rho_hbm, lam_hbm, mu_hbm)
    rows_in = [
        pltpu.make_async_copy(source, target, sems.at[1, i])
        for i, (source, target) in enumerate(((block_hbm, block_ref), (cell_hbm, cell_ref), (trace_hbm, trace_ref)))
    ]
    copies = [pltpu.make_async_copy(adj_hbm, base_ref.at[pl.ds(0, 9)], sems.at[0, 0])]
    for i, p in enumerate(params):
        copies.append(pltpu.make_async_copy(p, base_ref.at[9 + i], sems.at[0, 1 + i]))
    for copy in rows_in + copies:
        copy.start()
    for copy in rows_in:
        copy.wait()
    rows = cell_ref.shape[1]
    cell = cell_ref[...]
    key = ((cell // B) * ny + block_ref[...] * B + cell % B).astype(jnp.float32)
    live = lax.broadcasted_iota(jnp.int32, (1, rows), 1) < count_ref[0, 0]
    parts = [jnp.where(live, key, DEAD)] + [jnp.where(live, trace_ref[k], 0.0) for k in range(9)]
    parts += [jnp.zeros((1, rows), jnp.float32)] * 6
    pack = jnp.concatenate(
        [jnp.concatenate(parts[:8], axis=0), jnp.concatenate(parts[8:], axis=0), jnp.zeros((8, 128 - 2 * rows), jnp.float32)],
        axis=1,
    )
    low_ref[sum(X_HIGH)] = pack
    high_ref[sum(X_LOW)] = pack
    for copy in copies:
        copy.wait()
    for out, counts, side in ((low_ref, X_HIGH, 0), (high_ref, X_LOW, 1)):
        for f, (at, count) in enumerate(zip(starts(counts), counts)):
            out[pl.ds(at, count)] = base_ref[f, pl.ds(B - count if side else 0, count)]


def tiles_kernel(ny, own_ref, low_ref, high_ref, tiles_ref):
    row = lax.broadcasted_iota(jnp.int32, (8, 128), 0)
    group = lax.broadcasted_iota(jnp.int32, (8, 128), 1) // 32
    tile = jnp.zeros((8, 128), jnp.float32)
    for s, (ref, shift) in enumerate(((own_ref, W), (low_ref, W - B), (high_ref, W + B))):
        pack = ref[ref.shape[0] - 1]
        head = jnp.where(row == 0, pack + float(shift * ny), pack)
        head = pltpu.roll(head, 32 * s, 1) if s else head
        tail = pltpu.roll(pack, 64, 1)
        tail = pltpu.roll(tail, 2 * s, 0) if s else tail
        tile = jnp.where(group == s, head, tile)
        tile = jnp.where((group == 3) & (row // 2 == s), tail, tile)
    for d in range(tiles_ref.shape[0]):
        tiles_ref[d] = tile


def y_faces_kernel(base_ref, low_ref, high_ref, face_low_ref, face_high_ref):
    x_low, x_high = starts(X_LOW), starts(X_HIGH)
    for side, (out, counts) in enumerate(((face_low_ref, Y_HIGH), (face_high_ref, Y_LOW))):
        for f, (at, count) in enumerate(zip(starts(counts), counts)):
            for r in range(count):
                y = B - count + r if side else r
                row = (at + r) * XE
                below, above = X_LOW[f], X_HIGH[f]
                if below < W:
                    out[pl.ds(row, W - below), :] = jnp.zeros((W - below, 128), jnp.float32)
                out[pl.ds(row + W - below, below), :] = low_ref[pl.ds(x_low[f] * 8 + y, below, stride=8), :]
                out[pl.ds(row + W, B), :] = base_ref[pl.ds(f * 64 + y, B, stride=8), :]
                out[pl.ds(row + W + B, above), :] = high_ref[pl.ds(x_high[f] * 8 + y, above, stride=8), :]
                if above < W:
                    out[pl.ds(row + W + B + above, W - above), :] = jnp.zeros((W - above, 128), jnp.float32)


def surface_kernel(ny, place_ref, tiles_ref, surface_ref):
    group = lax.broadcasted_iota(jnp.int32, (8, 128), 1) // 32
    for s, first, count in ((0, W, B), (1, 0, W), (2, W + B, W)):
        cells = count * YR
        at = lax.broadcasted_iota(jnp.int32, (cells, 128), 0)
        local = at % YR
        local = jnp.where(local < 11, local, local - YR)
        y = place_ref[0] * B + local
        ident = jnp.where((y >= 0) & (y < ny), (first + at // YR) * ny + y, -10000000).astype(jnp.float32)
        hot, packed = [], []
        for source in range(0, tiles_ref.shape[0], 4):
            heads = tails = jnp.zeros((8, 128), jnp.float32)
            for i in range(4):
                tile = tiles_ref[source + i]
                head, tail = (32 * (i - s)) % 128, (32 * (i - 3)) % 128
                heads = jnp.where(group == i, pltpu.roll(tile, head, 1) if head else tile, heads)
                tails = jnp.where(group == i, pltpu.roll(tile, tail, 1) if tail else tile, tails)
            hot.append((ident == heads[0:1]).astype(jnp.float32))
            packed.append(jnp.concatenate([heads, pltpu.roll(tails, 8 - 2 * s, 0) if s else tails], axis=0))
        packed = jnp.concatenate(packed, axis=1)
        packed = jnp.concatenate([packed, jnp.zeros((112, packed.shape[1]), jnp.float32)], axis=0)
        surface_ref[pl.ds(first * YR, cells), :] = lax.dot_general(
            jnp.concatenate(hot, axis=1),
            packed,
            (((1,), (1,)), ((), ())),
            precision=lax.Precision.HIGHEST,
            preferred_element_type=jnp.float32,
        )


def block_kernel(base_ref, low_ref, high_ref, ext):
    zero8 = jnp.zeros((8, 128), jnp.float32)
    x_low, x_high = starts(X_LOW), starts(X_HIGH)
    for f in range(FIELDS):
        for e in range(XS):
            x = e - 1 - W
            if 0 <= x < B:
                plane = base_ref[f, x]
            elif -X_LOW[f] <= x < 0:
                plane = low_ref[x_low[f] + X_LOW[f] + x]
            elif B <= x < B + X_HIGH[f]:
                plane = high_ref[x_high[f] + x - B]
            else:
                plane = zero8
            ext[pl.ds(f * PLANE + e * YR, 8), :] = plane
            ext[pl.ds(f * PLANE + e * YR + 8, 8), :] = zero8


def steps_kernel(
    steps,
    _,
    forward_hbm,
    y_low_ref,
    y_high_ref,
    force_ref,
    ext,
    state_ref,
    kernels_ref,
    change_ref,
    rate_ref,
    forward_ref,
    sem,
    load_sem,
):
    loads = [pltpu.make_async_copy(forward_hbm.at[t], forward_ref.at[t], load_sem.at[t]) for t in range(steps)]
    for load in loads:
        load.start()
    for ref, counts, first in ((y_high_ref, Y_HIGH, 8), (y_low_ref, Y_LOW, YR)):
        for f, (at, count) in enumerate(zip(starts(counts), counts)):
            for r in range(count):
                row = f * PLANE + YR + (first + r if first == 8 else first - count + r)
                ext[pl.ds(row, XE, stride=YR), :] = ref[pl.ds((at + r) * XE, XE), :]

    lanes = lax.broadcasted_iota(jnp.int32, (YR, 128), 1)

    def y_up(v):
        return pltpu.roll(v, YR - 1, 0)

    def y_down(v):
        return pltpu.roll(v, 1, 0)

    def z_up(v):
        return jnp.where(lanes == 127, 0.0, pltpu.roll(v, 127, 1))

    def z_down(v):
        return jnp.where(lanes == 0, 0.0, pltpu.roll(v, 1, 1))

    def get(f, e, rows=YR):
        return ext[pl.ds(pl.multiple_of(f * PLANE + e * YR, YR), rows), :]

    def put(f, e, v):
        ext[pl.ds(pl.multiple_of(f * PLANE + e * YR, YR), v.shape[0]), :] = v

    for step in range(steps):

        def velocity(e):
            sxx, syy, szz, sxy, sxz, syz = [get(3 + f, e) for f in range(6)]
            ax = (get(3, e + 1) - sxx) + (sxy - y_down(sxy)) + (sxz - z_down(sxz))
            ay = (sxy - get(6, e - 1)) + (y_up(syy) - syy) + (syz - z_down(syz))
            az = (sxz - get(7, e - 1)) + (syz - y_down(syz)) + (z_up(szz) - szz)
            scale = DT * get(9, e)
            surface = force_ref[pl.ds(pl.multiple_of((e - 1) * YR, YR), YR), :]
            for c, accel in enumerate((ax, ay, az)):
                force = jnp.where(lanes == 0, pltpu.roll(surface, 127 - 3 * step - c, 1), 0.0)
                change = scale * (accel + force)
                put(c, e, get(c, e) + change)
                change_ref[c, e] = change[0:8]

        def stress(e):
            vx, vy, vz = [get(f, e) for f in range(3)]
            exx = vx - get(0, e - 1)
            eyy = vy - y_down(vy)
            ezz = vz - z_down(vz)
            exy = 0.5 * ((y_up(vx) - vx) + (get(1, e + 1) - vy))
            exz = 0.5 * ((z_up(vx) - vx) + (get(2, e + 1) - vz))
            eyz = 0.5 * ((z_up(vy) - vy) + (y_up(vz) - vz))
            rates = (exx, eyy, ezz, exy, exz, eyz)
            if step == steps - 1:
                rates = [rate[0:8] for rate in rates]
            rows = rates[0].shape[0]
            trace = rates[0] + rates[1] + rates[2]
            lam = get(10, e, rows) * trace
            twice = 2.0 * get(11, e, rows)
            for f, rate in enumerate(rates):
                if f < 3:
                    put(3 + f, e, get(3 + f, e, rows) + DT * (lam + twice * rate))
                else:
                    put(3 + f, e, get(3 + f, e, rows) + DT * twice * rate)
                rate_ref[f, e] = rate[0:8]

        def pair(body, first):
            def run(i, carry):
                e = first + 2 * i
                body(e)
                body(e + 1)
                return carry

            return run

        lax.fori_loop(0, (XE - 2 * step) // 2, pair(velocity, 1 + step), 0)
        lax.fori_loop(0, (XE - 2 * step - 2) // 2, pair(stress, 2 + step), 0)
        if step == steps - 1:
            copies = [
                pltpu.make_async_copy(
                    ext.reshape(FIELDS, XS, YR, 128).at[f, pl.ds(1 + W, B), pl.ds(0, B)], state_ref.at[f], sem.at[f]
                )
                for f in range(9)
            ]
            for copy in copies:
                copy.start()

        loads[step].wait()

        def sensitivities(x, carry):
            e = x + 1 + W
            f = [forward_ref[step, c, x].astype(jnp.float32) for c in range(9)]
            change = [change_ref[c, e] for c in range(3)]
            rate = [rate_ref[c, e] for c in range(6)]
            trace = rate[0] + rate[1] + rate[2]
            terms = (
                f[0] * change[0] + f[1] * change[1] + f[2] * change[2],
                DT * (f[3] + f[4] + f[5]) * trace,
                DT
                * 2.0
                * (
                    (f[3] * rate[0] + f[4] * rate[1] + f[5] * rate[2])
                    + 2.0 * (f[6] * rate[3] + f[7] * rate[4] + f[8] * rate[5])
                ),
            )
            for k, term in enumerate(terms):
                kernels_ref[k, x] = kernels_ref[k, x] + term if step else term
            return carry

        lax.fori_loop(0, B, sensitivities, 0, unroll=4)

    for copy in copies:
        copy.wait()


def sum_kernel(events, parts_ref, out_ref):
    size = parts_ref.shape[0] // events
    total = parts_ref[0:size]
    for s in range(1, events):
        total = total + parts_ref[size * s : size * s + size]
    for s in range(events):
        out_ref[size * s : size * s + size] = total


def f32(*shape):
    return jax.ShapeDtypeStruct(shape, jnp.float32)


def in_hbm(a):
    return pltpu.with_memory_space_constraint(a, pltpu.HBM)


def on_device(
    adjoint_state,
    forward_state,
    inv_density,
    lame_lambda,
    shear_modulus,
    station_block,
    station_cell,
    station_trace,
    source_count,
):
    n_sx, n_sy, n_ev = lax.axis_size("sx"), lax.axis_size("sy"), lax.axis_size("ev")
    steps = forward_state.shape[1]
    ny = n_sy * B
    adj = adjoint_state[0]
    up_x = [(i, i + 1) for i in range(n_sx - 1)]
    up_y = [(i, i + 1) for i in range(n_sy - 1)]
    down_x = [(b, a) for a, b in up_x]
    down_y = [(b, a) for a, b in up_y]

    rows = station_cell.shape[1]
    low_face, high_face, base = pl.pallas_call(
        functools.partial(x_faces_kernel, ny),
        out_shape=[f32(sum(X_HIGH) + 1, 8, 128), f32(sum(X_LOW) + 1, 8, 128), f32(FIELDS, B, 8, 128)],
        in_specs=[HBM] * 4 + [SMEM] + [HBM] * 3,
        out_specs=[VMEM] * 3,
        scratch_shapes=[
            pltpu.VMEM((1, rows), jnp.int32),
            pltpu.VMEM((1, rows), jnp.int32),
            pltpu.VMEM((9, 1, rows), jnp.float32),
            pltpu.SemaphoreType.DMA((2, 4)),
        ],
        compiler_params=pltpu.CompilerParams(vmem_limit_bytes=3 * MIB),
        name="x_faces",
    )(
        in_hbm(adj),
        in_hbm(inv_density),
        in_hbm(lame_lambda),
        in_hbm(shear_modulus),
        source_count,
        in_hbm(station_block[:, :, 0]),
        in_hbm(station_cell),
        in_hbm(jnp.transpose(station_trace, (2, 0, 1))),
    )
    low = lax.ppermute(high_face, "sx", up_x)
    high = lax.ppermute(low_face, "sx", down_x)

    tiles = pl.pallas_call(
        functools.partial(tiles_kernel, ny),
        out_shape=f32(n_sy, 8, 128),
        in_specs=[VMEM] * 3,
        out_specs=VMEM,
        compiler_params=pltpu.CompilerParams(vmem_limit_bytes=2 * MIB),
        name="tiles",
    )(low_face, low, high)
    tiles = lax.all_to_all(tiles, "sy", split_axis=0, concat_axis=0, tiled=True)

    flat = lambda a: a.reshape(-1, 128)
    y_low_face, y_high_face = pl.pallas_call(
        y_faces_kernel,
        out_shape=[f32(-(-XE * sum(c) // 8) * 8, 128) for c in (Y_HIGH, Y_LOW)],
        in_specs=[VMEM] * 3,
        out_specs=[VMEM] * 2,
        compiler_params=pltpu.CompilerParams(vmem_limit_bytes=4 * MIB),
        name="y_faces",
    )(flat(base), flat(low), flat(high))
    y_low = lax.ppermute(y_high_face, "sy", up_y)
    y_high = lax.ppermute(y_low_face, "sy", down_y)

    place = lax.axis_index("sy").astype(jnp.int32).reshape(1)
    surface = pl.pallas_call(
        functools.partial(surface_kernel, ny),
        out_shape=f32(XE * YR, 128),
        in_specs=[SMEM, VMEM],
        out_specs=VMEM,
        compiler_params=pltpu.CompilerParams(vmem_limit_bytes=4 * MIB),
        name="surface",
    )(place, tiles)

    ext = pl.pallas_call(
        block_kernel,
        out_shape=f32(FIELDS * PLANE, 128),
        in_specs=[VMEM] * 3,
        out_specs=VMEM,
        compiler_params=pltpu.CompilerParams(vmem_limit_bytes=4 * MIB),
        name="block",
    )(base, low, high)

    _, state, kernels = pl.pallas_call(
        functools.partial(steps_kernel, steps),
        out_shape=[f32(FIELDS * PLANE, 128), f32(9, B, 8, 128), f32(3, B, 8, 128)],
        in_specs=[VMEM, HBM, VMEM, VMEM, VMEM],
        out_specs=[VMEM, HBM, VMEM],
        input_output_aliases={0: 0},
        scratch_shapes=[
            pltpu.VMEM((3, XS, 8, 128), jnp.float32),
            pltpu.VMEM((6, XS, 8, 128), jnp.float32),
            pltpu.VMEM(forward_state.shape[1:], forward_state.dtype),
            pltpu.SemaphoreType.DMA((9,)),
            pltpu.SemaphoreType.DMA((steps,)),
        ],
        compiler_params=pltpu.CompilerParams(vmem_limit_bytes=8 * MIB),
        name="steps",
    )(ext, in_hbm(forward_state[0]), y_low, y_high, surface)

    parts = lax.all_to_all(kernels.reshape(3 * B, 8, 128), "ev", split_axis=0, concat_axis=0, tiled=True)
    shared = pl.pallas_call(
        functools.partial(sum_kernel, n_ev), out_shape=f32(3 * B, 8, 128), in_specs=[VMEM], out_specs=VMEM, compiler_params=pltpu.CompilerParams(vmem_limit_bytes=1 * MIB),
        name="event_sum"
    )(parts)
    total = lax.all_to_all(shared, "ev", split_axis=0, concat_axis=0, tiled=True)
    return state[None], total.reshape(3, B, 8, 128)


def solution(mesh):
    return jax.shard_map(
        on_device,
        mesh=mesh,
        in_specs=(
            P("ev", None, "sx", "sy", None),
            P("ev", None, None, "sx", "sy", None),
            P("sx", "sy", None),
            P("sx", "sy", None),
            P("sx", "sy", None),
            P("ev", ("sx", "sy"), None),
            P("ev", ("sx", "sy")),
            P("ev", ("sx", "sy"), None),
            P("ev", ("sx", "sy")),
        ),
        out_specs=(P("ev", None, "sx", "sy", None), P(None, "sx", "sy", None)),
        check_vma=False,
    )
```

```python
import functools

import jax
import jax.numpy as jnp
from jax import lax
from jax.experimental import pallas as pl
from jax.experimental.pallas import tpu as pltpu
from jax.sharding import PartitionSpec as P

DT = 0.35
W = 3
B = 8
XE = B + 2 * W
XS = XE + 2
YR = 16
FIELDS = 12
PLANE = XS * YR
X_HIGH = (2, 3, 3, 3, 3, 3, 3, 3, 3, 3, 2, 2)
X_LOW = (3, 2, 2, 3, 2, 2, 3, 3, 2, 3, 2, 2)
Y_HIGH = (3, 2, 3, 3, 3, 3, 3, 3, 3, 3, 2, 2)
Y_LOW = (2, 3, 2, 2, 3, 2, 3, 2, 3, 3, 2, 2)


def starts(counts):
    return [sum(counts[:f]) for f in range(len(counts) + 1)]


DEAD = -1.0e6
MIB = 1 << 20
VMEM = pl.BlockSpec(memory_space=pltpu.VMEM)
SMEM = pl.BlockSpec(memory_space=pltpu.SMEM)
HBM = pl.BlockSpec(memory_space=pltpu.HBM)


def x_faces_kernel(
    ny,
    adj_hbm,
    rho_hbm,
    lam_hbm,
    mu_hbm,
    count_ref,
    block_hbm,
    cell_hbm,
    trace_hbm,
    low_ref,
    high_ref,
    base_ref,
    block_ref,
    cell_ref,
    trace_ref,
    sems,
):
    params = (rho_hbm, lam_hbm, mu_hbm)
    rows_in = [
        pltpu.make_async_copy(source, target, sems.at[1, i])
        for i, (source, target) in enumerate(((block_hbm, block_ref), (cell_hbm, cell_ref), (trace_hbm, trace_ref)))
    ]
    copies = [pltpu.make_async_copy(adj_hbm, base_ref.at[pl.ds(0, 9)], sems.at[0, 0])]
    for i, p in enumerate(params):
        copies.append(pltpu.make_async_copy(p, base_ref.at[9 + i], sems.at[0, 1 + i]))
    for copy in rows_in + copies:
        copy.start()
    for copy in rows_in:
        copy.wait()
    rows = cell_ref.shape[1]
    cell = cell_ref[...]
    key = ((cell // B) * ny + block_ref[...] * B + cell % B).astype(jnp.float32)
    live = lax.broadcasted_iota(jnp.int32, (1, rows), 1) < count_ref[0, 0]
    parts = [jnp.where(live, key, DEAD)] + [jnp.where(live, trace_ref[k], 0.0) for k in range(9)]
    parts += [jnp.zeros((1, rows), jnp.float32)] * 6
    pack = jnp.concatenate(
        [jnp.concatenate(parts[:8], axis=0), jnp.concatenate(parts[8:], axis=0), jnp.zeros((8, 128 - 2 * rows), jnp.float32)],
        axis=1,
    )
    low_ref[sum(X_HIGH)] = pack
    high_ref[sum(X_LOW)] = pack
    for copy in copies:
        copy.wait()
    for out, counts, side in ((low_ref, X_HIGH, 0), (high_ref, X_LOW, 1)):
        for f, (at, count) in enumerate(zip(starts(counts), counts)):
            out[pl.ds(at, count)] = base_ref[f, pl.ds(B - count if side else 0, count)]


def tiles_kernel(ny, own_ref, low_ref, high_ref, tiles_ref):
    row = lax.broadcasted_iota(jnp.int32, (8, 128), 0)
    group = lax.broadcasted_iota(jnp.int32, (8, 128), 1) // 32
    tile = jnp.zeros((8, 128), jnp.float32)
    for s, (ref, shift) in enumerate(((own_ref, W), (low_ref, W - B), (high_ref, W + B))):
        pack = ref[ref.shape[0] - 1]
        head = jnp.where(row == 0, pack + float(shift * ny), pack)
        head = pltpu.roll(head, 32 * s, 1) if s else head
        tail = pltpu.roll(pack, 64, 1)
        tail = pltpu.roll(tail, 2 * s, 0) if s else tail
        tile = jnp.where(group == s, head, tile)
        tile = jnp.where((group == 3) & (row // 2 == s), tail, tile)
    for d in range(tiles_ref.shape[0]):
        tiles_ref[d] = tile


def y_faces_kernel(base_ref, low_ref, high_ref, face_low_ref, face_high_ref):
    x_low, x_high = starts(X_LOW), starts(X_HIGH)
    for side, (out, counts) in enumerate(((face_low_ref, Y_HIGH), (face_high_ref, Y_LOW))):
        for f, (at, count) in enumerate(zip(starts(counts), counts)):
            for r in range(count):
                y = B - count + r if side else r
                row = (at + r) * XE
                below, above = X_LOW[f], X_HIGH[f]
                if below < W:
                    out[pl.ds(row, W - below), :] = jnp.zeros((W - below, 128), jnp.float32)
                out[pl.ds(row + W - below, below), :] = low_ref[pl.ds(x_low[f] * 8 + y, below, stride=8), :]
                out[pl.ds(row + W, B), :] = base_ref[pl.ds(f * 64 + y, B, stride=8), :]
                out[pl.ds(row + W + B, above), :] = high_ref[pl.ds(x_high[f] * 8 + y, above, stride=8), :]
                if above < W:
                    out[pl.ds(row + W + B + above, W - above), :] = jnp.zeros((W - above, 128), jnp.float32)


def surface_kernel(ny, place_ref, tiles_ref, surface_ref):
    group = lax.broadcasted_iota(jnp.int32, (8, 128), 1) // 32
    for s, first, count in ((0, W, B), (1, 0, W), (2, W + B, W)):
        cells = count * YR
        at = lax.broadcasted_iota(jnp.int32, (cells, 128), 0)
        local = at % YR
        local = jnp.where(local < 11, local, local - YR)
        y = place_ref[0] * B + local
        ident = jnp.where((y >= 0) & (y < ny), (first + at // YR) * ny + y, -10000000).astype(jnp.float32)
        hot, packed = [], []
        for source in range(0, tiles_ref.shape[0], 4):
            heads = tails = jnp.zeros((8, 128), jnp.float32)
            for i in range(4):
                tile = tiles_ref[source + i]
                head, tail = (32 * (i - s)) % 128, (32 * (i - 3)) % 128
                heads = jnp.where(group == i, pltpu.roll(tile, head, 1) if head else tile, heads)
                tails = jnp.where(group == i, pltpu.roll(tile, tail, 1) if tail else tile, tails)
            hot.append((ident == heads[0:1]).astype(jnp.float32))
            packed.append(jnp.concatenate([heads, pltpu.roll(tails, 8 - 2 * s, 0) if s else tails], axis=0))
        packed = jnp.concatenate(packed, axis=1)
        packed = jnp.concatenate([packed, jnp.zeros((112, packed.shape[1]), jnp.float32)], axis=0)
        surface_ref[pl.ds(first * YR, cells), :] = lax.dot_general(
            jnp.concatenate(hot, axis=1),
            packed,
            (((1,), (1,)), ((), ())),
            precision=lax.Precision.HIGHEST,
            preferred_element_type=jnp.float32,
        )


def block_kernel(base_ref, low_ref, high_ref, ext):
    zero8 = jnp.zeros((8, 128), jnp.float32)
    x_low, x_high = starts(X_LOW), starts(X_HIGH)
    for f in range(FIELDS):
        for e in range(XS):
            x = e - 1 - W
            if 0 <= x < B:
                plane = base_ref[f, x]
            elif -X_LOW[f] <= x < 0:
                plane = low_ref[x_low[f] + X_LOW[f] + x]
            elif B <= x < B + X_HIGH[f]:
                plane = high_ref[x_high[f] + x - B]
            else:
                plane = zero8
            ext[pl.ds(f * PLANE + e * YR, 8), :] = plane
            ext[pl.ds(f * PLANE + e * YR + 8, 8), :] = zero8


def steps_kernel(
    steps,
    _,
    forward_hbm,
    y_low_ref,
    y_high_ref,
    force_ref,
    ext,
    state_ref,
    kernels_ref,
    change_ref,
    rate_ref,
    forward_ref,
    sem,
    load_sem,
):
    loads = [pltpu.make_async_copy(forward_hbm.at[t], forward_ref.at[t], load_sem.at[t]) for t in range(steps)]
    for load in loads:
        load.start()
    for ref, counts, first in ((y_high_ref, Y_HIGH, 8), (y_low_ref, Y_LOW, YR)):
        for f, (at, count) in enumerate(zip(starts(counts), counts)):
            for r in range(count):
                row = f * PLANE + YR + (first + r if first == 8 else first - count + r)
                ext[pl.ds(row, XE, stride=YR), :] = ref[pl.ds((at + r) * XE, XE), :]

    lanes = lax.broadcasted_iota(jnp.int32, (YR, 128), 1)

    def y_up(v):
        return pltpu.roll(v, YR - 1, 0)

    def y_down(v):
        return pltpu.roll(v, 1, 0)

    def z_up(v):
        return jnp.where(lanes == 127, 0.0, pltpu.roll(v, 127, 1))

    def z_down(v):
        return jnp.where(lanes == 0, 0.0, pltpu.roll(v, 1, 1))

    def get(f, e, rows=YR):
        return ext[pl.ds(pl.multiple_of(f * PLANE + e * YR, YR), rows), :]

    def put(f, e, v):
        ext[pl.ds(pl.multiple_of(f * PLANE + e * YR, YR), v.shape[0]), :] = v

    for step in range(steps):

        def velocity(e):
            sxx, syy, szz, sxy, sxz, syz = [get(3 + f, e) for f in range(6)]
            ax = (get(3, e + 1) - sxx) + (sxy - y_down(sxy)) + (sxz - z_down(sxz))
            ay = (sxy - get(6, e - 1)) + (y_up(syy) - syy) + (syz - z_down(syz))
            az = (sxz - get(7, e - 1)) + (syz - y_down(syz)) + (z_up(szz) - szz)
            scale = DT * get(9, e)
            surface = force_ref[pl.ds(pl.multiple_of((e - 1) * YR, YR), YR), :]
            for c, accel in enumerate((ax, ay, az)):
                force = jnp.where(lanes == 0, pltpu.roll(surface, 127 - 3 * step - c, 1), 0.0)
                change = scale * (accel + force)
                put(c, e, get(c, e) + change)
                change_ref[3 * step + c, e] = change[0:8]

        def stress(e):
            vx, vy, vz = [get(f, e) for f in range(3)]
            exx = vx - get(0, e - 1)
            eyy = vy - y_down(vy)
            ezz = vz - z_down(vz)
            exy = 0.5 * ((y_up(vx) - vx) + (get(1, e + 1) - vy))
            exz = 0.5 * ((z_up(vx) - vx) + (get(2, e + 1) - vz))
            eyz = 0.5 * ((z_up(vy) - vy) + (y_up(vz) - vz))
            rates = (exx, eyy, ezz, exy, exz, eyz)
            if step == steps - 1:
                rates = [rate[0:8] for rate in rates]
            rows = rates[0].shape[0]
            trace = rates[0] + rates[1] + rates[2]
            lam = get(10, e, rows) * trace
            twice = 2.0 * get(11, e, rows)
            for f, rate in enumerate(rates):
                if f < 3:
                    put(3 + f, e, get(3 + f, e, rows) + DT * (lam + twice * rate))
                else:
                    put(3 + f, e, get(3 + f, e, rows) + DT * twice * rate)
                rate_ref[6 * step + f, e] = rate[0:8]

        def pair(body, first):
            def run(i, carry):
                e = first + 2 * i
                body(e)
                body(e + 1)
                return carry

            return run

        lax.fori_loop(0, (XE - 2 * step) // 2, pair(velocity, 1 + step), 0)
        lax.fori_loop(0, (XE - 2 * step - 2) // 2, pair(stress, 2 + step), 0)
    copies = [
        pltpu.make_async_copy(
            ext.reshape(FIELDS, XS, YR, 128).at[f, pl.ds(1 + W, B), pl.ds(0, B)], state_ref.at[f], sem.at[f]
        )
        for f in range(9)
    ]
    for copy in copies:
        copy.start()
    for load in loads:
        load.wait()

    def sensitivities(x, carry):
        e = x + 1 + W
        totals = None
        for step in range(steps):
            f = [forward_ref[step, c, x].astype(jnp.float32) for c in range(9)]
            change = [change_ref[3 * step + c, e] for c in range(3)]
            rate = [rate_ref[6 * step + c, e] for c in range(6)]
            trace = rate[0] + rate[1] + rate[2]
            terms = (
                f[0] * change[0] + f[1] * change[1] + f[2] * change[2],
                DT * (f[3] + f[4] + f[5]) * trace,
                DT
                * 2.0
                * (
                    (f[3] * rate[0] + f[4] * rate[1] + f[5] * rate[2])
                    + 2.0 * (f[6] * rate[3] + f[7] * rate[4] + f[8] * rate[5])
                ),
            )
            totals = [total + term for total, term in zip(totals, terms)] if step else terms
        for k in range(3):
            kernels_ref[k, x] = totals[k]
        return carry

    lax.fori_loop(0, B, sensitivities, 0, unroll=2)

    for copy in copies:
        copy.wait()


def sum_kernel(events, parts_ref, out_ref):
    size = parts_ref.shape[0] // events
    total = parts_ref[0:size]
    for s in range(1, events):
        total = total + parts_ref[size * s : size * s + size]
    for s in range(events):
        out_ref[size * s : size * s + size] = total


def f32(*shape):
    return jax.ShapeDtypeStruct(shape, jnp.float32)


def in_hbm(a):
    return pltpu.with_memory_space_constraint(a, pltpu.HBM)


def on_device(
    adjoint_state,
    forward_state,
    inv_density,
    lame_lambda,
    shear_modulus,
    station_block,
    station_cell,
    station_trace,
    source_count,
):
    n_sx, n_sy, n_ev = lax.axis_size("sx"), lax.axis_size("sy"), lax.axis_size("ev")
    steps = forward_state.shape[1]
    ny = n_sy * B
    adj = adjoint_state[0]
    up_x = [(i, i + 1) for i in range(n_sx - 1)]
    up_y = [(i, i + 1) for i in range(n_sy - 1)]
    down_x = [(b, a) for a, b in up_x]
    down_y = [(b, a) for a, b in up_y]

    rows = station_cell.shape[1]
    low_face, high_face, base = pl.pallas_call(
        functools.partial(x_faces_kernel, ny),
        out_shape=[f32(sum(X_HIGH) + 1, 8, 128), f32(sum(X_LOW) + 1, 8, 128), f32(FIELDS, B, 8, 128)],
        in_specs=[HBM] * 4 + [SMEM] + [HBM] * 3,
        out_specs=[VMEM] * 3,
        scratch_shapes=[
            pltpu.VMEM((1, rows), jnp.int32),
            pltpu.VMEM((1, rows), jnp.int32),
            pltpu.VMEM((9, 1, rows), jnp.float32),
            pltpu.SemaphoreType.DMA((2, 4)),
        ],
        compiler_params=pltpu.CompilerParams(vmem_limit_bytes=3 * MIB),
        name="x_faces",
    )(
        in_hbm(adj),
        in_hbm(inv_density),
        in_hbm(lame_lambda),
        in_hbm(shear_modulus),
        source_count,
        in_hbm(station_block[:, :, 0]),
        in_hbm(station_cell),
        in_hbm(jnp.transpose(station_trace, (2, 0, 1))),
    )
    low = lax.ppermute(high_face, "sx", up_x)
    high = lax.ppermute(low_face, "sx", down_x)

    tiles = pl.pallas_call(
        functools.partial(tiles_kernel, ny),
        out_shape=f32(n_sy, 8, 128),
        in_specs=[VMEM] * 3,
        out_specs=VMEM,
        compiler_params=pltpu.CompilerParams(vmem_limit_bytes=2 * MIB),
        name="tiles",
    )(low_face, low, high)
    tiles = lax.all_to_all(tiles, "sy", split_axis=0, concat_axis=0, tiled=True)

    flat = lambda a: a.reshape(-1, 128)
    y_low_face, y_high_face = pl.pallas_call(
        y_faces_kernel,
        out_shape=[f32(-(-XE * sum(c) // 8) * 8, 128) for c in (Y_HIGH, Y_LOW)],
        in_specs=[VMEM] * 3,
        out_specs=[VMEM] * 2,
        compiler_params=pltpu.CompilerParams(vmem_limit_bytes=4 * MIB),
        name="y_faces",
    )(flat(base), flat(low), flat(high))
    y_low = lax.ppermute(y_high_face, "sy", up_y)
    y_high = lax.ppermute(y_low_face, "sy", down_y)

    place = lax.axis_index("sy").astype(jnp.int32).reshape(1)
    surface = pl.pallas_call(
        functools.partial(surface_kernel, ny),
        out_shape=f32(XE * YR, 128),
        in_specs=[SMEM, VMEM],
        out_specs=VMEM,
        compiler_params=pltpu.CompilerParams(vmem_limit_bytes=4 * MIB),
        name="surface",
    )(place, tiles)

    ext = pl.pallas_call(
        block_kernel,
        out_shape=f32(FIELDS * PLANE, 128),
        in_specs=[VMEM] * 3,
        out_specs=VMEM,
        compiler_params=pltpu.CompilerParams(vmem_limit_bytes=4 * MIB),
        name="block",
    )(base, low, high)

    _, state, kernels = pl.pallas_call(
        functools.partial(steps_kernel, steps),
        out_shape=[f32(FIELDS * PLANE, 128), f32(9, B, 8, 128), f32(3, B, 8, 128)],
        in_specs=[VMEM, HBM, VMEM, VMEM, VMEM],
        out_specs=[VMEM, HBM, VMEM],
        input_output_aliases={0: 0},
        scratch_shapes=[
            pltpu.VMEM((3 * steps, XS, 8, 128), jnp.float32),
            pltpu.VMEM((6 * steps, XS, 8, 128), jnp.float32),
            pltpu.VMEM(forward_state.shape[1:], forward_state.dtype),
            pltpu.SemaphoreType.DMA((9,)),
            pltpu.SemaphoreType.DMA((steps,)),
        ],
        compiler_params=pltpu.CompilerParams(vmem_limit_bytes=8 * MIB),
        name="steps",
    )(ext, in_hbm(forward_state[0]), y_low, y_high, surface)

    parts = lax.all_to_all(kernels.reshape(3 * B, 8, 128), "ev", split_axis=0, concat_axis=0, tiled=True)
    shared = pl.pallas_call(
        functools.partial(sum_kernel, n_ev), out_shape=f32(3 * B, 8, 128), in_specs=[VMEM], out_specs=VMEM, compiler_params=pltpu.CompilerParams(vmem_limit_bytes=1 * MIB),
        name="event_sum"
    )(parts)
    total = lax.all_to_all(shared, "ev", split_axis=0, concat_axis=0, tiled=True)
    return state[None], total.reshape(3, B, 8, 128)


def solution(mesh):
    return jax.shard_map(
        on_device,
        mesh=mesh,
        in_specs=(
            P("ev", None, "sx", "sy", None),
            P("ev", None, None, "sx", "sy", None),
            P("sx", "sy", None),
            P("sx", "sy", None),
            P("sx", "sy", None),
            P("ev", ("sx", "sy"), None),
            P("ev", ("sx", "sy")),
            P("ev", ("sx", "sy"), None),
            P("ev", ("sx", "sy")),
        ),
        out_specs=(P("ev", None, "sx", "sy", None), P(None, "sx", "sy", None)),
        check_vma=False,
    )
```

```python
import functools

import jax
import jax.numpy as jnp
from jax import lax
from jax.experimental import pallas as pl
from jax.experimental.pallas import tpu as pltpu
from jax.sharding import PartitionSpec as P

DT = 0.35
W = 3
B = 8
XE = B + 2 * W
XS = XE + 2
YR = 16
FIELDS = 12
PLANE = XS * YR
X_HIGH = (2, 3, 3, 3, 3, 3, 3, 3, 3, 3, 2, 2)
X_LOW = (3, 2, 2, 3, 2, 2, 3, 3, 2, 3, 2, 2)
Y_HIGH = (3, 2, 3, 3, 3, 3, 3, 3, 3, 3, 2, 2)
Y_LOW = (2, 3, 2, 2, 3, 2, 3, 2, 3, 3, 2, 2)


def starts(counts):
    return [sum(counts[:f]) for f in range(len(counts) + 1)]


DEAD = -1.0e6
MIB = 1 << 20
VMEM = pl.BlockSpec(memory_space=pltpu.VMEM)
SMEM = pl.BlockSpec(memory_space=pltpu.SMEM)
HBM = pl.BlockSpec(memory_space=pltpu.HBM)


def x_faces_kernel(
    ny,
    adj_hbm,
    rho_hbm,
    lam_hbm,
    mu_hbm,
    count_ref,
    block_hbm,
    cell_hbm,
    trace_hbm,
    low_ref,
    high_ref,
    base_ref,
    block_ref,
    cell_ref,
    trace_ref,
    sems,
):
    params = (rho_hbm, lam_hbm, mu_hbm)
    rows_in = [
        pltpu.make_async_copy(source, target, sems.at[1, i])
        for i, (source, target) in enumerate(((block_hbm, block_ref), (cell_hbm, cell_ref), (trace_hbm, trace_ref)))
    ]
    copies = [pltpu.make_async_copy(adj_hbm, base_ref.at[pl.ds(0, 9)], sems.at[0, 0])]
    for i, p in enumerate(params):
        copies.append(pltpu.make_async_copy(p, base_ref.at[9 + i], sems.at[0, 1 + i]))
    for copy in rows_in + copies:
        copy.start()
    for copy in rows_in:
        copy.wait()
    rows = cell_ref.shape[1]
    cell = cell_ref[...]
    key = ((cell // B) * ny + block_ref[...] * B + cell % B).astype(jnp.float32)
    live = lax.broadcasted_iota(jnp.int32, (1, rows), 1) < count_ref[0, 0]
    parts = [jnp.where(live, key, DEAD)] + [jnp.where(live, trace_ref[k], 0.0) for k in range(9)]
    parts += [jnp.zeros((1, rows), jnp.float32)] * 6
    pack = jnp.concatenate(
        [jnp.concatenate(parts[:8], axis=0), jnp.concatenate(parts[8:], axis=0), jnp.zeros((8, 128 - 2 * rows), jnp.float32)],
        axis=1,
    )
    low_ref[sum(X_HIGH)] = pack
    high_ref[sum(X_LOW)] = pack
    for copy in copies:
        copy.wait()
    for out, counts, side in ((low_ref, X_HIGH, 0), (high_ref, X_LOW, 1)):
        for f, (at, count) in enumerate(zip(starts(counts), counts)):
            out[pl.ds(at, count)] = base_ref[f, pl.ds(B - count if side else 0, count)]


def tiles_kernel(ny, own_ref, low_ref, high_ref, tiles_ref):
    row = lax.broadcasted_iota(jnp.int32, (8, 128), 0)
    group = lax.broadcasted_iota(jnp.int32, (8, 128), 1) // 32
    tile = jnp.zeros((8, 128), jnp.float32)
    for s, (ref, shift) in enumerate(((own_ref, W), (low_ref, W - B), (high_ref, W + B))):
        pack = ref[ref.shape[0] - 1]
        head = jnp.where(row == 0, pack + float(shift * ny), pack)
        head = pltpu.roll(head, 32 * s, 1) if s else head
        tail = pltpu.roll(pack, 64, 1)
        tail = pltpu.roll(tail, 2 * s, 0) if s else tail
        tile = jnp.where(group == s, head, tile)
        tile = jnp.where((group == 3) & (row // 2 == s), tail, tile)
    for d in range(tiles_ref.shape[0]):
        tiles_ref[d] = tile


def y_faces_kernel(base_ref, low_ref, high_ref, face_low_ref, face_high_ref):
    x_low, x_high = starts(X_LOW), starts(X_HIGH)
    for side, (out, counts) in enumerate(((face_low_ref, Y_HIGH), (face_high_ref, Y_LOW))):
        for f, (at, count) in enumerate(zip(starts(counts), counts)):
            for r in range(count):
                y = B - count + r if side else r
                row = (at + r) * XE
                below, above = X_LOW[f], X_HIGH[f]
                if below < W:
                    out[pl.ds(row, W - below), :] = jnp.zeros((W - below, 128), jnp.float32)
                out[pl.ds(row + W - below, below), :] = low_ref[pl.ds(x_low[f] * 8 + y, below, stride=8), :]
                out[pl.ds(row + W, B), :] = base_ref[pl.ds(f * 64 + y, B, stride=8), :]
                out[pl.ds(row + W + B, above), :] = high_ref[pl.ds(x_high[f] * 8 + y, above, stride=8), :]
                if above < W:
                    out[pl.ds(row + W + B + above, W - above), :] = jnp.zeros((W - above, 128), jnp.float32)


def surface_kernel(ny, place_ref, tiles_ref, surface_ref):
    group = lax.broadcasted_iota(jnp.int32, (8, 128), 1) // 32
    for s, first, count in ((0, W, B), (1, 0, W), (2, W + B, W)):
        cells = count * YR
        at = lax.broadcasted_iota(jnp.int32, (cells, 128), 0)
        local = at % YR
        local = jnp.where(local < 11, local, local - YR)
        y = place_ref[0] * B + local
        ident = jnp.where((y >= 0) & (y < ny), (first + at // YR) * ny + y, -10000000).astype(jnp.float32)
        hot, packed = [], []
        for source in range(0, tiles_ref.shape[0], 4):
            heads = tails = jnp.zeros((8, 128), jnp.float32)
            for i in range(4):
                tile = tiles_ref[source + i]
                head, tail = (32 * (i - s)) % 128, (32 * (i - 3)) % 128
                heads = jnp.where(group == i, pltpu.roll(tile, head, 1) if head else tile, heads)
                tails = jnp.where(group == i, pltpu.roll(tile, tail, 1) if tail else tile, tails)
            hot.append((ident == heads[0:1]).astype(jnp.float32))
            packed.append(jnp.concatenate([heads, pltpu.roll(tails, 8 - 2 * s, 0) if s else tails], axis=0))
        packed = jnp.concatenate(packed, axis=1)
        packed = jnp.concatenate([packed, jnp.zeros((112, packed.shape[1]), jnp.float32)], axis=0)
        surface_ref[pl.ds(first * YR, cells), :] = lax.dot_general(
            jnp.concatenate(hot, axis=1),
            packed,
            (((1,), (1,)), ((), ())),
            precision=lax.Precision.HIGHEST,
            preferred_element_type=jnp.float32,
        )


def block_kernel(base_ref, low_ref, high_ref, ext):
    zero8 = jnp.zeros((8, 128), jnp.float32)
    x_low, x_high = starts(X_LOW), starts(X_HIGH)
    for f in range(FIELDS):
        for e in range(XS):
            x = e - 1 - W
            if 0 <= x < B:
                plane = base_ref[f, x]
            elif -X_LOW[f] <= x < 0:
                plane = low_ref[x_low[f] + X_LOW[f] + x]
            elif B <= x < B + X_HIGH[f]:
                plane = high_ref[x_high[f] + x - B]
            else:
                plane = zero8
            ext[pl.ds(f * PLANE + e * YR, 8), :] = plane
            ext[pl.ds(f * PLANE + e * YR + 8, 8), :] = zero8


def steps_kernel(
    steps,
    _,
    forward_hbm,
    y_low_ref,
    y_high_ref,
    force_ref,
    ext,
    state_ref,
    kernels_ref,
    change_ref,
    rate_ref,
    forward_ref,
    sem,
    load_sem,
):
    loads = [pltpu.make_async_copy(forward_hbm.at[t], forward_ref.at[t], load_sem.at[t]) for t in range(steps)]
    for load in loads:
        load.start()
    for ref, counts, first in ((y_high_ref, Y_HIGH, 8), (y_low_ref, Y_LOW, YR)):
        for f, (at, count) in enumerate(zip(starts(counts), counts)):
            for r in range(count):
                row = f * PLANE + YR + (first + r if first == 8 else first - count + r)
                ext[pl.ds(row, XE, stride=YR), :] = ref[pl.ds((at + r) * XE, XE), :]

    lanes = lax.broadcasted_iota(jnp.int32, (YR, 128), 1)

    def y_up(v):
        return pltpu.roll(v, YR - 1, 0)

    def y_down(v):
        return pltpu.roll(v, 1, 0)

    def z_up(v):
        return jnp.where(lanes == 127, 0.0, pltpu.roll(v, 127, 1))

    def z_down(v):
        return jnp.where(lanes == 0, 0.0, pltpu.roll(v, 1, 1))

    def get(f, e, rows=YR):
        return ext[pl.ds(f * PLANE + e * YR, rows), :]

    def put(f, e, v):
        ext[pl.ds(f * PLANE + e * YR, v.shape[0]), :] = v

    for step in range(steps):

        def velocity(e):
            sxx, syy, szz, sxy, sxz, syz = [get(3 + f, e) for f in range(6)]
            ax = (get(3, e + 1) - sxx) + (sxy - y_down(sxy)) + (sxz - z_down(sxz))
            ay = (sxy - get(6, e - 1)) + (y_up(syy) - syy) + (syz - z_down(syz))
            az = (sxz - get(7, e - 1)) + (syz - y_down(syz)) + (z_up(szz) - szz)
            scale = DT * get(9, e)
            surface = force_ref[pl.ds((e - 1) * YR, YR), :]
            for c, accel in enumerate((ax, ay, az)):
                force = jnp.where(lanes == 0, pltpu.roll(surface, 127 - 3 * step - c, 1), 0.0)
                change = scale * (accel + force)
                put(c, e, get(c, e) + change)
                change_ref[3 * step + c, e] = change[0:8]

        def stress(e):
            vx, vy, vz = [get(f, e) for f in range(3)]
            exx = vx - get(0, e - 1)
            eyy = vy - y_down(vy)
            ezz = vz - z_down(vz)
            exy = 0.5 * ((y_up(vx) - vx) + (get(1, e + 1) - vy))
            exz = 0.5 * ((z_up(vx) - vx) + (get(2, e + 1) - vz))
            eyz = 0.5 * ((z_up(vy) - vy) + (y_up(vz) - vz))
            rates = (exx, eyy, ezz, exy, exz, eyz)
            if step == steps - 1:
                rates = [rate[0:8] for rate in rates]
            rows = rates[0].shape[0]
            trace = rates[0] + rates[1] + rates[2]
            lam = get(10, e, rows) * trace
            twice = 2.0 * get(11, e, rows)
            for f, rate in enumerate(rates):
                if f < 3:
                    put(3 + f, e, get(3 + f, e, rows) + DT * (lam + twice * rate))
                else:
                    put(3 + f, e, get(3 + f, e, rows) + DT * twice * rate)
                rate_ref[6 * step + f, e] = rate[0:8]

        for e in range(1 + step, 1 + XE - step):
            velocity(e)
        for e in range(2 + step, XE - step):
            stress(e)
    copies = [
        pltpu.make_async_copy(
            ext.reshape(FIELDS, XS, YR, 128).at[f, pl.ds(1 + W, B), pl.ds(0, B)], state_ref.at[f], sem.at[f]
        )
        for f in range(9)
    ]
    for copy in copies:
        copy.start()
    for load in loads:
        load.wait()

    def sensitivities(x, carry):
        e = x + 1 + W
        totals = None
        for step in range(steps):
            f = [forward_ref[step, c, x].astype(jnp.float32) for c in range(9)]
            change = [change_ref[3 * step + c, e] for c in range(3)]
            rate = [rate_ref[6 * step + c, e] for c in range(6)]
            trace = rate[0] + rate[1] + rate[2]
            terms = (
                f[0] * change[0] + f[1] * change[1] + f[2] * change[2],
                DT * (f[3] + f[4] + f[5]) * trace,
                DT
                * 2.0
                * (
                    (f[3] * rate[0] + f[4] * rate[1] + f[5] * rate[2])
                    + 2.0 * (f[6] * rate[3] + f[7] * rate[4] + f[8] * rate[5])
                ),
            )
            totals = [total + term for total, term in zip(totals, terms)] if step else terms
        for k in range(3):
            kernels_ref[k, x] = totals[k]
        return carry

    lax.fori_loop(0, B, sensitivities, 0, unroll=2)

    for copy in copies:
        copy.wait()


def sum_kernel(events, parts_ref, out_ref):
    size = parts_ref.shape[0] // events
    total = parts_ref[0:size]
    for s in range(1, events):
        total = total + parts_ref[size * s : size * s + size]
    for s in range(events):
        out_ref[size * s : size * s + size] = total


def f32(*shape):
    return jax.ShapeDtypeStruct(shape, jnp.float32)


def in_hbm(a):
    return pltpu.with_memory_space_constraint(a, pltpu.HBM)


def on_device(
    adjoint_state,
    forward_state,
    inv_density,
    lame_lambda,
    shear_modulus,
    station_block,
    station_cell,
    station_trace,
    source_count,
):
    n_sx, n_sy, n_ev = lax.axis_size("sx"), lax.axis_size("sy"), lax.axis_size("ev")
    steps = forward_state.shape[1]
    ny = n_sy * B
    adj = adjoint_state[0]
    up_x = [(i, i + 1) for i in range(n_sx - 1)]
    up_y = [(i, i + 1) for i in range(n_sy - 1)]
    down_x = [(b, a) for a, b in up_x]
    down_y = [(b, a) for a, b in up_y]

    rows = station_cell.shape[1]
    low_face, high_face, base = pl.pallas_call(
        functools.partial(x_faces_kernel, ny),
        out_shape=[f32(sum(X_HIGH) + 1, 8, 128), f32(sum(X_LOW) + 1, 8, 128), f32(FIELDS, B, 8, 128)],
        in_specs=[HBM] * 4 + [SMEM] + [HBM] * 3,
        out_specs=[VMEM] * 3,
        scratch_shapes=[
            pltpu.VMEM((1, rows), jnp.int32),
            pltpu.VMEM((1, rows), jnp.int32),
            pltpu.VMEM((9, 1, rows), jnp.float32),
            pltpu.SemaphoreType.DMA((2, 4)),
        ],
        compiler_params=pltpu.CompilerParams(vmem_limit_bytes=3 * MIB),
        name="x_faces",
    )(
        in_hbm(adj),
        in_hbm(inv_density),
        in_hbm(lame_lambda),
        in_hbm(shear_modulus),
        source_count,
        in_hbm(station_block[:, :, 0]),
        in_hbm(station_cell),
        in_hbm(jnp.transpose(station_trace, (2, 0, 1))),
    )
    low = lax.ppermute(high_face, "sx", up_x)
    high = lax.ppermute(low_face, "sx", down_x)

    tiles = pl.pallas_call(
        functools.partial(tiles_kernel, ny),
        out_shape=f32(n_sy, 8, 128),
        in_specs=[VMEM] * 3,
        out_specs=VMEM,
        compiler_params=pltpu.CompilerParams(vmem_limit_bytes=2 * MIB),
        name="tiles",
    )(low_face, low, high)
    tiles = lax.all_to_all(tiles, "sy", split_axis=0, concat_axis=0, tiled=True)

    flat = lambda a: a.reshape(-1, 128)
    y_low_face, y_high_face = pl.pallas_call(
        y_faces_kernel,
        out_shape=[f32(-(-XE * sum(c) // 8) * 8, 128) for c in (Y_HIGH, Y_LOW)],
        in_specs=[VMEM] * 3,
        out_specs=[VMEM] * 2,
        compiler_params=pltpu.CompilerParams(vmem_limit_bytes=4 * MIB),
        name="y_faces",
    )(flat(base), flat(low), flat(high))
    y_low = lax.ppermute(y_high_face, "sy", up_y)
    y_high = lax.ppermute(y_low_face, "sy", down_y)

    place = lax.axis_index("sy").astype(jnp.int32).reshape(1)
    surface = pl.pallas_call(
        functools.partial(surface_kernel, ny),
        out_shape=f32(XE * YR, 128),
        in_specs=[SMEM, VMEM],
        out_specs=VMEM,
        compiler_params=pltpu.CompilerParams(vmem_limit_bytes=4 * MIB),
        name="surface",
    )(place, tiles)

    ext = pl.pallas_call(
        block_kernel,
        out_shape=f32(FIELDS * PLANE, 128),
        in_specs=[VMEM] * 3,
        out_specs=VMEM,
        compiler_params=pltpu.CompilerParams(vmem_limit_bytes=4 * MIB),
        name="block",
    )(base, low, high)

    _, state, kernels = pl.pallas_call(
        functools.partial(steps_kernel, steps),
        out_shape=[f32(FIELDS * PLANE, 128), f32(9, B, 8, 128), f32(3, B, 8, 128)],
        in_specs=[VMEM, HBM, VMEM, VMEM, VMEM],
        out_specs=[VMEM, HBM, VMEM],
        input_output_aliases={0: 0},
        scratch_shapes=[
            pltpu.VMEM((3 * steps, XS, 8, 128), jnp.float32),
            pltpu.VMEM((6 * steps, XS, 8, 128), jnp.float32),
            pltpu.VMEM(forward_state.shape[1:], forward_state.dtype),
            pltpu.SemaphoreType.DMA((9,)),
            pltpu.SemaphoreType.DMA((steps,)),
        ],
        compiler_params=pltpu.CompilerParams(vmem_limit_bytes=8 * MIB),
        name="steps",
    )(ext, in_hbm(forward_state[0]), y_low, y_high, surface)

    parts = lax.all_to_all(kernels.reshape(3 * B, 8, 128), "ev", split_axis=0, concat_axis=0, tiled=True)
    shared = pl.pallas_call(
        functools.partial(sum_kernel, n_ev), out_shape=f32(3 * B, 8, 128), in_specs=[VMEM], out_specs=VMEM, compiler_params=pltpu.CompilerParams(vmem_limit_bytes=1 * MIB),
        name="event_sum"
    )(parts)
    total = lax.all_to_all(shared, "ev", split_axis=0, concat_axis=0, tiled=True)
    return state[None], total.reshape(3, B, 8, 128)


def solution(mesh):
    return jax.shard_map(
        on_device,
        mesh=mesh,
        in_specs=(
            P("ev", None, "sx", "sy", None),
            P("ev", None, None, "sx", "sy", None),
            P("sx", "sy", None),
            P("sx", "sy", None),
            P("sx", "sy", None),
            P("ev", ("sx", "sy"), None),
            P("ev", ("sx", "sy")),
            P("ev", ("sx", "sy"), None),
            P("ev", ("sx", "sy")),
        ),
        out_specs=(P("ev", None, "sx", "sy", None), P(None, "sx", "sy", None)),
        check_vma=False,
    )
```
